256 devices in a mesh: lat: 32 (over y, z), rad: 8 (over x, core).
Axes of the slice: x: 4, y: 4, z: 8, core: 2. Of those that a mesh axis runs over, the one named last changes fastest.
Arguments:
- source: float32 [128, 131072], P('rad', 'lat'), may hold values from -6 to 6
- to_modes: float32 [128, 128], replicated, may hold values from -0.5 to 0.5
- from_modes: float32 [128, 128], replicated, may hold values from -0.5 to 0.5
- eigenvalue: float32 [128], replicated, may hold values from 0.1 to 20
- shifts: float32 [131072], P('lat'), may hold values from 0.5 to 2
- weights: float32 [31, 131072], P(None, 'lat'), may hold values from 0.02 to 0.12
- neighbors: int32 [31, 1024], P(None, 'lat'), may hold values from -8 to 8, as said below
Outputs:
- smoothed: float32 [128, 131072], P('rad', 'lat')
- residual_norm: float32 [128], P('rad')
The draws below stay inside these ranges and needn't reach their ends.
Inputs may be any that keep to these rules, and one draw needn't show every extreme that they name: `neighbors`: every entry is nonzero; some entry equals -8.
All inputs are finite; a program needn't handle non-finite values.
Results may differ from the reference program's by a relative error of at most 0.000073.
Values sent between devices are 32-bit elements; how exact they have to be, the bound alone decides.
No kernel may reach another device: no remote copies, remote signals or barrier semaphores. Data moves between devices by JAX's collectives and lax.ppermute only.
A program may use at most 64 MiB of HBM per device.

```python
import math
import jax
import jax.numpy as jnp
from jax import lax

LEVELS = 128
STENCIL = 31
BLOCK = 128
HALO_BLOCKS = 8
NODES = 131072


def draw_neighbors(key, part):
    offsets = jax.random.randint(key, (STENCIL, NODES // BLOCK), -HALO_BLOCKS, HALO_BLOCKS + 1).astype(jnp.int32)
    offsets = jnp.where(offsets == 0, HALO_BLOCKS, offsets)
    offsets = offsets.at[0, 0].set(-HALO_BLOCKS)
    return offsets.astype(jnp.int32)


def shard_levels(rng, shape, split, smallest, largest):
    factor_of = 1.0
    for dim, parts in split:
        draws = jax.random.uniform(jax.random.fold_in(jax.random.fold_in(rng, 6), dim), (parts,), jnp.float32, smallest / len(split), largest / len(split))
        factor_of = factor_of * jnp.repeat(jnp.exp(draws), shape[dim] // parts).reshape((-1,) + (1,) * (len(shape) - 1 - dim))
    return factor_of


def scatter_about(stream_key, extent, width, most, split=(), held_as=jnp.bfloat16):
    values = jax.random.normal(stream_key, extent, jnp.float32) * width
    if len(split) > 0:
        values = shard_levels(stream_key, extent, split, -0.22, 0.18) * values
    return jnp.clip(values, min=-most, max=most).astype(held_as)


def setup_inputs(seed: int = 0) -> dict:
    key_list = jax.random.split(jax.random.key(seed), 8)
    return {
        "source": scatter_about(key_list[0], (LEVELS, NODES), 1.0, 6.0, ((0, 8), (1, 32)), jnp.float32),
        "to_modes": scatter_about(key_list[1], (LEVELS, LEVELS), LEVELS ** -0.5, 0.5, (), jnp.float32),
        "from_modes": scatter_about(key_list[2], (LEVELS, LEVELS), LEVELS ** -0.5, 0.5, (), jnp.float32),
        "eigenvalue": jnp.clip(jnp.exp(jax.random.uniform(key_list[3], (LEVELS,), jnp.float32, math.log(0.1), math.log(20.0))), 0.1, 20.0),
        "shifts": jnp.clip(0.5 + 1.5 * jax.random.uniform(key_list[4], (NODES,), jnp.float32) ** shard_levels(key_list[4], (NODES,), ((0, 32),), -0.2, 0.2), 0.5, 2.0),
        "weights": jnp.clip(0.02 + 0.09999999776482582 * jax.random.uniform(key_list[5], (STENCIL, NODES), jnp.float32) ** shard_levels(key_list[5], (STENCIL, NODES), ((1, 32),), -0.2, 0.2), 0.02, 0.12),
        "neighbors": draw_neighbors(jax.random.fold_in(key_list[7], 71), 0),
    }


def operate(field, eigenvalue, shifts, weights, neighbors):
    total = lax.optimization_barrier(jnp.sum(weights, axis=0))
    coeffs = (shifts + total)[None, :] + eigenvalue[:, None]
    result = coeffs * field
    node_count = field.shape[1]
    node_ids = jnp.arange(node_count, dtype=jnp.int32)
    block_ids = (node_ids // BLOCK).astype(jnp.int32)
    lane_ids = (node_ids % BLOCK).astype(jnp.int32)
    for slot_index in range(weights.shape[0]):
        block_off = jnp.take(neighbors[slot_index].astype(jnp.int32), block_ids)
        target = (((block_ids + block_off) * BLOCK + (lane_ids + slot_index) % BLOCK) % node_count).astype(jnp.int32)
        result = result - weights[slot_index][None, :] * jnp.take(field, target, axis=1)
    return result

def reference(source, to_modes, from_modes, eigenvalue, shifts, weights, neighbors):
    modal = jnp.dot(to_modes, source, precision=lax.Precision.HIGHEST, preferred_element_type=jnp.float32)
    image = operate(modal, eigenvalue, shifts, weights, neighbors)
    base = lax.optimization_barrier(jnp.sum(modal * modal, axis=1))
    power = lax.optimization_barrier(jnp.sum(image * image, axis=1))
    upper = 1.5 * jnp.sqrt(power / (base + 1e-06))
    lower = upper * 0.125
    center = ((upper + lower) * 0.5)[:, None]
    half_width = ((upper - lower) * 0.5)[:, None]
    sigma = center / half_width
    rho_zero = 1.0 / sigma
    rho_one = 1.0 / (2.0 * sigma - rho_zero)
    first = modal / center
    second_res = modal - image / center
    update = rho_one * rho_zero * first + 2.0 * rho_one / half_width * second_res
    iterate = first + update
    final_res = second_res - operate(update, eigenvalue, shifts, weights, neighbors)
    residual_norm = jnp.sqrt(lax.optimization_barrier(jnp.sum(final_res * final_res, axis=1)) / (base + 1e-06))
    smoothed = jnp.dot(from_modes, iterate, precision=lax.Precision.HIGHEST, preferred_element_type=jnp.float32)
    return (smoothed, residual_norm)
```

```python
import functools

import jax
import jax.numpy as jnp
import numpy as np
from jax import lax
from jax.experimental import pallas as pl
from jax.experimental.pallas import tpu as pltpu
from jax.sharding import Mesh, PartitionSpec as P

LANES = 128
HALO = 8
STENCIL = 31
ROWS = STENCIL + 1
BLOCKS = 32
EXT1 = BLOCKS + 2 * HALO
EXT2 = BLOCKS + 4 * HALO
SLAB = 16
PARTS = 8
PART = BLOCKS * LANES // PARTS
MODES = 128
WIDE = 2 * HALO * LANES
NEAR = HALO * LANES
LAT = ("y", "z")
RAD = ("x", "core")
STAGE_1 = ("y", "x", "core")
STAGE_2 = "z"
VMEM = pl.BlockSpec(memory_space=pltpu.VMEM)
SMEM = pl.BlockSpec(memory_space=pltpu.SMEM)
HIGHEST = lax.Precision.HIGHEST


def f32(*shape):
    return jax.ShapeDtypeStruct(shape, jnp.float32)


def mm(a, b):
    return jnp.dot(a, b, precision=HIGHEST, preferred_element_type=jnp.float32)


def pack_kernel(src, weights, shifts, neighbors, up, down, own):
    nb = neighbors[...].astype(jnp.float32)
    last = BLOCKS * LANES
    for out, start, near, blocks, place in (
        (up, last - WIDE, last - NEAR, BLOCKS - HALO, 0),
        (down, 0, 0, 0, HALO + BLOCKS),
    ):
        out[0:SLAB, 0:NEAR] = src[:, start : start + NEAR]
        out[SLAB : 2 * SLAB, 0:NEAR] = src[:, start + NEAR : start + WIDE]
        out[0:STENCIL, NEAR:WIDE] = weights[:, near : near + NEAR]
        out[STENCIL:ROWS, NEAR:WIDE] = shifts[:, near : near + NEAR]
        out[:, WIDE:] = jnp.zeros((ROWS, LANES), jnp.float32)
        out[0:STENCIL, WIDE + place : WIDE + place + HALO] = nb[:, blocks : blocks + HALO]
    own[...] = jnp.zeros((ROWS, LANES), jnp.float32)
    own[0:STENCIL, HALO : HALO + BLOCKS] = nb


def stencil_kernel(src, left, right, weights, shifts, own, out, x0, x1, w, diag, nbv, nbs, sem):
    lane = lax.broadcasted_iota(jnp.int32, (ROWS, LANES), 1)
    nb = jnp.where(
        lane < HALO, left[:, WIDE:], jnp.where(lane < HALO + BLOCKS, own[...], right[:, WIDE:])
    )
    nbv[...] = nb.astype(jnp.int32)
    copy = pltpu.make_async_copy(nbv, nbs, sem)
    copy.start()
    for half in range(2):
        rows = slice(half * SLAB, half * SLAB + SLAB)
        for j in range(HALO):
            cols = slice(j * LANES, (j + 1) * LANES)
            x0[half * HALO + j] = left[rows, cols]
            x0[2 * HALO + BLOCKS + half * HALO + j] = right[rows, cols]
    for j in range(BLOCKS):
        x0[2 * HALO + j] = src[:, j * LANES : (j + 1) * LANES]
    for r in range(PARTS):
        out[r, 0:SLAB, :] = src[:, r * PART : (r + 1) * PART]
    for j in range(HALO):
        cols = slice(NEAR + j * LANES, NEAR + (j + 1) * LANES)
        w[j] = left[:, cols]
        w[HALO + BLOCKS + j] = right[:, cols]
    for j in range(BLOCKS):
        cols = slice(j * LANES, (j + 1) * LANES)
        w[HALO + j, 0:STENCIL, :] = weights[:, cols]
        w[HALO + j, STENCIL:ROWS, :] = shifts[:, cols]
    copy.wait()

    def apply(field, block, centre, d):
        acc = d * field[block + centre]
        for s in range(STENCIL):
            moved = field[nbs[s, block] + (block + centre)]
            if s:
                moved = pltpu.roll(moved, LANES - s, 1)
            acc = acc - w[block, s : s + 1, :] * moved
        return acc

    def first(e, _):
        d = jnp.sum(w[e], axis=0, keepdims=True)
        diag[e] = d
        x1[e] = apply(x0, e, HALO, d)
        return 0

    lax.fori_loop(0, EXT1, first, 0)

    def second(b, _):
        part = lax.div(b, PART // LANES)
        cols = pl.ds(pl.multiple_of(lax.rem(b, PART // LANES) * LANES, LANES), LANES)
        e = b + HALO
        out[part, SLAB : 2 * SLAB, cols] = x1[e]
        out[part, 2 * SLAB : 3 * SLAB, cols] = apply(x1, e, 0, diag[e])
        return 0

    lax.fori_loop(0, BLOCKS, second, 0)


def gram_kernel(z, to_modes, eig, out, s):
    for r in range(PARTS):
        rows = slice(r * SLAB, (r + 1) * SLAB)
        for q in range(3):
            s[rows, q * PART : (q + 1) * PART] = z[r, q * SLAB : (q + 1) * SLAB, :]
    m = mm(to_modes[...], s[...])
    row = lax.broadcasted_iota(jnp.int32, (MODES, MODES), 0)
    col = lax.broadcasted_iota(jnp.int32, (MODES, MODES), 1)
    e = jnp.sum(jnp.where(row == col, eig[...], 0.0), axis=1, keepdims=True)
    m0, m1, m2 = (m[:, q * PART : (q + 1) * PART] for q in range(3))
    image = m1 + e * m0
    again = (m2 + e * m1) + e * image
    folded = []
    for a, b in ((m0, m0), (m0, image), (image, image), (m0, again), (image, again), (again, again)):
        p = a * b
        folded.append(sum(p[:, k * LANES : (k + 1) * LANES] for k in range(PART // LANES)))
    stack = jnp.concatenate(folded, axis=1)
    which = lax.broadcasted_iota(jnp.int32, (8, 6 * LANES), 1) // LANES
    pick = (which == lax.broadcasted_iota(jnp.int32, (8, 6 * LANES), 0)).astype(jnp.float32)
    g = lax.dot_general(
        pick, stack, (((1,), (1,)), ((), ())), precision=HIGHEST, preferred_element_type=jnp.float32
    )
    out[...] = jnp.broadcast_to(g[None], out.shape)


def relay_kernel(got, out):
    out[...] = jnp.broadcast_to(jnp.sum(got[...], axis=0)[None], out.shape)


def finish_kernel(got, z, to_modes, from_modes, eig, out, norm, s):
    g = jnp.sum(got[...], axis=0)
    mm_, mi, ii, mj, ij, jj = (g[k : k + 1, :] for k in range(6))
    e = eig[...]
    scale = mm_ + 1e-06
    upper = 1.5 * jnp.sqrt(ii / scale)
    lower = upper * 0.125
    center = (upper + lower) * 0.5
    half_width = (upper - lower) * 0.5
    sigma = center / half_width
    rho_zero = 1.0 / sigma
    rho_one = 1.0 / (2.0 * sigma - rho_zero)
    over = 1.0 / center
    c2 = 2.0 * rho_one / half_width
    u0 = rho_one * rho_zero * over + c2
    u1 = -c2 * over
    a = -over - u0
    b = -u1
    squares = mm_ + a * (2.0 * mi + a * ii) + b * (2.0 * (mj + a * ij) + b * jj)
    norm[...] = jnp.sqrt(jnp.maximum(squares, 0.0) / scale)
    for r in range(PARTS):
        for q in range(2):
            s[q * MODES + r * SLAB : q * MODES + (r + 1) * SLAB, :] = z[r, q * SLAB : (q + 1) * SLAB, :]
    from_m = from_modes[...]
    to_m = to_modes[...]
    mix = jnp.concatenate([mm(from_m * (over + u0 + u1 * e), to_m), mm(from_m * u1, to_m)], axis=1)
    out[...] = mm(mix, s[...]).reshape(out.shape)


def unpack_kernel(got, out):
    for r in range(PARTS):
        out[:, r * PART : (r + 1) * PART] = got[r]


def call(kernel, out_shape, in_specs, scratch=()):
    multiple = isinstance(out_shape, tuple)
    return pl.pallas_call(
        kernel,
        out_shape=out_shape,
        in_specs=in_specs,
        out_specs=(VMEM,) * len(out_shape) if multiple else VMEM,
        scratch_shapes=scratch,
        compiler_params=pltpu.CompilerParams(vmem_limit_bytes=32 * 1024 * 1024),
    )


def on_device(sizes, source, to_modes, from_modes, eigenvalue, shifts, weights, neighbors):
    lat = sizes["y"] * sizes["z"]
    shift_row = shifts.reshape(1, -1)
    eig = eigenvalue.reshape(1, -1)
    up, down, own = call(
        pack_kernel, (f32(ROWS, WIDE + LANES), f32(ROWS, WIDE + LANES), f32(ROWS, LANES)), [VMEM] * 4
    )(source, weights, shift_row, neighbors)
    left = lax.ppermute(up, LAT, [(i, (i + 1) % lat) for i in range(lat)])
    right = lax.ppermute(down, LAT, [((i + 1) % lat, i) for i in range(lat)])
    sent = call(
        stencil_kernel,
        f32(PARTS, 3 * SLAB, PART),
        [VMEM] * 6,
        [
            pltpu.VMEM((EXT2, SLAB, LANES), jnp.float32),
            pltpu.VMEM((EXT1, SLAB, LANES), jnp.float32),
            pltpu.VMEM((EXT1, ROWS, LANES), jnp.float32),
            pltpu.VMEM((EXT1, 1, LANES), jnp.float32),
            pltpu.VMEM((ROWS, LANES), jnp.int32),
            pltpu.SMEM((ROWS, LANES), jnp.int32),
            pltpu.SemaphoreType.DMA,
        ],
    )(source, left, right, weights, shift_row, own)
    z = lax.all_to_all(sent, RAD, 0, 0, tiled=True)
    peers_1 = sizes["y"] * sizes["x"] * sizes["core"]
    peers_2 = sizes["z"]
    g = call(
        gram_kernel,
        f32(peers_1, 8, LANES),
        [VMEM] * 3,
        [pltpu.VMEM((MODES, 3 * PART), jnp.float32)],
    )(z, to_modes, eig)
    g = lax.all_to_all(g, STAGE_1, 0, 0, tiled=True)
    g = call(relay_kernel, f32(peers_2, 8, LANES), [VMEM])(g)
    g = lax.all_to_all(g, STAGE_2, 0, 0, tiled=True)
    mixed, norm = call(
        finish_kernel,
        (f32(PARTS, SLAB, PART), f32(1, LANES)),
        [VMEM] * 5,
        [pltpu.VMEM((2 * MODES, PART), jnp.float32)],
    )(g, z, to_modes, from_modes, eig)
    got = lax.all_to_all(mixed, RAD, 0, 0, tiled=True)
    smoothed = call(unpack_kernel, f32(SLAB, BLOCKS * LANES), [VMEM])(got)
    residual_norm = lax.dynamic_slice_in_dim(norm[0], lax.axis_index(RAD) * SLAB, SLAB)
    return smoothed, residual_norm


def solution(mesh):
    names = ("y", "z", "x", "core")
    fine = Mesh(np.asarray(mesh.devices).reshape(4, 8, 4, 2), names)
    return jax.shard_map(
        functools.partial(on_device, dict(fine.shape)),
        mesh=fine,
        in_specs=(P(RAD, LAT), P(), P(), P(), P(LAT), P(None, LAT), P(None, LAT)),
        out_specs=(P(RAD, LAT), P(RAD)),
        check_vma=False,
    )
```

```python
import functools

import jax
import jax.numpy as jnp
import numpy as np
from jax import lax
from jax.experimental import pallas as pl
from jax.experimental.pallas import tpu as pltpu
from jax.sharding import Mesh, PartitionSpec as P

LANES = 128
HALO = 8
UNROLL = 8
STENCIL = 31
ROWS = STENCIL + 1
BLOCKS = 32
EXT1 = BLOCKS + 2 * HALO
EXT2 = BLOCKS + 4 * HALO
SLAB = 16
PARTS = 8
PART = BLOCKS * LANES // PARTS
MODES = 128
WIDE = 2 * HALO * LANES
NEAR = HALO * LANES
LAT = ("y", "z")
RAD = ("x", "core")
STAGE_1 = ("y", "x", "core")
STAGE_2 = "z"
VMEM = pl.BlockSpec(memory_space=pltpu.VMEM)
SMEM = pl.BlockSpec(memory_space=pltpu.SMEM)
HBM = pl.BlockSpec(memory_space=pltpu.HBM)
HIGHEST = lax.Precision.HIGHEST


def f32(*shape):
    return jax.ShapeDtypeStruct(shape, jnp.float32)


def mm(a, b):
    return jnp.dot(a, b, precision=HIGHEST, preferred_element_type=jnp.float32)


def start_all(sems, pairs):
    copies = [pltpu.make_async_copy(src, dst, sems.at[k]) for k, (src, dst) in enumerate(pairs)]
    for copy in copies:
        copy.start()
    return copies


def wait_all(copies):
    for copy in copies:
        copy.wait()


def pack_kernel(src, weights, shifts, neighbors, eig, up, down, own, nb_in, w_in, sh_in, eig_in, sems):
    last = BLOCKS * LANES
    ends = ((up, last - WIDE, last - NEAR), (down, 0, 0))
    pairs = [(neighbors, nb_in), (eig, eig_in)]
    for k, (out, start, near) in enumerate(ends):
        pairs += [
            (weights.at[:, pl.ds(near, NEAR)], w_in.at[k]),
            (shifts.at[:, pl.ds(near, NEAR)], sh_in.at[k]),
            (src.at[:, pl.ds(start, NEAR)], out.at[0:SLAB, 0:NEAR]),
            (src.at[:, pl.ds(start + NEAR, NEAR)], out.at[SLAB : 2 * SLAB, 0:NEAR]),
        ]
    wait_all(start_all(sems, pairs))
    nb = nb_in[...].astype(jnp.float32)
    for k, (out, first) in enumerate(((up, BLOCKS - HALO), (down, 0))):
        out[0:STENCIL, NEAR:WIDE] = w_in[k]
        out[STENCIL:ROWS, NEAR:WIDE] = sh_in[k]
        out[:, WIDE:] = jnp.zeros((ROWS, LANES), jnp.float32)
        out[0:STENCIL, WIDE : WIDE + HALO] = nb[:, first : first + HALO]
    own[...] = jnp.broadcast_to(eig_in[...], own.shape)


def deal_kernel(src, out, sems):
    wait_all(
        start_all(sems, [(src.at[:, pl.ds(r * PART, PART)], out.at[r]) for r in range(PARTS)])
    )


def column(start, block):
    return pl.ds(pl.multiple_of(start + block * LANES, LANES), LANES)


def apply(read, centre, d, weight, offset):
    acc = d * read(centre)
    for s in range(STENCIL):
        moved = read(offset(s) + centre)
        if s:
            moved = pltpu.roll(moved, LANES - s, 1)
        acc = acc - weight(s) * moved
    return acc


def inner_kernel(src, weights, shifts, nb, x1, diag):
    for j in range(BLOCKS):
        cols = slice(j * LANES, (j + 1) * LANES)
        diag[j] = jnp.sum(weights[:, cols], axis=0, keepdims=True) + shifts[:, cols]

    def step(i, _):
        for u in range(UNROLL):
            b = HALO + i * UNROLL + u
            x1[b - HALO] = apply(
                lambda c: src[:, column(0, c)],
                b,
                diag[b],
                lambda s: weights[s : s + 1, column(0, b)],
                lambda s: nb[s, b],
            )
        return 0

    lax.fori_loop(0, (BLOCKS - 2 * HALO) // UNROLL, step, 0)


def stencil_kernel(src, left, right, weights, diag, inner, nb, out, x0, x1, nbv, nbs, sems):
    nbv[0] = left[:, WIDE:].astype(jnp.int32)
    nbv[1] = right[:, WIDE:].astype(jnp.int32)
    copies = start_all(sems, [(nbv.at[k], nbs.at[k]) for k in range(2)])
    for half in range(2):
        rows = slice(half * SLAB, half * SLAB + SLAB)
        for j in range(HALO):
            cols = slice(j * LANES, (j + 1) * LANES)
            x0[half * HALO + j] = left[rows, cols]
            x0[2 * HALO + BLOCKS + half * HALO + j] = right[rows, cols]
    for j in range(BLOCKS):
        x0[2 * HALO + j] = src[:, j * LANES : (j + 1) * LANES]
    for j in range(BLOCKS - 2 * HALO):
        x1[2 * HALO + j] = inner[j]

    def own(b):
        x1[b + HALO] = apply(
            lambda c: x0[c],
            b + 2 * HALO,
            diag[b],
            lambda s: weights[s : s + 1, column(0, b)],
            lambda s: nb[s, b],
        )

    def far(side, ref, j):
        e = j + side * (HALO + BLOCKS)
        x1[e] = apply(
            lambda c: x0[c],
            e + HALO,
            jnp.sum(ref[:, column(NEAR, j)], axis=0, keepdims=True),
            lambda s: ref[s : s + 1, column(NEAR, j)],
            lambda s: nbs[side, s, j],
        )

    def first(i, _):
        for u in range(UNROLL):
            b = i * UNROLL + u
            own(b + jnp.where(b < HALO, 0, BLOCKS - 2 * HALO))
        return 0

    lax.fori_loop(0, 2 * HALO // UNROLL, first, 0)
    wait_all(copies)
    for side, ref in ((0, left), (1, right)):

        def outer(i, _, side=side, ref=ref):
            for u in range(UNROLL):
                far(side, ref, i * UNROLL + u)
            return 0

        lax.fori_loop(0, HALO // UNROLL, outer, 0)

    def second(i, _):
        for u in range(UNROLL):
            b = i * UNROLL + u
            part = lax.div(b, PART // LANES)
            cols = column(0, lax.rem(b, PART // LANES))
            e = b + HALO
            out[part, 0:SLAB, cols] = x1[e]
            out[part, SLAB : 2 * SLAB, cols] = apply(
                lambda c: x1[c],
                e,
                diag[b],
                lambda s: weights[s : s + 1, column(0, b)],
                lambda s: nb[s, b],
            )
        return 0

    lax.fori_loop(0, BLOCKS // UNROLL, second, 0)


def gram_kernel(z0, z12, to_modes, own, out, s):
    eig = own[0:1, :]
    for r in range(PARTS):
        rows = slice(r * SLAB, (r + 1) * SLAB)
        s[rows, 0:PART] = z0[r]
        for q in range(2):
            s[rows, (q + 1) * PART : (q + 2) * PART] = z12[r, q * SLAB : (q + 1) * SLAB, :]
    m = mm(to_modes[...], s[...])
    row = lax.broadcasted_iota(jnp.int32, (MODES, MODES), 0)
    col = lax.broadcasted_iota(jnp.int32, (MODES, MODES), 1)
    e = jnp.sum(jnp.where(row == col, eig, 0.0), axis=1, keepdims=True)
    m0, m1, m2 = (m[:, q * PART : (q + 1) * PART] for q in range(3))
    image = m1 + e * m0
    again = (m2 + e * m1) + e * image
    folded = []
    for a, b in ((m0, m0), (m0, image), (image, image), (m0, again), (image, again), (again, again)):
        p = a * b
        folded.append(sum(p[:, k * LANES : (k + 1) * LANES] for k in range(PART // LANES)))
    stack = jnp.concatenate(folded, axis=1)
    which = lax.broadcasted_iota(jnp.int32, (8, 6 * LANES), 1) // LANES
    pick = (which == lax.broadcasted_iota(jnp.int32, (8, 6 * LANES), 0)).astype(jnp.float32)
    g = lax.dot_general(
        pick, stack, (((1,), (1,)), ((), ())), precision=HIGHEST, preferred_element_type=jnp.float32
    )
    out[...] = jnp.broadcast_to(g[None], out.shape)


def relay_kernel(got, out):
    out[...] = jnp.broadcast_to(jnp.sum(got[...], axis=0)[None], out.shape)


def finish_kernel(got, z0, z12, to_modes, from_modes, own, out, norm, s):
    g = jnp.sum(got[...], axis=0)
    mm_, mi, ii, mj, ij, jj = (g[k : k + 1, :] for k in range(6))
    e = own[0:1, :]
    scale = mm_ + 1e-06
    upper = 1.5 * jnp.sqrt(ii / scale)
    lower = upper * 0.125
    center = (upper + lower) * 0.5
    half_width = (upper - lower) * 0.5
    sigma = center / half_width
    rho_zero = 1.0 / sigma
    rho_one = 1.0 / (2.0 * sigma - rho_zero)
    over = 1.0 / center
    c2 = 2.0 * rho_one / half_width
    u0 = rho_one * rho_zero * over + c2
    u1 = -c2 * over
    a = -over - u0
    b = -u1
    squares = mm_ + a * (2.0 * mi + a * ii) + b * (2.0 * (mj + a * ij) + b * jj)
    norm[...] = jnp.sqrt(jnp.maximum(squares, 0.0) / scale)
    for r in range(PARTS):
        s[r * SLAB : (r + 1) * SLAB, :] = z0[r]
        s[MODES + r * SLAB : MODES + (r + 1) * SLAB, :] = z12[r, 0:SLAB, :]
    from_m = from_modes[...]
    to_m = to_modes[...]
    mix = jnp.concatenate([mm(from_m * (over + u0 + u1 * e), to_m), mm(from_m * u1, to_m)], axis=1)
    out[...] = mm(mix, s[...]).reshape(out.shape)


def unpack_kernel(got, out):
    for r in range(PARTS):
        out[:, r * PART : (r + 1) * PART] = got[r]


def call(kernel, out_shape, in_specs, scratch=()):
    multiple = isinstance(out_shape, tuple)
    return pl.pallas_call(
        kernel,
        out_shape=out_shape,
        in_specs=in_specs,
        out_specs=(VMEM,) * len(out_shape) if multiple else VMEM,
        scratch_shapes=scratch,
        compiler_params=pltpu.CompilerParams(vmem_limit_bytes=32 * 1024 * 1024),
    )


def on_device(sizes, source, to_modes, from_modes, eigenvalue, shifts, weights, neighbors):
    lat = sizes["y"] * sizes["z"]
    shift_row = shifts.reshape(1, -1)
    eig = eigenvalue.reshape(1, -1)
    up, down, own = call(
        pack_kernel,
        (f32(ROWS, WIDE + LANES), f32(ROWS, WIDE + LANES), f32(8, LANES)),
        [HBM] * 5,
        [
            pltpu.VMEM((STENCIL, BLOCKS), jnp.int32),
            pltpu.VMEM((2, STENCIL, NEAR), jnp.float32),
            pltpu.VMEM((2, 1, NEAR), jnp.float32),
            pltpu.VMEM((1, LANES), jnp.float32),
            pltpu.SemaphoreType.DMA((10,)),
        ],
    )(*(pltpu.with_memory_space_constraint(v, pltpu.HBM) for v in (source, weights, shift_row, neighbors, eig)))
    left = lax.ppermute(up, LAT, [(i, (i + 1) % lat) for i in range(lat)])
    right = lax.ppermute(down, LAT, [((i + 1) % lat, i) for i in range(lat)])
    dealt = call(
        deal_kernel, f32(PARTS, SLAB, PART), [HBM], [pltpu.SemaphoreType.DMA((PARTS,))]
    )(pltpu.with_memory_space_constraint(source, pltpu.HBM))
    z0 = lax.all_to_all(dealt, RAD, 0, 0, tiled=True)
    inner, diag = call(
        inner_kernel,
        (f32(BLOCKS - 2 * HALO, SLAB, LANES), f32(BLOCKS, 1, LANES)),
        [VMEM] * 3 + [SMEM],
    )(source, weights, shift_row, neighbors)
    sent = call(
        stencil_kernel,
        f32(PARTS, 2 * SLAB, PART),
        [VMEM] * 6 + [SMEM],
        [
            pltpu.VMEM((EXT2, SLAB, LANES), jnp.float32),
            pltpu.VMEM((EXT1, SLAB, LANES), jnp.float32),
            pltpu.VMEM((2, ROWS, LANES), jnp.int32),
            pltpu.SMEM((2, ROWS, LANES), jnp.int32),
            pltpu.SemaphoreType.DMA((2,)),
        ],
    )(source, left, right, weights, diag, inner, neighbors)
    z12 = lax.all_to_all(sent, RAD, 0, 0, tiled=True)
    peers_1 = sizes["y"] * sizes["x"] * sizes["core"]
    peers_2 = sizes["z"]
    g = call(
        gram_kernel,
        f32(peers_1, 8, LANES),
        [VMEM] * 4,
        [pltpu.VMEM((MODES, 3 * PART), jnp.float32)],
    )(z0, z12, to_modes, own)
    g = lax.all_to_all(g, STAGE_1, 0, 0, tiled=True)
    g = call(relay_kernel, f32(peers_2, 8, LANES), [VMEM])(g)
    g = lax.all_to_all(g, STAGE_2, 0, 0, tiled=True)
    mixed, norm = call(
        finish_kernel,
        (f32(PARTS, SLAB, PART), f32(1, LANES)),
        [VMEM] * 6,
        [pltpu.VMEM((2 * MODES, PART), jnp.float32)],
    )(g, z0, z12, to_modes, from_modes, own)
    got = lax.all_to_all(mixed, RAD, 0, 0, tiled=True)
    smoothed = call(unpack_kernel, f32(SLAB, BLOCKS * LANES), [VMEM])(got)
    residual_norm = lax.dynamic_slice_in_dim(norm[0], lax.axis_index(RAD) * SLAB, SLAB)
    return smoothed, residual_norm


def solution(mesh):
    names = ("y", "z", "x", "core")
    fine = Mesh(np.asarray(mesh.devices).reshape(4, 8, 4, 2), names)
    return jax.shard_map(
        functools.partial(on_device, dict(fine.shape)),
        mesh=fine,
        in_specs=(P(RAD, LAT), P(), P(), P(), P(LAT), P(None, LAT), P(None, LAT)),
        out_specs=(P(RAD, LAT), P(RAD)),
        check_vma=False,
    )
```

```python
import functools

import jax
import jax.numpy as jnp
import numpy as np
from jax import lax
from jax.experimental import pallas as pl
from jax.experimental.pallas import tpu as pltpu
from jax.sharding import Mesh, PartitionSpec as P

LANES = 128
HALO = 8
UNROLL = 8
STENCIL = 31
ROWS = STENCIL + 1
BLOCKS = 32
EXT1 = BLOCKS + 2 * HALO
EXT2 = BLOCKS + 4 * HALO
SLAB = 16
PARTS = 8
PART = BLOCKS * LANES // PARTS
MODES = 128
WIDE = 2 * HALO * LANES
NEAR = HALO * LANES
LAT = ("y", "z")
RAD = ("x", "core")
STAGE_1 = ("y", "x", "core")
STAGE_2 = "z"
VMEM = pl.BlockSpec(memory_space=pltpu.VMEM)
SMEM = pl.BlockSpec(memory_space=pltpu.SMEM)
HBM = pl.BlockSpec(memory_space=pltpu.HBM)
HIGHEST = lax.Precision.HIGHEST


def f32(*shape):
    return jax.ShapeDtypeStruct(shape, jnp.float32)


def mm(a, b):
    return jnp.dot(a, b, precision=HIGHEST, preferred_element_type=jnp.float32)


def start_all(sems, pairs):
    copies = [pltpu.make_async_copy(src, dst, sems.at[k]) for k, (src, dst) in enumerate(pairs)]
    for copy in copies:
        copy.start()
    return copies


def wait_all(copies):
    for copy in copies:
        copy.wait()


def pack_kernel(src, weights, shifts, neighbors, eig, up, down, own, dealt, nb_in, w_in, sh_in, eig_in, sems):
    last = BLOCKS * LANES
    ends = ((up, last - WIDE, last - NEAR), (down, 0, 0))
    pairs = [(neighbors, nb_in), (eig, eig_in)]
    for k, (out, start, near) in enumerate(ends):
        pairs += [
            (weights.at[:, pl.ds(near, NEAR)], w_in.at[k]),
            (shifts.at[:, pl.ds(near, NEAR)], sh_in.at[k]),
            (src.at[:, pl.ds(start, NEAR)], out.at[0:SLAB, 0:NEAR]),
            (src.at[:, pl.ds(start + NEAR, NEAR)], out.at[SLAB : 2 * SLAB, 0:NEAR]),
        ]
    pairs += [(src.at[:, pl.ds(r * PART, PART)], dealt.at[r]) for r in range(PARTS)]
    wait_all(start_all(sems, pairs))
    nb = nb_in[...].astype(jnp.float32)
    for k, (out, first) in enumerate(((up, BLOCKS - HALO), (down, 0))):
        out[0:STENCIL, NEAR:WIDE] = w_in[k]
        out[STENCIL:ROWS, NEAR:WIDE] = sh_in[k]
        out[:, WIDE:] = jnp.zeros((ROWS, LANES), jnp.float32)
        out[0:STENCIL, WIDE : WIDE + HALO] = nb[:, first : first + HALO]
    own[...] = jnp.broadcast_to(eig_in[...], own.shape)


def column(start, block):
    return pl.ds(pl.multiple_of(start + block * LANES, LANES), LANES)


def apply(read, centre, d, weight, offset):
    acc = d * read(centre)
    for s in range(STENCIL):
        moved = read(offset(s) + centre)
        if s:
            moved = pltpu.roll(moved, LANES - s, 1)
        acc = acc - weight(s) * moved
    return acc


def inner_kernel(src, weights, shifts, nb, place_in, x1, diag, place):
    place[0] = place_in[0]
    for j in range(BLOCKS):
        cols = slice(j * LANES, (j + 1) * LANES)
        diag[j] = jnp.sum(weights[:, cols], axis=0, keepdims=True) + shifts[:, cols]

    def step(i, _):
        for u in range(UNROLL):
            b = HALO + i * UNROLL + u
            x1[b - HALO] = apply(
                lambda c: src[:, column(0, c)],
                b,
                diag[b],
                lambda s: weights[s : s + 1, column(0, b)],
                lambda s: nb[s, b],
            )
        return 0

    lax.fori_loop(0, (BLOCKS - 2 * HALO) // UNROLL, step, 0)


def stencil_kernel(src, left, right, weights, diag, inner, nb, out, x0, x1, nbv, nbs, sems):
    nbv[0] = left[:, WIDE:].astype(jnp.int32)
    nbv[1] = right[:, WIDE:].astype(jnp.int32)
    copies = start_all(sems, [(nbv.at[k], nbs.at[k]) for k in range(2)])
    for half in range(2):
        rows = slice(half * SLAB, half * SLAB + SLAB)
        for j in range(HALO):
            cols = slice(j * LANES, (j + 1) * LANES)
            x0[half * HALO + j] = left[rows, cols]
            x0[2 * HALO + BLOCKS + half * HALO + j] = right[rows, cols]
    for j in range(BLOCKS):
        x0[2 * HALO + j] = src[:, j * LANES : (j + 1) * LANES]
    for j in range(BLOCKS - 2 * HALO):
        x1[2 * HALO + j] = inner[j]

    def own(b):
        x1[b + HALO] = apply(
            lambda c: x0[c],
            b + 2 * HALO,
            diag[b],
            lambda s: weights[s : s + 1, column(0, b)],
            lambda s: nb[s, b],
        )

    def far(side, ref, j):
        e = j + side * (HALO + BLOCKS)
        x1[e] = apply(
            lambda c: x0[c],
            e + HALO,
            jnp.sum(ref[:, column(NEAR, j)], axis=0, keepdims=True),
            lambda s: ref[s : s + 1, column(NEAR, j)],
            lambda s: nbs[side, s, j],
        )

    def first(i, _):
        for u in range(UNROLL):
            b = i * UNROLL + u
            own(b + jnp.where(b < HALO, 0, BLOCKS - 2 * HALO))
        return 0

    lax.fori_loop(0, 2 * HALO // UNROLL, first, 0)
    wait_all(copies)
    for side, ref in ((0, left), (1, right)):

        def outer(i, _, side=side, ref=ref):
            for u in range(UNROLL):
                far(side, ref, i * UNROLL + u)
            return 0

        lax.fori_loop(0, HALO // UNROLL, outer, 0)

    def second(i, _):
        for u in range(UNROLL):
            b = i * UNROLL + u
            part = lax.div(b, PART // LANES)
            cols = column(0, lax.rem(b, PART // LANES))
            e = b + HALO
            out[part, 0:SLAB, cols] = x1[e]
            out[part, SLAB : 2 * SLAB, cols] = apply(
                lambda c: x1[c],
                e,
                diag[b],
                lambda s: weights[s : s + 1, column(0, b)],
                lambda s: nb[s, b],
            )
        return 0

    lax.fori_loop(0, BLOCKS // UNROLL, second, 0)


def gram_kernel(z0, z12, to_modes, own, out, s):
    eig = own[0:1, :]
    for r in range(PARTS):
        rows = slice(r * SLAB, (r + 1) * SLAB)
        s[rows, 0:PART] = z0[r]
        for q in range(2):
            s[rows, (q + 1) * PART : (q + 2) * PART] = z12[r, q * SLAB : (q + 1) * SLAB, :]
    m = mm(to_modes[...], s[...])
    row = lax.broadcasted_iota(jnp.int32, (MODES, MODES), 0)
    col = lax.broadcasted_iota(jnp.int32, (MODES, MODES), 1)
    e = jnp.sum(jnp.where(row == col, eig, 0.0), axis=1, keepdims=True)
    m0, m1, m2 = (m[:, q * PART : (q + 1) * PART] for q in range(3))
    image = m1 + e * m0
    again = (m2 + e * m1) + e * image
    folded = []
    for a, b in ((m0, m0), (m0, image), (image, image), (m0, again), (image, again), (again, again)):
        p = a * b
        folded.append(sum(p[:, k * LANES : (k + 1) * LANES] for k in range(PART // LANES)))
    stack = jnp.concatenate(folded, axis=1)
    which = lax.broadcasted_iota(jnp.int32, (8, 6 * LANES), 1) // LANES
    pick = (which == lax.broadcasted_iota(jnp.int32, (8, 6 * LANES), 0)).astype(jnp.float32)
    g = lax.dot_general(
        pick, stack, (((1,), (1,)), ((), ())), precision=HIGHEST, preferred_element_type=jnp.float32
    )
    out[...] = jnp.broadcast_to(g[None], out.shape)


def relay_kernel(got, out):
    out[...] = jnp.broadcast_to(jnp.sum(got[...], axis=0)[None], out.shape)


def finish_kernel(place, got, z0, z12, to_modes, from_modes, own, out, mine, s):
    g = jnp.sum(got[...], axis=0)
    mm_, mi, ii, mj, ij, jj = (g[k : k + 1, :] for k in range(6))
    e = own[0:1, :]
    scale = mm_ + 1e-06
    upper = 1.5 * jnp.sqrt(ii / scale)
    lower = upper * 0.125
    center = (upper + lower) * 0.5
    half_width = (upper - lower) * 0.5
    sigma = center / half_width
    rho_zero = 1.0 / sigma
    rho_one = 1.0 / (2.0 * sigma - rho_zero)
    over = 1.0 / center
    c2 = 2.0 * rho_one / half_width
    u0 = rho_one * rho_zero * over + c2
    u1 = -c2 * over
    a = -over - u0
    b = -u1
    squares = mm_ + a * (2.0 * mi + a * ii) + b * (2.0 * (mj + a * ij) + b * jj)
    norm = jnp.broadcast_to(jnp.sqrt(jnp.maximum(squares, 0.0) / scale), (8, LANES))
    mine[...] = pltpu.roll(norm, LANES - place[0] * SLAB, 1)[0:1, 0:SLAB]
    for r in range(PARTS):
        s[r * SLAB : (r + 1) * SLAB, :] = z0[r]
        s[MODES + r * SLAB : MODES + (r + 1) * SLAB, :] = z12[r, 0:SLAB, :]
    from_m = from_modes[...]
    to_m = to_modes[...]
    mix = jnp.concatenate([mm(from_m * (over + u0 + u1 * e), to_m), mm(from_m * u1, to_m)], axis=1)
    out[...] = mm(mix, s[...]).reshape(out.shape)


def unpack_kernel(got, out):
    for r in range(PARTS):
        out[:, r * PART : (r + 1) * PART] = got[r]


def call(kernel, out_shape, in_specs, scratch=(), out_specs=None):
    if out_specs is None:
        out_specs = (VMEM,) * len(out_shape) if isinstance(out_shape, tuple) else VMEM
    return pl.pallas_call(
        kernel,
        out_shape=out_shape,
        in_specs=in_specs,
        out_specs=out_specs,
        scratch_shapes=scratch,
        compiler_params=pltpu.CompilerParams(vmem_limit_bytes=32 * 1024 * 1024),
    )


def on_device(sizes, source, to_modes, from_modes, eigenvalue, shifts, weights, neighbors):
    lat = sizes["y"] * sizes["z"]
    place = lax.axis_index(RAD).astype(jnp.int32).reshape(1)
    shift_row = shifts.reshape(1, -1)
    eig = eigenvalue.reshape(1, -1)
    up, down, own, dealt = call(
        pack_kernel,
        (f32(ROWS, WIDE + LANES), f32(ROWS, WIDE + LANES), f32(8, LANES), f32(PARTS, SLAB, PART)),
        [HBM] * 5,
        [
            pltpu.VMEM((STENCIL, BLOCKS), jnp.int32),
            pltpu.VMEM((2, STENCIL, NEAR), jnp.float32),
            pltpu.VMEM((2, 1, NEAR), jnp.float32),
            pltpu.VMEM((1, LANES), jnp.float32),
            pltpu.SemaphoreType.DMA((10 + PARTS,)),
        ],
    )(*(pltpu.with_memory_space_constraint(v, pltpu.HBM) for v in (source, weights, shift_row, neighbors, eig)))
    left = lax.ppermute(up, LAT, [(i, (i + 1) % lat) for i in range(lat)])
    right = lax.ppermute(down, LAT, [((i + 1) % lat, i) for i in range(lat)])
    z0 = lax.all_to_all(dealt, RAD, 0, 0, tiled=True)
    inner, diag, place = call(
        inner_kernel,
        (
            f32(BLOCKS - 2 * HALO, SLAB, LANES),
            f32(BLOCKS, 1, LANES),
            jax.ShapeDtypeStruct((1,), jnp.int32),
        ),
        [VMEM] * 3 + [SMEM] * 2,
        out_specs=(VMEM, VMEM, SMEM),
    )(source, weights, shift_row, neighbors, place)
    sent = call(
        stencil_kernel,
        f32(PARTS, 2 * SLAB, PART),
        [VMEM] * 6 + [SMEM],
        [
            pltpu.VMEM((EXT2, SLAB, LANES), jnp.float32),
            pltpu.VMEM((EXT1, SLAB, LANES), jnp.float32),
            pltpu.VMEM((2, ROWS, LANES), jnp.int32),
            pltpu.SMEM((2, ROWS, LANES), jnp.int32),
            pltpu.SemaphoreType.DMA((2,)),
        ],
    )(source, left, right, weights, diag, inner, neighbors)
    z12 = lax.all_to_all(sent, RAD, 0, 0, tiled=True)
    peers_1 = sizes["y"] * sizes["x"] * sizes["core"]
    peers_2 = sizes["z"]
    g = call(
        gram_kernel,
        f32(peers_1, 8, LANES),
        [VMEM] * 4,
        [pltpu.VMEM((MODES, 3 * PART), jnp.float32)],
    )(z0, z12, to_modes, own)
    g = lax.all_to_all(g, STAGE_1, 0, 0, tiled=True)
    g = call(relay_kernel, f32(peers_2, 8, LANES), [VMEM])(g)
    g = lax.all_to_all(g, STAGE_2, 0, 0, tiled=True)
    mixed, residual_norm = call(
        finish_kernel,
        (f32(PARTS, SLAB, PART), f32(1, SLAB)),
        [SMEM] + [VMEM] * 6,
        [pltpu.VMEM((2 * MODES, PART), jnp.float32)],
    )(place, g, z0, z12, to_modes, from_modes, own)
    got = lax.all_to_all(mixed, RAD, 0, 0, tiled=True)
    smoothed = call(unpack_kernel, f32(SLAB, BLOCKS * LANES), [VMEM])(got)
    return smoothed, residual_norm.reshape(SLAB)


def solution(mesh):
    names = ("y", "z", "x", "core")
    fine = Mesh(np.asarray(mesh.devices).reshape(4, 8, 4, 2), names)
    return jax.shard_map(
        functools.partial(on_device, dict(fine.shape)),
        mesh=fine,
        in_specs=(P(RAD, LAT), P(), P(), P(), P(LAT), P(None, LAT), P(None, LAT)),
        out_specs=(P(RAD, LAT), P(RAD)),
        check_vma=False,
    )
```

```python
import functools

import jax
import jax.numpy as jnp
import numpy as np
from jax import lax
from jax.experimental import pallas as pl
from jax.experimental.pallas import tpu as pltpu
from jax.sharding import Mesh, PartitionSpec as P

LANES = 128
HALO = 8
UNROLL = 8
STENCIL = 31
ROWS = STENCIL + 1
BLOCKS = 32
EXT1 = BLOCKS + 2 * HALO
EXT2 = BLOCKS + 4 * HALO
SLAB = 16
PARTS = 8
PART = BLOCKS * LANES // PARTS
MODES = 128
WIDE = 2 * HALO * LANES
NEAR = HALO * LANES
LAT = ("y", "z")
RAD = ("x", "core")
STAGE_1 = ("y", "x", "core")
STAGE_2 = "z"
VMEM = pl.BlockSpec(memory_space=pltpu.VMEM)
SMEM = pl.BlockSpec(memory_space=pltpu.SMEM)
HBM = pl.BlockSpec(memory_space=pltpu.HBM)
HIGHEST = lax.Precision.HIGHEST


def f32(*shape):
    return jax.ShapeDtypeStruct(shape, jnp.float32)


def split(a):
    high = a.astype(jnp.bfloat16)
    return high, (a - high.astype(jnp.float32)).astype(jnp.bfloat16)


def mm(a, b):
    (ah, al), (bh, bl) = split(a), split(b)
    dot = functools.partial(jnp.dot, preferred_element_type=jnp.float32)
    return dot(ah, bh) + (dot(ah, bl) + dot(al, bh))


def start_all(sems, pairs):
    copies = [pltpu.make_async_copy(src, dst, sems.at[k]) for k, (src, dst) in enumerate(pairs)]
    for copy in copies:
        copy.start()
    return copies


def wait_all(copies):
    for copy in copies:
        copy.wait()


def pack_kernel(src, weights, shifts, neighbors, eig, up, down, own, dealt, nb_in, w_in, sh_in, eig_in, sems):
    last = BLOCKS * LANES
    ends = ((up, last - WIDE, last - NEAR), (down, 0, 0))
    pairs = [(neighbors, nb_in), (eig, eig_in)]
    for k, (out, start, near) in enumerate(ends):
        pairs += [
            (weights.at[:, pl.ds(near, NEAR)], w_in.at[k]),
            (shifts.at[:, pl.ds(near, NEAR)], sh_in.at[k]),
            (src.at[:, pl.ds(start, NEAR)], out.at[0:SLAB, 0:NEAR]),
            (src.at[:, pl.ds(start + NEAR, NEAR)], out.at[SLAB : 2 * SLAB, 0:NEAR]),
        ]
    pairs += [(src.at[:, pl.ds(r * PART, PART)], dealt.at[r]) for r in range(PARTS)]
    copies = start_all(sems, pairs)
    wait_all(copies[: -PARTS])
    nb = nb_in[...].astype(jnp.float32)
    for k, (out, first) in enumerate(((up, BLOCKS - HALO), (down, 0))):
        out[0:STENCIL, NEAR:WIDE] = w_in[k]
        out[STENCIL:ROWS, NEAR:WIDE] = sh_in[k]
        out[:, WIDE:] = jnp.zeros((ROWS, LANES), jnp.float32)
        out[0:STENCIL, WIDE : WIDE + HALO] = nb[:, first : first + HALO]
    own[...] = jnp.broadcast_to(eig_in[...], own.shape)
    wait_all(copies[-PARTS:])


def column(start, block):
    return pl.ds(pl.multiple_of(start + block * LANES, LANES), LANES)


def apply(read, centre, d, weight, offset):
    acc = d * read(centre)
    for s in range(STENCIL):
        moved = read(offset(s) + centre)
        if s:
            moved = pltpu.roll(moved, LANES - s, 1)
        acc = acc - weight(s) * moved
    return acc


def inner_kernel(src, weights, shifts, nb_in, place_in, x1, diag, place, nb, sems):
    copies = start_all(sems, [(nb_in, nb)])
    place[...] = place_in[...]
    for j in range(BLOCKS):
        cols = slice(j * LANES, (j + 1) * LANES)
        diag[j] = jnp.sum(weights[:, cols], axis=0, keepdims=True) + shifts[:, cols]
    wait_all(copies)

    def step(i, _):
        for u in range(UNROLL):
            b = HALO + i * UNROLL + u
            x1[b - HALO] = apply(
                lambda c: src[:, column(0, c)],
                b,
                diag[b],
                lambda s: weights[s : s + 1, column(0, b)],
                lambda s: nb[s, b],
            )
        return 0

    lax.fori_loop(0, (BLOCKS - 2 * HALO) // UNROLL, step, 0)


def stencil_kernel(src, left, right, weights, diag, inner, nb_in, out, x0, x1, nbv, nbs, nb, sems):
    nbv[0] = left[:, WIDE:].astype(jnp.int32)
    nbv[1] = right[:, WIDE:].astype(jnp.int32)
    copies = start_all(sems, [(nb_in, nb)] + [(nbv.at[k], nbs.at[k]) for k in range(2)])
    for half in range(2):
        rows = slice(half * SLAB, half * SLAB + SLAB)
        for j in range(HALO):
            cols = slice(j * LANES, (j + 1) * LANES)
            x0[half * HALO + j] = left[rows, cols]
            x0[2 * HALO + BLOCKS + half * HALO + j] = right[rows, cols]
    for j in range(BLOCKS):
        x0[2 * HALO + j] = src[:, j * LANES : (j + 1) * LANES]
    for j in range(BLOCKS - 2 * HALO):
        x1[2 * HALO + j] = inner[j]

    def own(b):
        x1[b + HALO] = apply(
            lambda c: x0[c],
            b + 2 * HALO,
            diag[b],
            lambda s: weights[s : s + 1, column(0, b)],
            lambda s: nb[s, b],
        )

    def far(side, ref, j):
        e = j + side * (HALO + BLOCKS)
        x1[e] = apply(
            lambda c: x0[c],
            e + HALO,
            jnp.sum(ref[:, column(NEAR, j)], axis=0, keepdims=True),
            lambda s: ref[s : s + 1, column(NEAR, j)],
            lambda s: nbs[side, s, j],
        )

    def first(i, _):
        for u in range(UNROLL):
            b = i * UNROLL + u
            own(b + jnp.where(b < HALO, 0, BLOCKS - 2 * HALO))
        return 0

    copies[0].wait()
    lax.fori_loop(0, 2 * HALO // UNROLL, first, 0)
    wait_all(copies[1:])
    for side, ref in ((0, left), (1, right)):

        def outer(i, _, side=side, ref=ref):
            for u in range(UNROLL):
                far(side, ref, i * UNROLL + u)
            return 0

        lax.fori_loop(0, HALO // UNROLL, outer, 0)

    def second(i, _):
        for u in range(UNROLL):
            b = i * UNROLL + u
            part = lax.div(b, PART // LANES)
            cols = column(0, lax.rem(b, PART // LANES))
            e = b + HALO
            out[part, 0:SLAB, cols] = x1[e]
            out[part, SLAB : 2 * SLAB, cols] = apply(
                lambda c: x1[c],
                e,
                diag[b],
                lambda s: weights[s : s + 1, column(0, b)],
                lambda s: nb[s, b],
            )
        return 0

    lax.fori_loop(0, BLOCKS // UNROLL, second, 0)


def gram_kernel(z0, z12, to_modes, own, out, s):
    eig = own[0:1, :]
    for r in range(PARTS):
        rows = slice(r * SLAB, (r + 1) * SLAB)
        s[rows, 0:PART] = z0[r]
        for q in range(2):
            s[rows, (q + 1) * PART : (q + 2) * PART] = z12[r, q * SLAB : (q + 1) * SLAB, :]
    m = mm(to_modes[...], s[...])
    row = lax.broadcasted_iota(jnp.int32, (MODES, MODES), 0)
    col = lax.broadcasted_iota(jnp.int32, (MODES, MODES), 1)
    e = jnp.sum(jnp.where(row == col, eig, 0.0), axis=1, keepdims=True)
    m0, m1, m2 = (m[:, q * PART : (q + 1) * PART] for q in range(3))
    image = m1 + e * m0
    again = (m2 + e * m1) + e * image
    folded = []
    for a, b in ((m0, m0), (m0, image), (image, image), (m0, again), (image, again), (again, again)):
        p = a * b
        folded.append(sum(p[:, k * LANES : (k + 1) * LANES] for k in range(PART // LANES)))
    stack = jnp.concatenate(folded, axis=1)
    which = lax.broadcasted_iota(jnp.int32, (8, 6 * LANES), 1) // LANES
    pick = (which == lax.broadcasted_iota(jnp.int32, (8, 6 * LANES), 0)).astype(jnp.float32)
    g = lax.dot_general(
        pick, stack, (((1,), (1,)), ((), ())), precision=HIGHEST, preferred_element_type=jnp.float32
    )
    out[...] = jnp.broadcast_to(g[None], out.shape)


def relay_kernel(got, out):
    out[...] = jnp.broadcast_to(jnp.sum(got[...], axis=0)[None], out.shape)


def finish_kernel(place, got, z0, z12, to_modes, from_modes, own, out, mine, s):
    g = jnp.sum(got[...], axis=0)
    mm_, mi, ii, mj, ij, jj = (g[k : k + 1, :] for k in range(6))
    e = own[0:1, :]
    scale = mm_ + 1e-06
    upper = 1.5 * jnp.sqrt(ii / scale)
    lower = upper * 0.125
    center = (upper + lower) * 0.5
    half_width = (upper - lower) * 0.5
    sigma = center / half_width
    rho_zero = 1.0 / sigma
    rho_one = 1.0 / (2.0 * sigma - rho_zero)
    over = 1.0 / center
    c2 = 2.0 * rho_one / half_width
    u0 = rho_one * rho_zero * over + c2
    u1 = -c2 * over
    a = -over - u0
    b = -u1
    squares = mm_ + a * (2.0 * mi + a * ii) + b * (2.0 * (mj + a * ij) + b * jj)
    norm = jnp.sqrt(jnp.maximum(squares, 0.0) / scale)
    here = place[0:1, 0:SLAB]
    picked = norm[:, 0:SLAB]
    for r in range(1, PARTS):
        picked = jnp.where(here == r, norm[:, r * SLAB : (r + 1) * SLAB], picked)
    mine[...] = picked
    for r in range(PARTS):
        s[r * SLAB : (r + 1) * SLAB, :] = z0[r]
        s[MODES + r * SLAB : MODES + (r + 1) * SLAB, :] = z12[r, 0:SLAB, :]
    from_m = from_modes[...]
    to_m = to_modes[...]
    mix = jnp.concatenate([mm(from_m * (over + u0 + u1 * e), to_m), mm(from_m * u1, to_m)], axis=1)
    out[...] = mm(mix, s[...]).reshape(out.shape)


def unpack_kernel(got, out, sems):
    wait_all(
        start_all(sems, [(got.at[r], out.at[:, pl.ds(r * PART, PART)]) for r in range(PARTS)])
    )


def call(kernel, out_shape, in_specs, scratch=(), out_specs=None):
    if out_specs is None:
        out_specs = (VMEM,) * len(out_shape) if isinstance(out_shape, tuple) else VMEM
    return pl.pallas_call(
        kernel,
        out_shape=out_shape,
        in_specs=in_specs,
        out_specs=out_specs,
        scratch_shapes=scratch,
        compiler_params=pltpu.CompilerParams(vmem_limit_bytes=32 * 1024 * 1024),
    )


def pinned(value):
    return pltpu.with_memory_space_constraint(value, pltpu.HBM)


def on_device(sizes, source, to_modes, from_modes, eigenvalue, shifts, weights, neighbors):
    lat = sizes["y"] * sizes["z"]
    place = jnp.full((8, LANES), lax.axis_index(RAD).astype(jnp.float32))
    shift_row = shifts.reshape(1, -1)
    eig = eigenvalue.reshape(1, -1)
    up, down, own, dealt = call(
        pack_kernel,
        (f32(ROWS, WIDE + LANES), f32(ROWS, WIDE + LANES), f32(8, LANES), f32(PARTS, SLAB, PART)),
        [HBM] * 5,
        [
            pltpu.VMEM((STENCIL, BLOCKS), jnp.int32),
            pltpu.VMEM((2, STENCIL, NEAR), jnp.float32),
            pltpu.VMEM((2, 1, NEAR), jnp.float32),
            pltpu.VMEM((1, LANES), jnp.float32),
            pltpu.SemaphoreType.DMA((10 + PARTS,)),
        ],
        out_specs=(VMEM, VMEM, VMEM, HBM),
    )(*(pinned(v) for v in (source, weights, shift_row, neighbors, eig)))
    left = lax.ppermute(up, LAT, [(i, (i + 1) % lat) for i in range(lat)])
    right = lax.ppermute(down, LAT, [((i + 1) % lat, i) for i in range(lat)])
    z0 = lax.all_to_all(dealt, RAD, 0, 0, tiled=True)
    inner, diag, place = call(
        inner_kernel,
        (
            f32(BLOCKS - 2 * HALO, SLAB, LANES),
            f32(BLOCKS, 1, LANES),
            f32(8, LANES),
        ),
        [VMEM] * 3 + [HBM, VMEM],
        [pltpu.SMEM((STENCIL, BLOCKS), jnp.int32), pltpu.SemaphoreType.DMA((1,))],
    )(source, weights, shift_row, pinned(neighbors), place)
    sent = call(
        stencil_kernel,
        f32(PARTS, 2 * SLAB, PART),
        [VMEM] * 6 + [HBM],
        [
            pltpu.VMEM((EXT2, SLAB, LANES), jnp.float32),
            pltpu.VMEM((EXT1, SLAB, LANES), jnp.float32),
            pltpu.VMEM((2, ROWS, LANES), jnp.int32),
            pltpu.SMEM((2, ROWS, LANES), jnp.int32),
            pltpu.SMEM((STENCIL, BLOCKS), jnp.int32),
            pltpu.SemaphoreType.DMA((3,)),
        ],
    )(source, left, right, weights, diag, inner, pinned(neighbors))
    z12 = lax.all_to_all(sent, RAD, 0, 0, tiled=True)
    peers_1 = sizes["y"] * sizes["x"] * sizes["core"]
    peers_2 = sizes["z"]
    g = call(
        gram_kernel,
        f32(peers_1, 8, LANES),
        [VMEM] * 4,
        [pltpu.VMEM((MODES, 3 * PART), jnp.float32)],
    )(z0, z12, to_modes, own)
    g = lax.all_to_all(g, STAGE_1, 0, 0, tiled=True)
    g = call(relay_kernel, f32(peers_2, 8, LANES), [VMEM])(g)
    g = lax.all_to_all(g, STAGE_2, 0, 0, tiled=True)
    mixed, residual_norm = call(
        finish_kernel,
        (f32(PARTS, SLAB, PART), f32(1, SLAB)),
        [VMEM] * 7,
        [pltpu.VMEM((2 * MODES, PART), jnp.float32)],
    )(place, g, z0, z12, to_modes, from_modes, own)
    got = lax.all_to_all(mixed, RAD, 0, 0, tiled=True)
    smoothed = call(
        unpack_kernel,
        f32(SLAB, BLOCKS * LANES),
        [VMEM],
        [pltpu.SemaphoreType.DMA((PARTS,))],
        out_specs=HBM,
    )(got)
    return smoothed, residual_norm.reshape(SLAB)


def solution(mesh):
    names = ("y", "z", "x", "core")
    fine = Mesh(np.asarray(mesh.devices).reshape(4, 8, 4, 2), names)
    return jax.shard_map(
        functools.partial(on_device, dict(fine.shape)),
        mesh=fine,
        in_specs=(P(RAD, LAT), P(), P(), P(), P(LAT), P(None, LAT), P(None, LAT)),
        out_specs=(P(RAD, LAT), P(RAD)),
        check_vma=False,
    )
```

```python
import functools

import jax
import jax.numpy as jnp
import numpy as np
from jax import lax
from jax.experimental import pallas as pl
from jax.experimental.pallas import tpu as pltpu
from jax.sharding import Mesh, PartitionSpec as P

LANES = 128
HALO = 8
UNROLL = 8
STENCIL = 31
ROWS = STENCIL + 1
BLOCKS = 32
EXT1 = BLOCKS + 2 * HALO
EXT2 = BLOCKS + 4 * HALO
SLAB = 16
PARTS = 8
PART = BLOCKS * LANES // PARTS
MODES = 128
WIDE = 2 * HALO * LANES
NEAR = HALO * LANES
LAT = ("y", "z")
RAD = ("x", "core")
STAGE_1 = ("y", "x", "core")
STAGE_2 = "z"
VMEM = pl.BlockSpec(memory_space=pltpu.VMEM)
SMEM = pl.BlockSpec(memory_space=pltpu.SMEM)
HBM = pl.BlockSpec(memory_space=pltpu.HBM)
HIGHEST = lax.Precision.HIGHEST


def f32(*shape):
    return jax.ShapeDtypeStruct(shape, jnp.float32)


def split(a):
    high = a.astype(jnp.bfloat16)
    return high, (a - high.astype(jnp.float32)).astype(jnp.bfloat16)


def mm(a, b):
    (ah, al), (bh, bl) = split(a), split(b)
    dot = functools.partial(jnp.dot, preferred_element_type=jnp.float32)
    return dot(ah, bh) + (dot(ah, bl) + dot(al, bh))


def start_all(sems, pairs):
    copies = [pltpu.make_async_copy(src, dst, sems.at[k]) for k, (src, dst) in enumerate(pairs)]
    for copy in copies:
        copy.start()
    return copies


def wait_all(copies):
    for copy in copies:
        copy.wait()


def pack_kernel(src, weights, shifts, neighbors, eig, up, down, own, nb_in, sh_in, w_in, eig_in, sems):
    last = BLOCKS * LANES
    ends = ((up, last - WIDE, last - NEAR), (down, 0, 0))
    pairs = [(neighbors, nb_in), (eig, eig_in), (shifts, sh_in)]
    for k, (out, start, near) in enumerate(ends):
        pairs += [
            (weights.at[:, pl.ds(near, NEAR)], w_in.at[k]),
            (src.at[:, pl.ds(start, NEAR)], out.at[0:SLAB, 0:NEAR]),
            (src.at[:, pl.ds(start + NEAR, NEAR)], out.at[SLAB : 2 * SLAB, 0:NEAR]),
        ]
    wait_all(start_all(sems, pairs))
    nb = nb_in[...].astype(jnp.float32)
    for k, (out, first) in enumerate(((up, BLOCKS - HALO), (down, 0))):
        near = first * LANES
        out[0:STENCIL, NEAR:WIDE] = w_in[k]
        out[STENCIL:ROWS, NEAR:WIDE] = sh_in[:, near : near + NEAR]
        out[:, WIDE:] = jnp.zeros((ROWS, LANES), jnp.float32)
        out[0:STENCIL, WIDE : WIDE + HALO] = nb[:, first : first + HALO]
    own[...] = jnp.broadcast_to(eig_in[...], own.shape)


def column(start, block):
    return pl.ds(pl.multiple_of(start + block * LANES, LANES), LANES)


def apply(read, centre, d, weight, offset):
    acc = d * read(centre)
    for s in range(STENCIL):
        moved = read(offset(s) + centre)
        if s:
            moved = pltpu.roll(moved, LANES - s, 1)
        acc = acc - weight(s) * moved
    return acc


def inner_kernel(src, weights, shifts, nb_in, place_in, x1, diag, place, dealt, nb, sems):
    copies = start_all(sems, [(nb_in, nb)])
    place[...] = place_in[...]
    for r in range(PARTS):
        dealt[r] = src[:, r * PART : (r + 1) * PART]
    for j in range(BLOCKS):
        cols = slice(j * LANES, (j + 1) * LANES)
        diag[j] = jnp.sum(weights[:, cols], axis=0, keepdims=True) + shifts[:, cols]
    wait_all(copies)

    def step(i, _):
        for u in range(UNROLL):
            b = HALO + i * UNROLL + u
            x1[b - HALO] = apply(
                lambda c: src[:, column(0, c)],
                b,
                diag[b],
                lambda s: weights[s : s + 1, column(0, b)],
                lambda s: nb[s, b],
            )
        return 0

    lax.fori_loop(0, (BLOCKS - 2 * HALO) // UNROLL, step, 0)


def stencil_kernel(src, left, right, weights, diag, inner, nb_in, out, x0, x1, nbv, nbs, nb, sems):
    nbv[0] = left[:, WIDE:].astype(jnp.int32)
    nbv[1] = right[:, WIDE:].astype(jnp.int32)
    copies = start_all(sems, [(nb_in, nb)] + [(nbv.at[k], nbs.at[k]) for k in range(2)])
    for half in range(2):
        rows = slice(half * SLAB, half * SLAB + SLAB)
        for j in range(HALO):
            cols = slice(j * LANES, (j + 1) * LANES)
            x0[half * HALO + j] = left[rows, cols]
            x0[2 * HALO + BLOCKS + half * HALO + j] = right[rows, cols]
    for j in range(BLOCKS):
        x0[2 * HALO + j] = src[:, j * LANES : (j + 1) * LANES]
    for j in range(BLOCKS - 2 * HALO):
        x1[2 * HALO + j] = inner[j]

    def own(b):
        x1[b + HALO] = apply(
            lambda c: x0[c],
            b + 2 * HALO,
            diag[b],
            lambda s: weights[s : s + 1, column(0, b)],
            lambda s: nb[s, b],
        )

    def far(side, ref, j):
        e = j + side * (HALO + BLOCKS)
        x1[e] = apply(
            lambda c: x0[c],
            e + HALO,
            jnp.sum(ref[:, column(NEAR, j)], axis=0, keepdims=True),
            lambda s: ref[s : s + 1, column(NEAR, j)],
            lambda s: nbs[side, s, j],
        )

    def first(i, _):
        for u in range(UNROLL):
            b = i * UNROLL + u
            own(b + jnp.where(b < HALO, 0, BLOCKS - 2 * HALO))
        return 0

    copies[0].wait()
    lax.fori_loop(0, 2 * HALO // UNROLL, first, 0)
    wait_all(copies[1:])
    for side, ref in ((0, left), (1, right)):

        def outer(i, _, side=side, ref=ref):
            for u in range(UNROLL):
                far(side, ref, i * UNROLL + u)
            return 0

        lax.fori_loop(0, HALO // UNROLL, outer, 0)

    def second(i, _):
        for u in range(UNROLL):
            b = i * UNROLL + u
            part = lax.div(b, PART // LANES)
            cols = column(0, lax.rem(b, PART // LANES))
            e = b + HALO
            out[part, 0:SLAB, cols] = x1[e]
            out[part, SLAB : 2 * SLAB, cols] = apply(
                lambda c: x1[c],
                e,
                diag[b],
                lambda s: weights[s : s + 1, column(0, b)],
                lambda s: nb[s, b],
            )
        return 0

    lax.fori_loop(0, BLOCKS // UNROLL, second, 0)


def gram_kernel(z0, z12, to_modes, own, out, s):
    eig = own[0:1, :]
    for r in range(PARTS):
        rows = slice(r * SLAB, (r + 1) * SLAB)
        s[rows, 0:PART] = z0[r]
        for q in range(2):
            s[rows, (q + 1) * PART : (q + 2) * PART] = z12[r, q * SLAB : (q + 1) * SLAB, :]
    m = mm(to_modes[...], s[...])
    row = lax.broadcasted_iota(jnp.int32, (MODES, MODES), 0)
    col = lax.broadcasted_iota(jnp.int32, (MODES, MODES), 1)
    e = jnp.sum(jnp.where(row == col, eig, 0.0), axis=1, keepdims=True)
    m0, m1, m2 = (m[:, q * PART : (q + 1) * PART] for q in range(3))
    image = m1 + e * m0
    again = (m2 + e * m1) + e * image
    folded = []
    for a, b in ((m0, m0), (m0, image), (image, image), (m0, again), (image, again), (again, again)):
        p = a * b
        folded.append(sum(p[:, k * LANES : (k + 1) * LANES] for k in range(PART // LANES)))
    stack = jnp.concatenate(folded, axis=1)
    which = lax.broadcasted_iota(jnp.int32, (8, 6 * LANES), 1) // LANES
    pick = (which == lax.broadcasted_iota(jnp.int32, (8, 6 * LANES), 0)).astype(jnp.float32)
    g = lax.dot_general(
        pick, stack, (((1,), (1,)), ((), ())), precision=HIGHEST, preferred_element_type=jnp.float32
    )
    out[...] = jnp.broadcast_to(g[None], out.shape)


def relay_kernel(got, out):
    out[...] = jnp.broadcast_to(jnp.sum(got[...], axis=0)[None], out.shape)


def finish_kernel(place, got, z0, z12, to_modes, from_modes, own, out, mine, s):
    g = jnp.sum(got[...], axis=0)
    mm_, mi, ii, mj, ij, jj = (g[k : k + 1, :] for k in range(6))
    e = own[0:1, :]
    scale = mm_ + 1e-06
    upper = 1.5 * jnp.sqrt(ii / scale)
    lower = upper * 0.125
    center = (upper + lower) * 0.5
    half_width = (upper - lower) * 0.5
    sigma = center / half_width
    rho_zero = 1.0 / sigma
    rho_one = 1.0 / (2.0 * sigma - rho_zero)
    over = 1.0 / center
    c2 = 2.0 * rho_one / half_width
    u0 = rho_one * rho_zero * over + c2
    u1 = -c2 * over
    a = -over - u0
    b = -u1
    squares = mm_ + a * (2.0 * mi + a * ii) + b * (2.0 * (mj + a * ij) + b * jj)
    norm = jnp.sqrt(jnp.maximum(squares, 0.0) / scale)
    here = place[0:1, 0:SLAB]
    picked = norm[:, 0:SLAB]
    for r in range(1, PARTS):
        picked = jnp.where(here == r, norm[:, r * SLAB : (r + 1) * SLAB], picked)
    mine[...] = picked
    for r in range(PARTS):
        s[r * SLAB : (r + 1) * SLAB, :] = z0[r]
        s[MODES + r * SLAB : MODES + (r + 1) * SLAB, :] = z12[r, 0:SLAB, :]
    from_m = from_modes[...]
    to_m = to_modes[...]
    mix = jnp.concatenate([mm(from_m * (over + u0 + u1 * e), to_m), mm(from_m * u1, to_m)], axis=1)
    out[...] = mm(mix, s[...]).reshape(out.shape)


def unpack_kernel(got, out):
    for r in range(PARTS):
        out[:, r * PART : (r + 1) * PART] = got[r]


def call(kernel, out_shape, in_specs, scratch=(), out_specs=None):
    if out_specs is None:
        out_specs = (VMEM,) * len(out_shape) if isinstance(out_shape, tuple) else VMEM
    return pl.pallas_call(
        kernel,
        out_shape=out_shape,
        in_specs=in_specs,
        out_specs=out_specs,
        scratch_shapes=scratch,
        compiler_params=pltpu.CompilerParams(vmem_limit_bytes=32 * 1024 * 1024),
    )


def pinned(value):
    return pltpu.with_memory_space_constraint(value, pltpu.HBM)


def on_device(sizes, source, to_modes, from_modes, eigenvalue, shifts, weights, neighbors):
    lat = sizes["y"] * sizes["z"]
    place = jnp.full((8, LANES), lax.axis_index(RAD).astype(jnp.float32))
    shift_row = shifts.reshape(1, -1)
    eig = eigenvalue.reshape(1, -1)
    up, down, own, nb, shift_row = call(
        pack_kernel,
        (f32(ROWS, WIDE + LANES), f32(ROWS, WIDE + LANES), f32(8, LANES),
         jax.ShapeDtypeStruct(neighbors.shape, neighbors.dtype), f32(1, BLOCKS * LANES)),
        [HBM] * 5,
        [
            pltpu.VMEM((2, STENCIL, NEAR), jnp.float32),
            pltpu.VMEM((1, LANES), jnp.float32),
            pltpu.SemaphoreType.DMA((9,)),
        ],
    )(*(pinned(v) for v in (source, weights, shift_row, neighbors, eig)))
    left = lax.ppermute(up, LAT, [(i, (i + 1) % lat) for i in range(lat)])
    right = lax.ppermute(down, LAT, [((i + 1) % lat, i) for i in range(lat)])
    inner, diag, place, dealt = call(
        inner_kernel,
        (
            f32(BLOCKS - 2 * HALO, SLAB, LANES),
            f32(BLOCKS, 1, LANES),
            f32(8, LANES),
            f32(PARTS, SLAB, PART),
        ),
        [VMEM] * 5,
        [pltpu.SMEM((STENCIL, BLOCKS), jnp.int32), pltpu.SemaphoreType.DMA((1,))],
    )(source, weights, shift_row, nb, place)
    z0 = lax.all_to_all(dealt, RAD, 0, 0, tiled=True)
    sent = call(
        stencil_kernel,
        f32(PARTS, 2 * SLAB, PART),
        [VMEM] * 7,
        [
            pltpu.VMEM((EXT2, SLAB, LANES), jnp.float32),
            pltpu.VMEM((EXT1, SLAB, LANES), jnp.float32),
            pltpu.VMEM((2, ROWS, LANES), jnp.int32),
            pltpu.SMEM((2, ROWS, LANES), jnp.int32),
            pltpu.SMEM((STENCIL, BLOCKS), jnp.int32),
            pltpu.SemaphoreType.DMA((3,)),
        ],
    )(source, left, right, weights, diag, inner, nb)
    z12 = lax.all_to_all(sent, RAD, 0, 0, tiled=True)
    peers_1 = sizes["y"] * sizes["x"] * sizes["core"]
    peers_2 = sizes["z"]
    g = call(
        gram_kernel,
        f32(peers_1, 8, LANES),
        [VMEM] * 4,
        [pltpu.VMEM((MODES, 3 * PART), jnp.float32)],
    )(z0, z12, to_modes, own)
    g = lax.all_to_all(g, STAGE_1, 0, 0, tiled=True)
    g = call(relay_kernel, f32(peers_2, 8, LANES), [VMEM])(g)
    g = lax.all_to_all(g, STAGE_2, 0, 0, tiled=True)
    mixed, residual_norm = call(
        finish_kernel,
        (f32(PARTS, SLAB, PART), f32(1, SLAB)),
        [VMEM] * 7,
        [pltpu.VMEM((2 * MODES, PART), jnp.float32)],
    )(place, g, z0, z12, to_modes, from_modes, own)
    got = lax.all_to_all(mixed, RAD, 0, 0, tiled=True)
    smoothed = call(unpack_kernel, f32(SLAB, BLOCKS * LANES), [VMEM])(got)
    return smoothed, residual_norm.reshape(SLAB)


def solution(mesh):
    names = ("y", "z", "x", "core")
    fine = Mesh(np.asarray(mesh.devices).reshape(4, 8, 4, 2), names)
    return jax.shard_map(
        functools.partial(on_device, dict(fine.shape)),
        mesh=fine,
        in_specs=(P(RAD, LAT), P(), P(), P(), P(LAT), P(None, LAT), P(None, LAT)),
        out_specs=(P(RAD, LAT), P(RAD)),
        check_vma=False,
    )
```

```python
import functools

import jax
import jax.numpy as jnp
import numpy as np
from jax import lax
from jax.experimental import pallas as pl
from jax.experimental.pallas import tpu as pltpu
from jax.sharding import Mesh, PartitionSpec as P

LANES = 128
HALO = 8
UNROLL = 8
STENCIL = 31
ROWS = STENCIL + 1
BLOCKS = 32
EXT1 = BLOCKS + 2 * HALO
EXT2 = BLOCKS + 4 * HALO
SLAB = 16
PARTS = 8
PART = BLOCKS * LANES // PARTS
MODES = 128
FLAT = SLAB * PART // LANES
WIDE = 2 * HALO * LANES
NEAR = HALO * LANES
LAT = ("y", "z")
RAD = ("x", "core")
VMEM = pl.BlockSpec(memory_space=pltpu.VMEM)
SMEM = pl.BlockSpec(memory_space=pltpu.SMEM)
HBM = pl.BlockSpec(memory_space=pltpu.HBM)
HIGHEST = lax.Precision.HIGHEST


def f32(*shape):
    return jax.ShapeDtypeStruct(shape, jnp.float32)


def split(a):
    high = a.astype(jnp.bfloat16)
    return high, (a - high.astype(jnp.float32)).astype(jnp.bfloat16)


def mm(a, b):
    (ah, al), (bh, bl) = split(a), split(b)
    dot = functools.partial(jnp.dot, preferred_element_type=jnp.float32)
    return dot(ah, bh) + (dot(ah, bl) + dot(al, bh))


def start_all(sems, pairs):
    copies = [pltpu.make_async_copy(src, dst, sems.at[k]) for k, (src, dst) in enumerate(pairs)]
    for copy in copies:
        copy.start()
    return copies


def wait_all(copies):
    for copy in copies:
        copy.wait()


def pack_kernel(src, weights, shifts, neighbors, eig, up, down, own, nb_in, sh_in, w_in, eig_in, sems):
    last = BLOCKS * LANES
    ends = ((up, last - WIDE, last - NEAR), (down, 0, 0))
    pairs = [(neighbors, nb_in), (eig, eig_in), (shifts, sh_in)]
    for k, (out, start, near) in enumerate(ends):
        pairs += [
            (weights.at[:, pl.ds(near, NEAR)], w_in.at[k]),
            (src.at[:, pl.ds(start, NEAR)], out.at[0:SLAB, 0:NEAR]),
            (src.at[:, pl.ds(start + NEAR, NEAR)], out.at[SLAB : 2 * SLAB, 0:NEAR]),
        ]
    wait_all(start_all(sems, pairs))
    nb = nb_in[...].astype(jnp.float32)
    for k, (out, first) in enumerate(((up, BLOCKS - HALO), (down, 0))):
        near = first * LANES
        out[0:STENCIL, NEAR:WIDE] = w_in[k]
        out[STENCIL:ROWS, NEAR:WIDE] = sh_in[:, near : near + NEAR]
        out[:, WIDE:] = jnp.zeros((ROWS, LANES), jnp.float32)
        out[0:STENCIL, WIDE : WIDE + HALO] = nb[:, first : first + HALO]
    own[...] = jnp.broadcast_to(eig_in[...], own.shape)


def column(start, block):
    return pl.ds(pl.multiple_of(start + block * LANES, LANES), LANES)


def apply(read, centre, d, weight, offset):
    acc = d * read(centre)
    for s in range(STENCIL):
        moved = read(offset(s) + centre)
        if s:
            moved = pltpu.roll(moved, LANES - s, 1)
        acc = acc - weight(s) * moved
    return acc


def inner_kernel(src, weights, shifts, nb_in, place_in, x1, diag, place, dealt, nb, sems):
    copies = start_all(sems, [(nb_in, nb)])
    place[...] = place_in[...]
    for r in range(PARTS):
        dealt[r] = src[:, r * PART : (r + 1) * PART]
    for j in range(BLOCKS):
        cols = slice(j * LANES, (j + 1) * LANES)
        diag[j] = jnp.sum(weights[:, cols], axis=0, keepdims=True) + shifts[:, cols]
    wait_all(copies)

    def step(i, _):
        for u in range(UNROLL):
            b = HALO + i * UNROLL + u
            x1[b - HALO] = apply(
                lambda c: src[:, column(0, c)],
                b,
                diag[b],
                lambda s: weights[s : s + 1, column(0, b)],
                lambda s: nb[s, b],
            )
        return 0

    lax.fori_loop(0, (BLOCKS - 2 * HALO) // UNROLL, step, 0)


def edge_kernel(src, left, right, weights, diag, inner, nb_in, out, x0, x1, nb, sems):
    copies = start_all(sems, [(nb_in, nb)])
    for half in range(2):
        rows = slice(half * SLAB, half * SLAB + SLAB)
        for j in range(HALO):
            cols = slice(j * LANES, (j + 1) * LANES)
            x0[half * HALO + j] = left[rows, cols]
            x0[2 * HALO + BLOCKS + half * HALO + j] = right[rows, cols]
    for j in range(BLOCKS):
        x0[2 * HALO + j] = src[:, j * LANES : (j + 1) * LANES]
    for j in range(HALO, BLOCKS - HALO):
        x1[j] = inner[j - HALO]
        part, place = divmod(j, PART // LANES)
        out[part, :, place * LANES : (place + 1) * LANES] = inner[j - HALO]
    wait_all(copies)

    def step(i, _):
        for u in range(UNROLL):
            b = i * (BLOCKS - HALO) + u
            value = apply(
                lambda c: x0[c],
                b + 2 * HALO,
                diag[b],
                lambda s: weights[s : s + 1, column(0, b)],
                lambda s: nb[s, b],
            )
            x1[b] = value
            out[lax.div(b, PART // LANES), :, column(0, lax.rem(b, PART // LANES))] = value
        return 0

    lax.fori_loop(0, 2, step, 0)


def outer_kernel(x0, x1_own, left, right, weights, diag, nb_in, out, x1, nbv, nbs, nb, sems):
    nbv[0] = left[:, WIDE:].astype(jnp.int32)
    nbv[1] = right[:, WIDE:].astype(jnp.int32)
    copies = start_all(sems, [(nbv.at[k], nbs.at[k]) for k in range(2)] + [(nb_in, nb)])
    for j in range(BLOCKS):
        x1[HALO + j] = x1_own[j]
    wait_all(copies)
    for side, ref in ((0, left), (1, right)):
        for j in range(HALO):
            e = j + side * (HALO + BLOCKS)
            cols = slice(NEAR + j * LANES, NEAR + (j + 1) * LANES)
            x1[e] = apply(
                lambda c: x0[c],
                e + HALO,
                jnp.sum(ref[:, cols], axis=0, keepdims=True),
                lambda s: ref[s : s + 1, cols],
                lambda s: nbs[side, s, j],
            )

    def step(i, _):
        for u in range(UNROLL):
            b = i * UNROLL + u
            rows = pl.ds(pl.multiple_of(lax.rem(b, PART // LANES) * SLAB, SLAB), SLAB)
            out[lax.div(b, PART // LANES), rows, :] = apply(
                lambda c: x1[c],
                b + HALO,
                diag[b],
                lambda s: weights[s : s + 1, column(0, b)],
                lambda s: nb[s, b],
            )
        return 0

    lax.fori_loop(0, BLOCKS // UNROLL, step, 0)


def sums(pairs, first):
    folded = []
    for a, b in pairs:
        p = a * b
        folded.append(sum(p[:, k * LANES : (k + 1) * LANES] for k in range(PART // LANES)))
    stack = jnp.concatenate(folded, axis=1)
    shape = (8, stack.shape[1])
    which = lax.broadcasted_iota(jnp.int32, shape, 1) // LANES + first
    pick = (which == lax.broadcasted_iota(jnp.int32, shape, 0)).astype(jnp.float32)
    return lax.dot_general(
        pick, stack, (((1,), (1,)), ((), ())), precision=HIGHEST, preferred_element_type=jnp.float32
    )


def gram_kernel(z0, z1, second, to_modes, own, out, modal, image, partial, s):
    for r in range(PARTS):
        rows = slice(r * SLAB, (r + 1) * SLAB)
        s[rows, 0:PART] = z0[r]
        s[rows, PART : 2 * PART] = z1[r]
    m = mm(to_modes[...], s[...])
    row = lax.broadcasted_iota(jnp.int32, (MODES, MODES), 0)
    col = lax.broadcasted_iota(jnp.int32, (MODES, MODES), 1)
    e = jnp.sum(jnp.where(row == col, own[0:1, :], 0.0), axis=1, keepdims=True)
    m0, m1 = m[:, 0:PART], m[:, PART : 2 * PART]
    i0 = m1 + e * m0
    modal[...] = m0
    image[...] = i0
    partial[...] = e * (m1 + i0)
    g = sums(((m0, m0), (m0, i0), (i0, i0)), 0)
    for r in range(PARTS):
        out[r, 0:FLAT, :] = second[r]
        out[r, FLAT:, :] = g


def again_kernel(z2, modal, image, partial, to_modes, out, s):
    for r in range(PARTS):
        for j in range(PART // LANES):
            cols = slice(j * LANES, (j + 1) * LANES)
            s[r * SLAB : (r + 1) * SLAB, cols] = z2[r, j * SLAB : (j + 1) * SLAB, :]
    again = mm(to_modes[...], s[...]) + partial[...]
    m0, i0 = modal[...], image[...]
    g = jnp.sum(z2[:, FLAT:, :], axis=0) + sums(((m0, again), (i0, again), (again, again)), 3)
    out[...] = jnp.broadcast_to(g[None], out.shape)


def finish_kernel(got, z0, z1, to_modes, from_modes, own, out, side, s):
    g = jnp.sum(got[...], axis=0)
    mm_, mi, ii, mj, ij, jj = (g[k : k + 1, :] for k in range(6))
    e = own[0:1, :]
    scale = mm_ + 1e-06
    upper = 1.5 * jnp.sqrt(ii / scale)
    lower = upper * 0.125
    center = (upper + lower) * 0.5
    half_width = (upper - lower) * 0.5
    sigma = center / half_width
    rho_zero = 1.0 / sigma
    rho_one = 1.0 / (2.0 * sigma - rho_zero)
    over = 1.0 / center
    c2 = 2.0 * rho_one / half_width
    u0 = rho_one * rho_zero * over + c2
    u1 = -c2 * over
    a = -over - u0
    b = -u1
    side[0:1, :] = mm_ + a * (2.0 * mi + a * ii)
    side[1:2, :] = scale
    ours = jnp.broadcast_to(b * (2.0 * (mj + a * ij) + b * jj), (8, LANES))
    for r in range(PARTS):
        s[r * SLAB : (r + 1) * SLAB, :] = z0[r]
        s[MODES + r * SLAB : MODES + (r + 1) * SLAB, :] = z1[r]
    from_m = from_modes[...]
    to_m = to_modes[...]
    mix = jnp.concatenate([mm(from_m * (over + u0 + u1 * e), to_m), mm(from_m * u1, to_m)], axis=1)
    value = mm(mix, s[...])
    for r in range(PARTS):
        for j in range(PART // LANES):
            cols = slice(j * LANES, (j + 1) * LANES)
            out[r, j * SLAB : (j + 1) * SLAB, :] = value[r * SLAB : (r + 1) * SLAB, cols]
        out[r, FLAT:, :] = ours


def unpack_kernel(got, side, place, out, mine):
    for r in range(PARTS):
        for j in range(PART // LANES):
            start = r * PART + j * LANES
            out[:, start : start + LANES] = got[r, j * SLAB : (j + 1) * SLAB, :]
    squares = side[0:1, :] + sum(got[r, FLAT : FLAT + 1, :] for r in range(PARTS))
    norm = jnp.sqrt(jnp.maximum(squares, 0.0) / side[1:2, :])
    here = place[0:1, 0:SLAB]
    picked = norm[:, 0:SLAB]
    for r in range(1, PARTS):
        picked = jnp.where(here == r, norm[:, r * SLAB : (r + 1) * SLAB], picked)
    mine[...] = picked


def call(kernel, out_shape, in_specs, scratch=(), out_specs=None):
    if out_specs is None:
        out_specs = (VMEM,) * len(out_shape) if isinstance(out_shape, tuple) else VMEM
    return pl.pallas_call(
        kernel,
        out_shape=out_shape,
        in_specs=in_specs,
        out_specs=out_specs,
        scratch_shapes=scratch,
        compiler_params=pltpu.CompilerParams(vmem_limit_bytes=32 * 1024 * 1024),
    )


def pinned(value):
    return pltpu.with_memory_space_constraint(value, pltpu.HBM)


def on_device(sizes, source, to_modes, from_modes, eigenvalue, shifts, weights, neighbors):
    lat = sizes["y"] * sizes["z"]
    place = jnp.full((8, LANES), lax.axis_index(RAD).astype(jnp.float32))
    shift_row = shifts.reshape(1, -1)
    eig = eigenvalue.reshape(1, -1)
    up, down, own, nb, shift_row = call(
        pack_kernel,
        (f32(ROWS, WIDE + LANES), f32(ROWS, WIDE + LANES), f32(8, LANES),
         jax.ShapeDtypeStruct(neighbors.shape, neighbors.dtype), f32(1, BLOCKS * LANES)),
        [HBM] * 5,
        [
            pltpu.VMEM((2, STENCIL, NEAR), jnp.float32),
            pltpu.VMEM((1, LANES), jnp.float32),
            pltpu.SemaphoreType.DMA((9,)),
        ],
    )(*(pinned(v) for v in (source, weights, shift_row, neighbors, eig)))
    left = lax.ppermute(up, LAT, [(i, (i + 1) % lat) for i in range(lat)])
    right = lax.ppermute(down, LAT, [((i + 1) % lat, i) for i in range(lat)])
    inner, diag, place, dealt = call(
        inner_kernel,
        (
            f32(BLOCKS - 2 * HALO, SLAB, LANES),
            f32(BLOCKS, 1, LANES),
            f32(8, LANES),
            f32(PARTS, SLAB, PART),
        ),
        [VMEM] * 5,
        [pltpu.SMEM((STENCIL, BLOCKS), jnp.int32), pltpu.SemaphoreType.DMA((1,))],
    )(source, weights, shift_row, nb, place)
    z0 = lax.all_to_all(dealt, RAD, 0, 0, tiled=True)
    first, x0, x1 = call(
        edge_kernel,
        (f32(PARTS, SLAB, PART), f32(EXT2, SLAB, LANES), f32(BLOCKS, SLAB, LANES)),
        [VMEM] * 7,
        [pltpu.SMEM((STENCIL, BLOCKS), jnp.int32), pltpu.SemaphoreType.DMA((1,))],
    )(source, left, right, weights, diag, inner, nb)
    z1 = lax.all_to_all(first, RAD, 0, 0, tiled=True)
    second = call(
        outer_kernel,
        f32(PARTS, FLAT, LANES),
        [VMEM] * 7,
        [
            pltpu.VMEM((EXT1, SLAB, LANES), jnp.float32),
            pltpu.VMEM((2, ROWS, LANES), jnp.int32),
            pltpu.SMEM((2, ROWS, LANES), jnp.int32),
            pltpu.SMEM((STENCIL, BLOCKS), jnp.int32),
            pltpu.SemaphoreType.DMA((3,)),
        ],
    )(x0, x1, left, right, weights, diag, nb)
    sent, modal, image, partial = call(
        gram_kernel,
        (f32(PARTS, FLAT + 8, LANES),) + (f32(MODES, PART),) * 3,
        [VMEM] * 5,
        [pltpu.VMEM((MODES, 2 * PART), jnp.float32)],
    )(z0, z1, second, to_modes, own)
    z2 = lax.all_to_all(sent, RAD, 0, 0, tiled=True)
    g = call(
        again_kernel,
        f32(lat, 8, LANES),
        [VMEM] * 5,
        [pltpu.VMEM((MODES, PART), jnp.float32)],
    )(z2, modal, image, partial, to_modes)
    g = lax.all_to_all(g, LAT, 0, 0, tiled=True)
    mixed, side = call(
        finish_kernel,
        (f32(PARTS, FLAT + 8, LANES), f32(8, LANES)),
        [VMEM] * 6,
        [pltpu.VMEM((2 * MODES, PART), jnp.float32)],
    )(g, z0, z1, to_modes, from_modes, own)
    got = lax.all_to_all(mixed, RAD, 0, 0, tiled=True)
    smoothed, residual_norm = call(
        unpack_kernel, (f32(SLAB, BLOCKS * LANES), f32(1, SLAB)), [VMEM] * 3
    )(got, side, place)
    return smoothed, residual_norm.reshape(SLAB)


def solution(mesh):
    names = ("y", "z", "x", "core")
    fine = Mesh(np.asarray(mesh.devices).reshape(4, 8, 4, 2), names)
    return jax.shard_map(
        functools.partial(on_device, dict(fine.shape)),
        mesh=fine,
        in_specs=(P(RAD, LAT), P(), P(), P(), P(LAT), P(None, LAT), P(None, LAT)),
        out_specs=(P(RAD, LAT), P(RAD)),
        check_vma=False,
    )
```

```python
import functools

import jax
import jax.numpy as jnp
import numpy as np
from jax import lax
from jax.experimental import pallas as pl
from jax.experimental.pallas import tpu as pltpu
from jax.sharding import Mesh, PartitionSpec as P

LANES = 128
HALO = 8
UNROLL = 8
STENCIL = 31
ROWS = STENCIL + 1
BLOCKS = 32
EXT1 = BLOCKS + 2 * HALO
EXT2 = BLOCKS + 4 * HALO
SLAB = 16
PARTS = 8
PART = BLOCKS * LANES // PARTS
MODES = 128
FLAT = SLAB * PART // LANES
WIDE = 2 * HALO * LANES
NEAR = HALO * LANES
HALF = NEAR // 2
TAIL = HALF + NEAR
LAT = ("y", "z")
RAD = ("x", "core")


def work(microseconds):
    return pl.CostEstimate(
        flops=int(microseconds * 1e9), transcendentals=0, bytes_accessed=0
    )


VMEM = pl.BlockSpec(memory_space=pltpu.VMEM)
SMEM = pl.BlockSpec(memory_space=pltpu.SMEM)
HBM = pl.BlockSpec(memory_space=pltpu.HBM)
COST_0 = work(3)
COST_1 = work(3)
COST_2 = work(10)
HIGHEST = lax.Precision.HIGHEST


def f32(*shape):
    return jax.ShapeDtypeStruct(shape, jnp.float32)


def split(a):
    high = a.astype(jnp.bfloat16)
    return high, (a - high.astype(jnp.float32)).astype(jnp.bfloat16)


def mm(a, b):
    (ah, al), (bh, bl) = split(a), split(b)
    dot = functools.partial(jnp.dot, preferred_element_type=jnp.float32)
    return dot(ah, bh) + (dot(ah, bl) + dot(al, bh))


def start_all(sems, pairs):
    copies = [pltpu.make_async_copy(src, dst, sems.at[k]) for k, (src, dst) in enumerate(pairs)]
    for copy in copies:
        copy.start()
    return copies


def wait_all(copies):
    for copy in copies:
        copy.wait()


def pack_kernel(src, weights, shifts, neighbors, eig, up, down, up_far, down_far, own, nb_in, sh_in, w_in, eig_in, sems):
    last = BLOCKS * LANES
    ends = ((up, up_far, last - NEAR, last - WIDE), (down, down_far, 0, NEAR))
    pairs = [(neighbors, nb_in), (eig, eig_in), (shifts, sh_in)]
    for k, (near_out, far_out, near, far) in enumerate(ends):
        pairs += [
            (src.at[:, pl.ds(near, NEAR)], near_out),
            (weights.at[:, pl.ds(near, NEAR)], w_in.at[k]),
            (src.at[:, pl.ds(far, HALF)], far_out.at[0:SLAB, 0:HALF]),
            (src.at[:, pl.ds(far + HALF, HALF)], far_out.at[SLAB : 2 * SLAB, 0:HALF]),
        ]
    wait_all(start_all(sems, pairs))
    nb = nb_in[...].astype(jnp.float32)
    for k, (_, out, near, _) in enumerate(ends):
        block = near // LANES
        out[0:STENCIL, HALF:TAIL] = w_in[k]
        out[STENCIL:ROWS, HALF:TAIL] = sh_in[:, near : near + NEAR]
        out[:, TAIL:] = jnp.zeros((ROWS, LANES), jnp.float32)
        out[0:STENCIL, TAIL : TAIL + HALO] = nb[:, block : block + HALO]
    own[...] = jnp.broadcast_to(eig_in[...], own.shape)


def column(start, block):
    return pl.ds(pl.multiple_of(start + block * LANES, LANES), LANES)


def apply(read, centre, d, weight, offset):
    acc = d * read(centre)
    for s in range(STENCIL):
        moved = read(offset(s) + centre)
        if s:
            moved = pltpu.roll(moved, LANES - s, 1)
        acc = acc - weight(s) * moved
    return acc


def inner_kernel(src, weights, shifts, nb_in, place_in, x1, diag, place, nb, sems):
    copies = start_all(sems, [(nb_in, nb)])
    place[...] = place_in[...]
    for j in range(BLOCKS):
        cols = slice(j * LANES, (j + 1) * LANES)
        diag[j] = jnp.sum(weights[:, cols], axis=0, keepdims=True) + shifts[:, cols]
    wait_all(copies)

    def step(i, _):
        for u in range(UNROLL):
            b = HALO + i * UNROLL + u
            x1[b - HALO] = apply(
                lambda c: src[:, column(0, c)],
                b,
                diag[b],
                lambda s: weights[s : s + 1, column(0, b)],
                lambda s: nb[s, b],
            )
        return 0

    lax.fori_loop(0, (BLOCKS - 2 * HALO) // UNROLL, step, 0)


def edge_kernel(src, left, right, weights, diag, inner, nb_in, out, x0, x1, nb, sems):
    copies = start_all(sems, [(nb_in, nb)])
    for j in range(HALO):
        cols = slice(j * LANES, (j + 1) * LANES)
        x0[j] = left[:, cols]
        x0[HALO + BLOCKS + j] = right[:, cols]
    for j in range(BLOCKS):
        x0[HALO + j] = src[:, j * LANES : (j + 1) * LANES]
    for r in range(PARTS):
        out[r, 0:SLAB, :] = src[:, r * PART : (r + 1) * PART]
    for j in range(HALO, BLOCKS - HALO):
        x1[j] = inner[j - HALO]
        part, place = divmod(j, PART // LANES)
        out[part, SLAB:, place * LANES : (place + 1) * LANES] = inner[j - HALO]
    wait_all(copies)

    def step(i, _):
        for u in range(UNROLL):
            b = i * (BLOCKS - HALO) + u
            value = apply(
                lambda c: x0[c],
                b + HALO,
                diag[b],
                lambda s: weights[s : s + 1, column(0, b)],
                lambda s: nb[s, b],
            )
            x1[b] = value
            out[lax.div(b, PART // LANES), SLAB:, column(0, lax.rem(b, PART // LANES))] = value
        return 0

    lax.fori_loop(0, 2, step, 0)


def outer_kernel(x0_near, x1_own, left, right, weights, diag, nb_in, out, x0, x1, nbv, nbs, nb, sems):
    nbv[0] = left[:, TAIL:].astype(jnp.int32)
    nbv[1] = right[:, TAIL:].astype(jnp.int32)
    copies = start_all(sems, [(nbv.at[k], nbs.at[k]) for k in range(2)] + [(nb_in, nb)])
    for half in range(2):
        rows = slice(half * SLAB, half * SLAB + SLAB)
        for j in range(HALO // 2):
            cols = slice(j * LANES, (j + 1) * LANES)
            x0[half * HALO // 2 + j] = left[rows, cols]
            x0[3 * HALO + BLOCKS + half * HALO // 2 + j] = right[rows, cols]
    for j in range(EXT1):
        x0[HALO + j] = x0_near[j]
    for j in range(BLOCKS):
        x1[HALO + j] = x1_own[j]
    wait_all(copies)
    for side, ref in ((0, left), (1, right)):
        for j in range(HALO):
            e = j + side * (HALO + BLOCKS)
            cols = slice(HALF + j * LANES, HALF + (j + 1) * LANES)
            x1[e] = apply(
                lambda c: x0[c],
                e + HALO,
                jnp.sum(ref[:, cols], axis=0, keepdims=True),
                lambda s: ref[s : s + 1, cols],
                lambda s: nbs[side, s, j],
            )

    def step(i, _):
        for u in range(UNROLL):
            b = i * UNROLL + u
            rows = pl.ds(pl.multiple_of(lax.rem(b, PART // LANES) * SLAB, SLAB), SLAB)
            out[lax.div(b, PART // LANES), rows, :] = apply(
                lambda c: x1[c],
                b + HALO,
                diag[b],
                lambda s: weights[s : s + 1, column(0, b)],
                lambda s: nb[s, b],
            )
        return 0

    lax.fori_loop(0, BLOCKS // UNROLL, step, 0)


def sums(pairs, first):
    folded = []
    for a, b in pairs:
        p = a * b
        folded.append(sum(p[:, k * LANES : (k + 1) * LANES] for k in range(PART // LANES)))
    stack = jnp.concatenate(folded, axis=1)
    shape = (8, stack.shape[1])
    which = lax.broadcasted_iota(jnp.int32, shape, 1) // LANES + first
    pick = (which == lax.broadcasted_iota(jnp.int32, shape, 0)).astype(jnp.float32)
    return lax.dot_general(
        pick, stack, (((1,), (1,)), ((), ())), precision=HIGHEST, preferred_element_type=jnp.float32
    )


def gram_kernel(z01, second, to_modes, own, out, modal, image, partial, s):
    for r in range(PARTS):
        rows = slice(r * SLAB, (r + 1) * SLAB)
        s[rows, 0:PART] = z01[r, 0:SLAB, :]
        s[rows, PART : 2 * PART] = z01[r, SLAB:, :]
    m = mm(to_modes[...], s[...])
    row = lax.broadcasted_iota(jnp.int32, (MODES, MODES), 0)
    col = lax.broadcasted_iota(jnp.int32, (MODES, MODES), 1)
    e = jnp.sum(jnp.where(row == col, own[0:1, :], 0.0), axis=1, keepdims=True)
    m0, m1 = m[:, 0:PART], m[:, PART : 2 * PART]
    i0 = m1 + e * m0
    modal[...] = m0
    image[...] = i0
    partial[...] = e * (m1 + i0)
    g = sums(((m0, m0), (m0, i0), (i0, i0)), 0)
    for r in range(PARTS):
        out[r, 0:FLAT, :] = second[r]
        out[r, FLAT:, :] = g


def again_kernel(z2, modal, image, partial, to_modes, out, s):
    for r in range(PARTS):
        for j in range(PART // LANES):
            cols = slice(j * LANES, (j + 1) * LANES)
            s[r * SLAB : (r + 1) * SLAB, cols] = z2[r, j * SLAB : (j + 1) * SLAB, :]
    again = mm(to_modes[...], s[...]) + partial[...]
    m0, i0 = modal[...], image[...]
    g = jnp.sum(z2[:, FLAT:, :], axis=0) + sums(((m0, again), (i0, again), (again, again)), 3)
    out[...] = jnp.broadcast_to(g[None], out.shape)


def finish_kernel(got, z01, to_modes, from_modes, own, out, side, s):
    g = jnp.sum(got[...], axis=0)
    mm_, mi, ii, mj, ij, jj = (g[k : k + 1, :] for k in range(6))
    e = own[0:1, :]
    scale = mm_ + 1e-06
    upper = 1.5 * jnp.sqrt(ii / scale)
    lower = upper * 0.125
    center = (upper + lower) * 0.5
    half_width = (upper - lower) * 0.5
    sigma = center / half_width
    rho_zero = 1.0 / sigma
    rho_one = 1.0 / (2.0 * sigma - rho_zero)
    over = 1.0 / center
    c2 = 2.0 * rho_one / half_width
    u0 = rho_one * rho_zero * over + c2
    u1 = -c2 * over
    a = -over - u0
    b = -u1
    side[0:1, :] = mm_ + a * (2.0 * mi + a * ii)
    side[1:2, :] = scale
    ours = jnp.broadcast_to(b * (2.0 * (mj + a * ij) + b * jj), (8, LANES))
    for r in range(PARTS):
        s[r * SLAB : (r + 1) * SLAB, :] = z01[r, 0:SLAB, :]
        s[MODES + r * SLAB : MODES + (r + 1) * SLAB, :] = z01[r, SLAB:, :]
    from_m = from_modes[...]
    to_m = to_modes[...]
    mix = jnp.concatenate([mm(from_m * (over + u0 + u1 * e), to_m), mm(from_m * u1, to_m)], axis=1)
    value = mm(mix, s[...])
    for r in range(PARTS):
        for j in range(PART // LANES):
            cols = slice(j * LANES, (j + 1) * LANES)
            out[r, j * SLAB : (j + 1) * SLAB, :] = value[r * SLAB : (r + 1) * SLAB, cols]
        out[r, FLAT:, :] = ours


def unpack_kernel(got, side, place, out, mine):
    for r in range(PARTS):
        for j in range(PART // LANES):
            start = r * PART + j * LANES
            out[:, start : start + LANES] = got[r, j * SLAB : (j + 1) * SLAB, :]
    squares = side[0:1, :] + sum(got[r, FLAT : FLAT + 1, :] for r in range(PARTS))
    norm = jnp.sqrt(jnp.maximum(squares, 0.0) / side[1:2, :])
    here = place[0:1, 0:SLAB]
    picked = norm[:, 0:SLAB]
    for r in range(1, PARTS):
        picked = jnp.where(here == r, norm[:, r * SLAB : (r + 1) * SLAB], picked)
    mine[...] = picked


def call(kernel, out_shape, in_specs, scratch=(), out_specs=None, cost=None):
    if out_specs is None:
        out_specs = (VMEM,) * len(out_shape) if isinstance(out_shape, tuple) else VMEM
    return pl.pallas_call(
        kernel,
        out_shape=out_shape,
        in_specs=in_specs,
        out_specs=out_specs,
        scratch_shapes=scratch,
        cost_estimate=cost,
        compiler_params=pltpu.CompilerParams(vmem_limit_bytes=32 * 1024 * 1024),
    )


def pinned(value):
    return pltpu.with_memory_space_constraint(value, pltpu.HBM)


def on_device(sizes, source, to_modes, from_modes, eigenvalue, shifts, weights, neighbors):
    lat = sizes["y"] * sizes["z"]
    place = jnp.full((8, LANES), lax.axis_index(RAD).astype(jnp.float32))
    shift_row = shifts.reshape(1, -1)
    eig = eigenvalue.reshape(1, -1)
    nears, fars = f32(SLAB, NEAR), f32(ROWS, TAIL + LANES)
    offsets = jax.ShapeDtypeStruct(neighbors.shape, neighbors.dtype)
    up, down, up_far, down_far, own, nb, shift_row = call(
        pack_kernel,
        (nears, nears, fars, fars, f32(8, LANES), offsets, f32(1, BLOCKS * LANES)),
        [HBM] * 5,
        [
            pltpu.VMEM((2, STENCIL, NEAR), jnp.float32),
            pltpu.VMEM((1, LANES), jnp.float32),
            pltpu.SemaphoreType.DMA((11,)),
        ],
    )(*(pinned(v) for v in (source, weights, shift_row, neighbors, eig)))
    onward = [(i, (i + 1) % lat) for i in range(lat)]
    back = [(j, i) for i, j in onward]
    left, right = lax.ppermute(up, LAT, onward), lax.ppermute(down, LAT, back)
    left_far, right_far = lax.ppermute(up_far, LAT, onward), lax.ppermute(down_far, LAT, back)
    smem_offsets = pltpu.SMEM((STENCIL, BLOCKS), jnp.int32)
    inner, diag, place = call(
        inner_kernel,
        (f32(BLOCKS - 2 * HALO, SLAB, LANES), f32(BLOCKS, 1, LANES), f32(8, LANES)),
        [VMEM] * 5,
        [smem_offsets, pltpu.SemaphoreType.DMA((1,))],
        cost=COST_0,
    )(source, weights, shift_row, nb, place)
    first, x0, x1 = call(
        edge_kernel,
        (f32(PARTS, 2 * SLAB, PART), f32(EXT1, SLAB, LANES), f32(BLOCKS, SLAB, LANES)),
        [VMEM] * 7,
        [smem_offsets, pltpu.SemaphoreType.DMA((1,))],
        cost=COST_1,
    )(source, left, right, weights, diag, inner, nb)
    z01 = lax.all_to_all(first, RAD, 0, 0, tiled=True)
    second = call(
        outer_kernel,
        f32(PARTS, FLAT, LANES),
        [VMEM] * 7,
        [
            pltpu.VMEM((EXT2, SLAB, LANES), jnp.float32),
            pltpu.VMEM((EXT1, SLAB, LANES), jnp.float32),
            pltpu.VMEM((2, ROWS, LANES), jnp.int32),
            pltpu.SMEM((2, ROWS, LANES), jnp.int32),
            smem_offsets,
            pltpu.SemaphoreType.DMA((3,)),
        ],
        cost=COST_2,
    )(x0, x1, left_far, right_far, weights, diag, nb)
    sent, modal, image, partial = call(
        gram_kernel,
        (f32(PARTS, FLAT + 8, LANES),) + (f32(MODES, PART),) * 3,
        [VMEM] * 4,
        [pltpu.VMEM((MODES, 2 * PART), jnp.float32)],
    )(z01, second, to_modes, own)
    z2 = lax.all_to_all(sent, RAD, 0, 0, tiled=True)
    g = call(
        again_kernel,
        f32(lat, 8, LANES),
        [VMEM] * 5,
        [pltpu.VMEM((MODES, PART), jnp.float32)],
    )(z2, modal, image, partial, to_modes)
    g = lax.all_to_all(g, LAT, 0, 0, tiled=True)
    mixed, side = call(
        finish_kernel,
        (f32(PARTS, FLAT + 8, LANES), f32(8, LANES)),
        [VMEM] * 5,
        [pltpu.VMEM((2 * MODES, PART), jnp.float32)],
    )(g, z01, to_modes, from_modes, own)
    got = lax.all_to_all(mixed, RAD, 0, 0, tiled=True)
    smoothed, residual_norm = call(
        unpack_kernel, (f32(SLAB, BLOCKS * LANES), f32(1, SLAB)), [VMEM] * 3
    )(got, side, place)
    return smoothed, residual_norm.reshape(SLAB)


def solution(mesh):
    names = ("y", "z", "x", "core")
    fine = Mesh(np.asarray(mesh.devices).reshape(4, 8, 4, 2), names)
    return jax.shard_map(
        functools.partial(on_device, dict(fine.shape)),
        mesh=fine,
        in_specs=(P(RAD, LAT), P(), P(), P(), P(LAT), P(None, LAT), P(None, LAT)),
        out_specs=(P(RAD, LAT), P(RAD)),
        check_vma=False,
    )
```

```python
import functools

import jax
import jax.numpy as jnp
import numpy as np
from jax import lax
from jax.experimental import pallas as pl
from jax.experimental.pallas import tpu as pltpu
from jax.sharding import Mesh, PartitionSpec as P

LANES = 128
HALO = 8
UNROLL = 8
STENCIL = 31
ROWS = STENCIL + 1
BLOCKS = 32
EXT1 = BLOCKS + 2 * HALO
EXT2 = BLOCKS + 4 * HALO
SLAB = 16
PARTS = 8
PART = BLOCKS * LANES // PARTS
MODES = 128
FLAT = SLAB * PART // 8
WIDE = 2 * HALO * LANES
NEAR = HALO * LANES
HALF = NEAR // 2
TAIL = HALF + NEAR
LAT = ("y", "z")
RAD = ("x", "core")


def work(microseconds):
    return pl.CostEstimate(
        flops=int(microseconds * 1e9), transcendentals=0, bytes_accessed=0
    )


VMEM = pl.BlockSpec(memory_space=pltpu.VMEM)
SMEM = pl.BlockSpec(memory_space=pltpu.SMEM)
HBM = pl.BlockSpec(memory_space=pltpu.HBM)
COST_0 = work(3)
COST_1 = work(3)
COST_2 = work(10)
HIGHEST = lax.Precision.HIGHEST


def f32(*shape):
    return jax.ShapeDtypeStruct(shape, jnp.float32)


def split(a):
    high = a.astype(jnp.bfloat16)
    return high, (a - high.astype(jnp.float32)).astype(jnp.bfloat16)


def mm(a, b):
    (ah, al), (bh, bl) = split(a), split(b)
    dot = functools.partial(jnp.dot, preferred_element_type=jnp.float32)
    return dot(ah, bh) + (dot(ah, bl) + dot(al, bh))


def start_all(sems, pairs):
    copies = [pltpu.make_async_copy(src, dst, sems.at[k]) for k, (src, dst) in enumerate(pairs)]
    for copy in copies:
        copy.start()
    return copies


def wait_all(copies):
    for copy in copies:
        copy.wait()


def odd():
    return lax.rem(lax.axis_index("z"), 2)


def aligned(start):
    return pl.multiple_of(start, LANES)


def pack_kernel(src, weights, shifts, neighbors, eig, *refs):
    nears, fars, (own, nb_in, sh_in, w_in, eig_in, sems) = refs[0:2], refs[2:4], refs[4:]
    last = BLOCKS * LANES
    pairs = [(neighbors, nb_in), (eig, eig_in), (shifts, sh_in)]
    rightward = [odd() == k for k in range(2)]
    starts = [aligned(jnp.where(up, last - NEAR, 0)) for up in rightward]
    for k in range(2):
        far = aligned(jnp.where(rightward[k], last - WIDE, NEAR))
        pairs += [
            (src.at[:, pl.ds(starts[k], NEAR)], nears[k]),
            (weights.at[:, pl.ds(starts[k], NEAR)], w_in.at[k]),
            (src.at[:, pl.ds(far, HALF)], fars[k].at[0:SLAB, 0:HALF]),
            (src.at[:, pl.ds(aligned(far + HALF), HALF)], fars[k].at[SLAB : 2 * SLAB, 0:HALF]),
        ]
    wait_all(start_all(sems, pairs))
    nb = nb_in[...].astype(jnp.float32)
    for k in range(2):
        fars[k][0:STENCIL, HALF:TAIL] = w_in[k]
        fars[k][STENCIL:ROWS, HALF:TAIL] = sh_in[:, pl.ds(starts[k], NEAR)]
        fars[k][:, TAIL:] = jnp.zeros((ROWS, LANES), jnp.float32)
        fars[k][0:STENCIL, TAIL : TAIL + HALO] = jnp.where(
            rightward[k], nb[:, BLOCKS - HALO :], nb[:, :HALO]
        )
    own[...] = jnp.broadcast_to(eig_in[...], own.shape)


def column(start, block):
    return pl.ds(pl.multiple_of(start + block * LANES, LANES), LANES)


def apply(read, centre, d, weight, offset):
    acc = d * read(centre)
    for s in range(STENCIL):
        moved = read(offset(s) + centre)
        if s:
            moved = pltpu.roll(moved, LANES - s, 1)
        acc = acc - weight(s) * moved
    return acc


def inner_kernel(src, weights, shifts, nb_in, place_in, x1, diag, place, nb, sems):
    copies = start_all(sems, [(nb_in, nb)])
    place[...] = place_in[...]
    for j in range(BLOCKS):
        cols = slice(j * LANES, (j + 1) * LANES)
        diag[j] = jnp.sum(weights[:, cols], axis=0, keepdims=True) + shifts[:, cols]
    wait_all(copies)

    def step(i, _):
        for u in range(UNROLL):
            b = HALO + i * UNROLL + u
            x1[b - HALO] = apply(
                lambda c: src[:, column(0, c)],
                b,
                diag[b],
                lambda s: weights[s : s + 1, column(0, b)],
                lambda s: nb[s, b],
            )
        return 0

    lax.fori_loop(0, (BLOCKS - 2 * HALO) // UNROLL, step, 0)


def edge_kernel(src, near_0, near_1, weights, diag, inner, nb_in, out, x0, x1, nb, sems):
    copies = start_all(sems, [(nb_in, nb)])
    for k, near in enumerate((near_0, near_1)):
        base = jnp.where(odd() == k, HALO + BLOCKS, 0)
        for j in range(HALO):
            x0[base + j] = near[:, j * LANES : (j + 1) * LANES]
    for j in range(BLOCKS):
        x0[HALO + j] = src[:, j * LANES : (j + 1) * LANES]
    for r in range(PARTS):
        out[r, 0:SLAB, :] = src[:, r * PART : (r + 1) * PART]
    for j in range(HALO, BLOCKS - HALO):
        x1[j] = inner[j - HALO]
        part, place = divmod(j, PART // LANES)
        out[part, SLAB:, place * LANES : (place + 1) * LANES] = inner[j - HALO]
    wait_all(copies)

    def step(i, _):
        for u in range(UNROLL):
            b = i * (BLOCKS - HALO) + u
            value = apply(
                lambda c: x0[c],
                b + HALO,
                diag[b],
                lambda s: weights[s : s + 1, column(0, b)],
                lambda s: nb[s, b],
            )
            x1[b] = value
            out[lax.div(b, PART // LANES), SLAB:, column(0, lax.rem(b, PART // LANES))] = value
        return 0

    lax.fori_loop(0, 2, step, 0)


def outer_kernel(x0_near, x1_own, far_0, far_1, weights, diag, nb_in, out, x0, x1, nbv, nbs, nb, sems):
    nbv[0] = far_0[:, TAIL:].astype(jnp.int32)
    nbv[1] = far_1[:, TAIL:].astype(jnp.int32)
    copies = start_all(sems, [(nbv.at[k], nbs.at[k]) for k in range(2)] + [(nb_in, nb)])
    for k, far in enumerate((far_0, far_1)):
        base = jnp.where(odd() == k, 3 * HALO + BLOCKS, 0)
        for j in range(HALO):
            half, place = divmod(j, HALO // 2)
            x0[base + j] = far[half * SLAB : (half + 1) * SLAB, place * LANES : (place + 1) * LANES]
    for j in range(EXT1):
        x0[HALO + j] = x0_near[j]
    for j in range(BLOCKS):
        x1[HALO + j] = x1_own[j]
    wait_all(copies)
    for side, ref in ((0, far_0), (1, far_1)):
        base = jnp.where(odd() == side, HALO + BLOCKS, 0)
        for j in range(HALO):
            e = base + j
            cols = slice(HALF + j * LANES, HALF + (j + 1) * LANES)
            x1[e] = apply(
                lambda c: x0[c],
                e + HALO,
                jnp.sum(ref[:, cols], axis=0, keepdims=True),
                lambda s: ref[s : s + 1, cols],
                lambda s: nbs[side, s, j],
            )

    def step(i, _):
        for u in range(UNROLL):
            b = i * UNROLL + u
            value = apply(
                lambda c: x1[c],
                b + HALO,
                diag[b],
                lambda s: weights[s : s + 1, column(0, b)],
                lambda s: nb[s, b],
            )
            place = lax.rem(b, PART // LANES)
            for half in range(SLAB // 8):
                out[lax.div(b, PART // LANES), :, column(half * PART, place)] = value[half * 8 : half * 8 + 8]
        return 0

    lax.fori_loop(0, BLOCKS // UNROLL, step, 0)


def sums(pairs, first):
    folded = []
    for a, b in pairs:
        p = a * b
        folded.append(sum(p[:, k * LANES : (k + 1) * LANES] for k in range(PART // LANES)))
    stack = jnp.concatenate(folded, axis=1)
    shape = (8, stack.shape[1])
    which = lax.broadcasted_iota(jnp.int32, shape, 1) // LANES + first
    pick = (which == lax.broadcasted_iota(jnp.int32, shape, 0)).astype(jnp.float32)
    return lax.dot_general(
        pick, stack, (((1,), (1,)), ((), ())), precision=HIGHEST, preferred_element_type=jnp.float32
    )


def gram_kernel(z01, second, to_modes, own, out, modal, image, partial, s):
    for r in range(PARTS):
        rows = slice(r * SLAB, (r + 1) * SLAB)
        s[rows, 0:PART] = z01[r, 0:SLAB, :]
        s[rows, PART : 2 * PART] = z01[r, SLAB:, :]
    m = mm(to_modes[...], s[...])
    row = lax.broadcasted_iota(jnp.int32, (MODES, MODES), 0)
    col = lax.broadcasted_iota(jnp.int32, (MODES, MODES), 1)
    e = jnp.sum(jnp.where(row == col, own[0:1, :], 0.0), axis=1, keepdims=True)
    m0, m1 = m[:, 0:PART], m[:, PART : 2 * PART]
    i0 = m1 + e * m0
    modal[...] = m0
    image[...] = i0
    partial[...] = e * (m1 + i0)
    g = sums(((m0, m0), (m0, i0), (i0, i0)), 0)
    for r in range(PARTS):
        out[r, :, 0:FLAT] = second[r]
        out[r, :, FLAT:] = g


def again_kernel(z2, modal, image, partial, to_modes, out, s):
    for r in range(PARTS):
        for half in range(SLAB // 8):
            row = r * SLAB + half * 8
            s[row : row + 8, :] = z2[r, :, half * PART : (half + 1) * PART]
    again = mm(to_modes[...], s[...]) + partial[...]
    m0, i0 = modal[...], image[...]
    g = jnp.sum(z2[:, :, FLAT:], axis=0) + sums(((m0, again), (i0, again), (again, again)), 3)
    out[...] = jnp.broadcast_to(g[None], out.shape)


def finish_kernel(got, z01, to_modes, from_modes, own, out, side, s):
    g = jnp.sum(got[...], axis=0)
    mm_, mi, ii, mj, ij, jj = (g[k : k + 1, :] for k in range(6))
    e = own[0:1, :]
    scale = mm_ + 1e-06
    upper = 1.5 * jnp.sqrt(ii / scale)
    lower = upper * 0.125
    center = (upper + lower) * 0.5
    half_width = (upper - lower) * 0.5
    sigma = center / half_width
    rho_zero = 1.0 / sigma
    rho_one = 1.0 / (2.0 * sigma - rho_zero)
    over = 1.0 / center
    c2 = 2.0 * rho_one / half_width
    u0 = rho_one * rho_zero * over + c2
    u1 = -c2 * over
    a = -over - u0
    b = -u1
    side[0:1, :] = mm_ + a * (2.0 * mi + a * ii)
    side[1:2, :] = scale
    ours = jnp.broadcast_to(b * (2.0 * (mj + a * ij) + b * jj), (8, LANES))
    for r in range(PARTS):
        s[r * SLAB : (r + 1) * SLAB, :] = z01[r, 0:SLAB, :]
        s[MODES + r * SLAB : MODES + (r + 1) * SLAB, :] = z01[r, SLAB:, :]
    from_m = from_modes[...]
    to_m = to_modes[...]
    mix = jnp.concatenate([mm(from_m * (over + u0 + u1 * e), to_m), mm(from_m * u1, to_m)], axis=1)
    value = mm(mix, s[...])
    for r in range(PARTS):
        for half in range(SLAB // 8):
            row = r * SLAB + half * 8
            out[r, :, half * PART : (half + 1) * PART] = value[row : row + 8, :]
        out[r, :, FLAT:] = ours


def unpack_kernel(got, side, place, out, mine):
    for r in range(PARTS):
        for half in range(SLAB // 8):
            rows = slice(half * 8, half * 8 + 8)
            out[rows, r * PART : (r + 1) * PART] = got[r, :, half * PART : (half + 1) * PART]
    squares = side[0:1, :] + sum(got[r, 0:1, FLAT:] for r in range(PARTS))
    norm = jnp.sqrt(jnp.maximum(squares, 0.0) / side[1:2, :])
    here = place[0:1, 0:SLAB]
    picked = norm[:, 0:SLAB]
    for r in range(1, PARTS):
        picked = jnp.where(here == r, norm[:, r * SLAB : (r + 1) * SLAB], picked)
    mine[...] = picked


def call(kernel, out_shape, in_specs, scratch=(), out_specs=None, cost=None):
    if out_specs is None:
        out_specs = (VMEM,) * len(out_shape) if isinstance(out_shape, tuple) else VMEM
    return pl.pallas_call(
        kernel,
        out_shape=out_shape,
        in_specs=in_specs,
        out_specs=out_specs,
        scratch_shapes=scratch,
        cost_estimate=cost,
        compiler_params=pltpu.CompilerParams(vmem_limit_bytes=32 * 1024 * 1024),
    )


def pinned(value):
    return pltpu.with_memory_space_constraint(value, pltpu.HBM)


def on_device(sizes, source, to_modes, from_modes, eigenvalue, shifts, weights, neighbors):
    lat = sizes["y"] * sizes["z"]
    place = jnp.full((8, LANES), lax.axis_index(RAD).astype(jnp.float32))
    shift_row = shifts.reshape(1, -1)
    eig = eigenvalue.reshape(1, -1)
    nears, fars = f32(SLAB, NEAR), f32(ROWS, TAIL + LANES)
    offsets = jax.ShapeDtypeStruct(neighbors.shape, neighbors.dtype)
    near_0, near_1, far_0, far_1, own, nb, shift_row = call(
        pack_kernel,
        (nears, nears, fars, fars, f32(8, LANES), offsets, f32(1, BLOCKS * LANES)),
        [HBM] * 5,
        [
            pltpu.VMEM((2, STENCIL, NEAR), jnp.float32),
            pltpu.VMEM((1, LANES), jnp.float32),
            pltpu.SemaphoreType.DMA((11,)),
        ],
    )(*(pinned(v) for v in (source, weights, shift_row, neighbors, eig)))
    swaps = [
        [(i, (i + turn) % lat) for i, turn in ((i, 1 if i % 2 == k else -1) for i in range(lat))]
        for k in range(2)
    ]
    near_0, near_1 = lax.ppermute(near_0, LAT, swaps[0]), lax.ppermute(near_1, LAT, swaps[1])
    far_0, far_1 = lax.ppermute(far_0, LAT, swaps[0]), lax.ppermute(far_1, LAT, swaps[1])
    smem_offsets = pltpu.SMEM((STENCIL, BLOCKS), jnp.int32)
    inner, diag, place = call(
        inner_kernel,
        (f32(BLOCKS - 2 * HALO, SLAB, LANES), f32(BLOCKS, 1, LANES), f32(8, LANES)),
        [VMEM] * 5,
        [smem_offsets, pltpu.SemaphoreType.DMA((1,))],
        cost=COST_0,
    )(source, weights, shift_row, nb, place)
    first, x0, x1 = call(
        edge_kernel,
        (f32(PARTS, 2 * SLAB, PART), f32(EXT1, SLAB, LANES), f32(BLOCKS, SLAB, LANES)),
        [VMEM] * 7,
        [smem_offsets, pltpu.SemaphoreType.DMA((1,))],
        cost=COST_1,
    )(source, near_0, near_1, weights, diag, inner, nb)
    z01 = lax.all_to_all(first, RAD, 0, 0, tiled=True)
    second = call(
        outer_kernel,
        f32(PARTS, 8, FLAT),
        [VMEM] * 7,
        [
            pltpu.VMEM((EXT2, SLAB, LANES), jnp.float32),
            pltpu.VMEM((EXT1, SLAB, LANES), jnp.float32),
            pltpu.VMEM((2, ROWS, LANES), jnp.int32),
            pltpu.SMEM((2, ROWS, LANES), jnp.int32),
            smem_offsets,
            pltpu.SemaphoreType.DMA((3,)),
        ],
        cost=COST_2,
    )(x0, x1, far_0, far_1, weights, diag, nb)
    sent, modal, image, partial = call(
        gram_kernel,
        (f32(PARTS, 8, FLAT + LANES),) + (f32(MODES, PART),) * 3,
        [VMEM] * 4,
        [pltpu.VMEM((MODES, 2 * PART), jnp.float32)],
    )(z01, second, to_modes, own)
    z2 = lax.all_to_all(sent, RAD, 0, 0, tiled=True)
    g = call(
        again_kernel,
        f32(lat, 8, LANES),
        [VMEM] * 5,
        [pltpu.VMEM((MODES, PART), jnp.float32)],
    )(z2, modal, image, partial, to_modes)
    g = lax.all_to_all(g, LAT, 0, 0, tiled=True)
    mixed, side = call(
        finish_kernel,
        (f32(PARTS, 8, FLAT + LANES), f32(8, LANES)),
        [VMEM] * 5,
        [pltpu.VMEM((2 * MODES, PART), jnp.float32)],
    )(g, z01, to_modes, from_modes, own)
    got = lax.all_to_all(mixed, RAD, 0, 0, tiled=True)
    smoothed, residual_norm = call(
        unpack_kernel, (f32(SLAB, BLOCKS * LANES), f32(1, SLAB)), [VMEM] * 3
    )(got, side, place)
    return smoothed, residual_norm.reshape(SLAB)


def solution(mesh):
    names = ("y", "z", "x", "core")
    fine = Mesh(np.asarray(mesh.devices).reshape(4, 8, 4, 2), names)
    return jax.shard_map(
        functools.partial(on_device, dict(fine.shape)),
        mesh=fine,
        in_specs=(P(RAD, LAT), P(), P(), P(), P(LAT), P(None, LAT), P(None, LAT)),
        out_specs=(P(RAD, LAT), P(RAD)),
        check_vma=False,
    )
```

```python
import functools

import jax
import jax.numpy as jnp
import numpy as np
from jax import lax
from jax.experimental import pallas as pl
from jax.experimental.pallas import tpu as pltpu
from jax.sharding import Mesh, PartitionSpec as P

LANES = 128
HALO = 8
UNROLL = 8
STENCIL = 31
ROWS = STENCIL + 1
BLOCKS = 32
EXT1 = BLOCKS + 2 * HALO
EXT2 = BLOCKS + 4 * HALO
SLAB = 16
PARTS = 8
PART = BLOCKS * LANES // PARTS
MODES = 128
FLAT = SLAB * PART // 8
WIDE = 2 * HALO * LANES
NEAR = HALO * LANES
HALF = NEAR // 2
TAIL = HALF + NEAR
LAT = ("y", "z")
RAD = ("x", "core")


def work(microseconds):
    return pl.CostEstimate(
        flops=int(microseconds * 1e9), transcendentals=0, bytes_accessed=0
    )


VMEM = pl.BlockSpec(memory_space=pltpu.VMEM)
SMEM = pl.BlockSpec(memory_space=pltpu.SMEM)
HBM = pl.BlockSpec(memory_space=pltpu.HBM)
COST_0 = work(3)
COST_1 = work(3)
COST_2 = work(10)
HIGHEST = lax.Precision.HIGHEST


def f32(*shape):
    return jax.ShapeDtypeStruct(shape, jnp.float32)


def split(a):
    high = a.astype(jnp.bfloat16)
    return high, (a - high.astype(jnp.float32)).astype(jnp.bfloat16)


def mm(a, b):
    (ah, al), (bh, bl) = split(a), split(b)
    dot = functools.partial(jnp.dot, preferred_element_type=jnp.float32)
    return dot(ah, bh) + (dot(ah, bl) + dot(al, bh))


def start_all(sems, pairs):
    copies = [pltpu.make_async_copy(src, dst, sems.at[k]) for k, (src, dst) in enumerate(pairs)]
    for copy in copies:
        copy.start()
    return copies


def wait_all(copies):
    for copy in copies:
        copy.wait()


def odd():
    return lax.rem(lax.axis_index("z"), 2)


def aligned(start):
    return pl.multiple_of(start, LANES)


def rightward(swap):
    return odd() == swap


def pack_kernel(src, weights, shifts, neighbors, eig, near_0, near_1, own, nb, shift_row, eig_in, sems):
    pairs = [(neighbors, nb), (eig, eig_in), (shifts, shift_row)]
    for k, near in enumerate((near_0, near_1)):
        start = aligned(jnp.where(rightward(k), BLOCKS * LANES - NEAR, 0))
        pairs.append((src.at[:, pl.ds(start, NEAR)], near))
    wait_all(start_all(sems, pairs))
    own[...] = jnp.broadcast_to(eig_in[...], own.shape)


def column(start, block):
    return pl.ds(pl.multiple_of(start + block * LANES, LANES), LANES)


def apply(read, centre, d, weight, offset):
    acc = d * read(centre)
    for s in range(STENCIL):
        moved = read(offset(s) + centre)
        if s:
            moved = pltpu.roll(moved, LANES - s, 1)
        acc = acc - weight(s) * moved
    return acc


def inner_kernel(src, weights, shifts, nb_in, place_in, x1, diag, place, far_0, far_1, nb, sems):
    copies = start_all(sems, [(nb_in, nb)])
    place[...] = place_in[...]
    offsets = nb_in[...].astype(jnp.float32)
    for k, out in enumerate((far_0, far_1)):
        up = rightward(k)
        near = aligned(jnp.where(up, BLOCKS * LANES - NEAR, 0))
        far = aligned(jnp.where(up, BLOCKS * LANES - WIDE, NEAR))
        out[0:SLAB, 0:HALF] = src[:, pl.ds(far, HALF)]
        out[SLAB : 2 * SLAB, 0:HALF] = src[:, pl.ds(aligned(far + HALF), HALF)]
        out[0:STENCIL, HALF:TAIL] = weights[:, pl.ds(near, NEAR)]
        out[STENCIL:ROWS, HALF:TAIL] = shifts[:, pl.ds(near, NEAR)]
        out[:, TAIL:] = jnp.zeros((ROWS, LANES), jnp.float32)
        out[0:STENCIL, TAIL : TAIL + HALO] = jnp.where(
            up, offsets[:, BLOCKS - HALO :], offsets[:, :HALO]
        )
    for j in range(BLOCKS):
        cols = slice(j * LANES, (j + 1) * LANES)
        diag[j] = jnp.sum(weights[:, cols], axis=0, keepdims=True) + shifts[:, cols]
    wait_all(copies)

    def step(i, _):
        for u in range(UNROLL):
            b = HALO + i * UNROLL + u
            x1[b - HALO] = apply(
                lambda c: src[:, column(0, c)],
                b,
                diag[b],
                lambda s: weights[s : s + 1, column(0, b)],
                lambda s: nb[s, b],
            )
        return 0

    lax.fori_loop(0, (BLOCKS - 2 * HALO) // UNROLL, step, 0)


def edge_kernel(src, near_0, near_1, weights, diag, inner, nb_in, out, x0, x1, nb, sems):
    copies = start_all(sems, [(nb_in, nb)])
    for k, near in enumerate((near_0, near_1)):
        base = jnp.where(odd() == k, HALO + BLOCKS, 0)
        for j in range(HALO):
            x0[base + j] = near[:, j * LANES : (j + 1) * LANES]
    for j in range(BLOCKS):
        x0[HALO + j] = src[:, j * LANES : (j + 1) * LANES]
    for r in range(PARTS):
        out[r, 0:SLAB, :] = src[:, r * PART : (r + 1) * PART]
    for j in range(HALO, BLOCKS - HALO):
        x1[j] = inner[j - HALO]
        part, place = divmod(j, PART // LANES)
        out[part, SLAB:, place * LANES : (place + 1) * LANES] = inner[j - HALO]
    wait_all(copies)

    def step(i, _):
        for u in range(UNROLL):
            b = i * (BLOCKS - HALO) + u
            value = apply(
                lambda c: x0[c],
                b + HALO,
                diag[b],
                lambda s: weights[s : s + 1, column(0, b)],
                lambda s: nb[s, b],
            )
            x1[b] = value
            out[lax.div(b, PART // LANES), SLAB:, column(0, lax.rem(b, PART // LANES))] = value
        return 0

    lax.fori_loop(0, 2, step, 0)


def outer_kernel(x0_near, x1_own, far_0, far_1, weights, diag, nb_in, out, x0, x1, nbv, nbs, nb, sems):
    nbv[0] = far_0[:, TAIL:].astype(jnp.int32)
    nbv[1] = far_1[:, TAIL:].astype(jnp.int32)
    copies = start_all(sems, [(nbv.at[k], nbs.at[k]) for k in range(2)] + [(nb_in, nb)])
    for k, far in enumerate((far_0, far_1)):
        base = jnp.where(odd() == k, 3 * HALO + BLOCKS, 0)
        for j in range(HALO):
            half, place = divmod(j, HALO // 2)
            x0[base + j] = far[half * SLAB : (half + 1) * SLAB, place * LANES : (place + 1) * LANES]
    for j in range(EXT1):
        x0[HALO + j] = x0_near[j]
    for j in range(BLOCKS):
        x1[HALO + j] = x1_own[j]
    wait_all(copies)
    for side, ref in ((0, far_0), (1, far_1)):
        base = jnp.where(odd() == side, HALO + BLOCKS, 0)
        for j in range(HALO):
            e = base + j
            cols = slice(HALF + j * LANES, HALF + (j + 1) * LANES)
            x1[e] = apply(
                lambda c: x0[c],
                e + HALO,
                jnp.sum(ref[:, cols], axis=0, keepdims=True),
                lambda s: ref[s : s + 1, cols],
                lambda s: nbs[side, s, j],
            )

    def step(i, _):
        for u in range(UNROLL):
            b = i * UNROLL + u
            value = apply(
                lambda c: x1[c],
                b + HALO,
                diag[b],
                lambda s: weights[s : s + 1, column(0, b)],
                lambda s: nb[s, b],
            )
            place = lax.rem(b, PART // LANES)
            for half in range(SLAB // 8):
                out[lax.div(b, PART // LANES), :, column(half * PART, place)] = value[half * 8 : half * 8 + 8]
        return 0

    lax.fori_loop(0, BLOCKS // UNROLL, step, 0)


def sums(pairs, first):
    folded = []
    for a, b in pairs:
        p = a * b
        folded.append(sum(p[:, k * LANES : (k + 1) * LANES] for k in range(PART // LANES)))
    stack = jnp.concatenate(folded, axis=1)
    shape = (8, stack.shape[1])
    which = lax.broadcasted_iota(jnp.int32, shape, 1) // LANES + first
    pick = (which == lax.broadcasted_iota(jnp.int32, shape, 0)).astype(jnp.float32)
    return lax.dot_general(
        pick, stack, (((1,), (1,)), ((), ())), precision=HIGHEST, preferred_element_type=jnp.float32
    )


def gram_kernel(z01, second, to_modes, own, out, modal, image, partial, s):
    for r in range(PARTS):
        rows = slice(r * SLAB, (r + 1) * SLAB)
        s[rows, 0:PART] = z01[r, 0:SLAB, :]
        s[rows, PART : 2 * PART] = z01[r, SLAB:, :]
    m = mm(to_modes[...], s[...])
    row = lax.broadcasted_iota(jnp.int32, (MODES, MODES), 0)
    col = lax.broadcasted_iota(jnp.int32, (MODES, MODES), 1)
    e = jnp.sum(jnp.where(row == col, own[0:1, :], 0.0), axis=1, keepdims=True)
    m0, m1 = m[:, 0:PART], m[:, PART : 2 * PART]
    i0 = m1 + e * m0
    modal[...] = m0
    image[...] = i0
    partial[...] = e * (m1 + i0)
    g = sums(((m0, m0), (m0, i0), (i0, i0)), 0)
    for r in range(PARTS):
        out[r, :, 0:FLAT] = second[r]
        out[r, :, FLAT:] = g


def again_kernel(z2, modal, image, partial, to_modes, out, s):
    for r in range(PARTS):
        for half in range(SLAB // 8):
            row = r * SLAB + half * 8
            s[row : row + 8, :] = z2[r, :, half * PART : (half + 1) * PART]
    again = mm(to_modes[...], s[...]) + partial[...]
    m0, i0 = modal[...], image[...]
    g = jnp.sum(z2[:, :, FLAT:], axis=0) + sums(((m0, again), (i0, again), (again, again)), 3)
    out[...] = jnp.broadcast_to(g[None], out.shape)


def finish_kernel(got, z01, to_modes, from_modes, own, out, side, s):
    g = jnp.sum(got[...], axis=0)
    mm_, mi, ii, mj, ij, jj = (g[k : k + 1, :] for k in range(6))
    e = own[0:1, :]
    scale = mm_ + 1e-06
    upper = 1.5 * jnp.sqrt(ii / scale)
    lower = upper * 0.125
    center = (upper + lower) * 0.5
    half_width = (upper - lower) * 0.5
    sigma = center / half_width
    rho_zero = 1.0 / sigma
    rho_one = 1.0 / (2.0 * sigma - rho_zero)
    over = 1.0 / center
    c2 = 2.0 * rho_one / half_width
    u0 = rho_one * rho_zero * over + c2
    u1 = -c2 * over
    a = -over - u0
    b = -u1
    side[0:1, :] = mm_ + a * (2.0 * mi + a * ii)
    side[1:2, :] = scale
    ours = jnp.broadcast_to(b * (2.0 * (mj + a * ij) + b * jj), (8, LANES))
    for r in range(PARTS):
        s[r * SLAB : (r + 1) * SLAB, :] = z01[r, 0:SLAB, :]
        s[MODES + r * SLAB : MODES + (r + 1) * SLAB, :] = z01[r, SLAB:, :]
    from_m = from_modes[...]
    to_m = to_modes[...]
    mix = jnp.concatenate([mm(from_m * (over + u0 + u1 * e), to_m), mm(from_m * u1, to_m)], axis=1)
    value = mm(mix, s[...])
    for r in range(PARTS):
        for half in range(SLAB // 8):
            row = r * SLAB + half * 8
            out[r, :, half * PART : (half + 1) * PART] = value[row : row + 8, :]
        out[r, :, FLAT:] = ours


def unpack_kernel(got, side, place, out, mine):
    for r in range(PARTS):
        for half in range(SLAB // 8):
            rows = slice(half * 8, half * 8 + 8)
            out[rows, r * PART : (r + 1) * PART] = got[r, :, half * PART : (half + 1) * PART]
    squares = side[0:1, :] + sum(got[r, 0:1, FLAT:] for r in range(PARTS))
    norm = jnp.sqrt(jnp.maximum(squares, 0.0) / side[1:2, :])
    here = place[0:1, 0:SLAB]
    picked = norm[:, 0:SLAB]
    for r in range(1, PARTS):
        picked = jnp.where(here == r, norm[:, r * SLAB : (r + 1) * SLAB], picked)
    mine[...] = picked


def call(kernel, out_shape, in_specs, scratch=(), out_specs=None, cost=None):
    if out_specs is None:
        out_specs = (VMEM,) * len(out_shape) if isinstance(out_shape, tuple) else VMEM
    return pl.pallas_call(
        kernel,
        out_shape=out_shape,
        in_specs=in_specs,
        out_specs=out_specs,
        scratch_shapes=scratch,
        cost_estimate=cost,
        compiler_params=pltpu.CompilerParams(vmem_limit_bytes=32 * 1024 * 1024),
    )


def pinned(value):
    return pltpu.with_memory_space_constraint(value, pltpu.HBM)


def on_device(sizes, source, to_modes, from_modes, eigenvalue, shifts, weights, neighbors):
    lat = sizes["y"] * sizes["z"]
    place = jnp.full((8, LANES), lax.axis_index(RAD).astype(jnp.float32))
    shift_row = shifts.reshape(1, -1)
    eig = eigenvalue.reshape(1, -1)
    nears, fars = f32(SLAB, NEAR), f32(ROWS, TAIL + LANES)
    offsets = jax.ShapeDtypeStruct(neighbors.shape, neighbors.dtype)
    near_0, near_1, own, nb, shift_row = call(
        pack_kernel,
        (nears, nears, f32(8, LANES), offsets, f32(1, BLOCKS * LANES)),
        [HBM] * 5,
        [pltpu.VMEM((1, LANES), jnp.float32), pltpu.SemaphoreType.DMA((5,))],
    )(*(pinned(v) for v in (source, weights, shift_row, neighbors, eig)))
    swaps = [
        [(i, (i + turn) % lat) for i, turn in ((i, 1 if i % 2 == k else -1) for i in range(lat))]
        for k in range(2)
    ]
    near_0, near_1 = lax.ppermute(near_0, LAT, swaps[0]), lax.ppermute(near_1, LAT, swaps[1])
    smem_offsets = pltpu.SMEM((STENCIL, BLOCKS), jnp.int32)
    inner, diag, place, far_0, far_1 = call(
        inner_kernel,
        (f32(BLOCKS - 2 * HALO, SLAB, LANES), f32(BLOCKS, 1, LANES), f32(8, LANES), fars, fars),
        [VMEM] * 5,
        [smem_offsets, pltpu.SemaphoreType.DMA((1,))],
        cost=COST_0,
    )(source, weights, shift_row, nb, place)
    far_0, far_1 = lax.ppermute(far_0, LAT, swaps[0]), lax.ppermute(far_1, LAT, swaps[1])
    first, x0, x1 = call(
        edge_kernel,
        (f32(PARTS, 2 * SLAB, PART), f32(EXT1, SLAB, LANES), f32(BLOCKS, SLAB, LANES)),
        [VMEM] * 7,
        [smem_offsets, pltpu.SemaphoreType.DMA((1,))],
        cost=COST_1,
    )(source, near_0, near_1, weights, diag, inner, nb)
    z01 = lax.all_to_all(first, RAD, 0, 0, tiled=True)
    second = call(
        outer_kernel,
        f32(PARTS, 8, FLAT),
        [VMEM] * 7,
        [
            pltpu.VMEM((EXT2, SLAB, LANES), jnp.float32),
            pltpu.VMEM((EXT1, SLAB, LANES), jnp.float32),
            pltpu.VMEM((2, ROWS, LANES), jnp.int32),
            pltpu.SMEM((2, ROWS, LANES), jnp.int32),
            smem_offsets,
            pltpu.SemaphoreType.DMA((3,)),
        ],
        cost=COST_2,
    )(x0, x1, far_0, far_1, weights, diag, nb)
    sent, modal, image, partial = call(
        gram_kernel,
        (f32(PARTS, 8, FLAT + LANES),) + (f32(MODES, PART),) * 3,
        [VMEM] * 4,
        [pltpu.VMEM((MODES, 2 * PART), jnp.float32)],
    )(z01, second, to_modes, own)
    z2 = lax.all_to_all(sent, RAD, 0, 0, tiled=True)
    g = call(
        again_kernel,
        f32(lat, 8, LANES),
        [VMEM] * 5,
        [pltpu.VMEM((MODES, PART), jnp.float32)],
    )(z2, modal, image, partial, to_modes)
    g = lax.all_to_all(g, LAT, 0, 0, tiled=True)
    mixed, side = call(
        finish_kernel,
        (f32(PARTS, 8, FLAT + LANES), f32(8, LANES)),
        [VMEM] * 5,
        [pltpu.VMEM((2 * MODES, PART), jnp.float32)],
    )(g, z01, to_modes, from_modes, own)
    got = lax.all_to_all(mixed, RAD, 0, 0, tiled=True)
    smoothed, residual_norm = call(
        unpack_kernel, (f32(SLAB, BLOCKS * LANES), f32(1, SLAB)), [VMEM] * 3
    )(got, side, place)
    return smoothed, residual_norm.reshape(SLAB)


def solution(mesh):
    names = ("y", "z", "x", "core")
    fine = Mesh(np.asarray(mesh.devices).reshape(4, 8, 4, 2), names)
    return jax.shard_map(
        functools.partial(on_device, dict(fine.shape)),
        mesh=fine,
        in_specs=(P(RAD, LAT), P(), P(), P(), P(LAT), P(None, LAT), P(None, LAT)),
        out_specs=(P(RAD, LAT), P(RAD)),
        check_vma=False,
    )
```

```python
import functools

import jax
import jax.numpy as jnp
import numpy as np
from jax import lax
from jax.experimental import pallas as pl
from jax.experimental.pallas import tpu as pltpu
from jax.sharding import Mesh, PartitionSpec as P

LANES = 128
HALO = 8
UNROLL = 8
STENCIL = 31
ROWS = STENCIL + 1
BLOCKS = 32
EXT1 = BLOCKS + 2 * HALO
EXT2 = BLOCKS + 4 * HALO
SLAB = 16
PARTS = 8
PART = BLOCKS * LANES // PARTS
MODES = 128
FLAT = SLAB * PART // 8
WIDE = 2 * HALO * LANES
NEAR = HALO * LANES
HALF = NEAR // 2
TAIL = HALF + NEAR
LAT = ("y", "z")
RAD = ("x", "core")


def work(microseconds):
    return pl.CostEstimate(
        flops=int(microseconds * 1e9), transcendentals=0, bytes_accessed=0
    )


VMEM = pl.BlockSpec(memory_space=pltpu.VMEM)
SMEM = pl.BlockSpec(memory_space=pltpu.SMEM)
HBM = pl.BlockSpec(memory_space=pltpu.HBM)
COST_0 = work(3)
COST_1 = work(3)
COST_2 = work(10)
HIGHEST = lax.Precision.HIGHEST


def f32(*shape):
    return jax.ShapeDtypeStruct(shape, jnp.float32)


def split(a):
    high = a.astype(jnp.bfloat16)
    return high, (a - high.astype(jnp.float32)).astype(jnp.bfloat16)


def mm(a, b):
    (ah, al), (bh, bl) = split(a), split(b)
    dot = functools.partial(jnp.dot, preferred_element_type=jnp.float32)
    return dot(ah, bh) + (dot(ah, bl) + dot(al, bh))


def start_all(sems, pairs):
    copies = [pltpu.make_async_copy(src, dst, sems.at[k]) for k, (src, dst) in enumerate(pairs)]
    for copy in copies:
        copy.start()
    return copies


def wait_all(copies):
    for copy in copies:
        copy.wait()


def odd():
    return lax.rem(lax.axis_index("z"), 2)


def aligned(start):
    return pl.multiple_of(start, LANES)


def rightward(swap):
    return odd() == swap


def pack_kernel(src, weights, shifts, neighbors, eig, near_0, near_1, own, nb, shift_row, eig_in, sems):
    pairs = [(neighbors, nb), (eig, eig_in), (shifts, shift_row)]
    for k, near in enumerate((near_0, near_1)):
        start = aligned(jnp.where(rightward(k), BLOCKS * LANES - NEAR, 0))
        pairs.append((src.at[:, pl.ds(start, NEAR)], near))
    wait_all(start_all(sems, pairs))
    own[...] = jnp.broadcast_to(eig_in[...], own.shape)


def column(start, block):
    return pl.ds(pl.multiple_of(start + block * LANES, LANES), LANES)


def apply(read, centre, d, weight, offset):
    acc = d * read(centre)
    for s in range(STENCIL):
        moved = read(offset(s) + centre)
        if s:
            moved = pltpu.roll(moved, LANES - s, 1)
        acc = acc - weight(s) * moved
    return acc


def inner_kernel(src, weights, shifts, nb_in, place_in, x1, diag, place, nb, sems):
    copies = start_all(sems, [(nb_in, nb)])
    place[...] = place_in[...]
    for j in range(BLOCKS):
        cols = slice(j * LANES, (j + 1) * LANES)
        diag[j] = jnp.sum(weights[:, cols], axis=0, keepdims=True) + shifts[:, cols]
    wait_all(copies)

    def step(i, _):
        for u in range(UNROLL):
            b = HALO + i * UNROLL + u
            x1[b - HALO] = apply(
                lambda c: src[:, column(0, c)],
                b,
                diag[b],
                lambda s: weights[s : s + 1, column(0, b)],
                lambda s: nb[s, b],
            )
        return 0

    lax.fori_loop(0, (BLOCKS - 2 * HALO) // UNROLL, step, 0)


def edge_kernel(src, near_0, near_1, weights, shifts, diag, inner, nb_in, out, x0, x1, far_0, far_1, nb, sems):
    copies = start_all(sems, [(nb_in, nb)])
    offsets = nb_in[...].astype(jnp.float32)
    for k, far_out in enumerate((far_0, far_1)):
        up = rightward(k)
        near = aligned(jnp.where(up, BLOCKS * LANES - NEAR, 0))
        far = aligned(jnp.where(up, BLOCKS * LANES - WIDE, NEAR))
        far_out[0:SLAB, 0:HALF] = src[:, pl.ds(far, HALF)]
        far_out[SLAB : 2 * SLAB, 0:HALF] = src[:, pl.ds(aligned(far + HALF), HALF)]
        far_out[0:STENCIL, HALF:TAIL] = weights[:, pl.ds(near, NEAR)]
        far_out[STENCIL:ROWS, HALF:TAIL] = shifts[:, pl.ds(near, NEAR)]
        far_out[:, TAIL:] = jnp.zeros((ROWS, LANES), jnp.float32)
        far_out[0:STENCIL, TAIL : TAIL + HALO] = jnp.where(
            up, offsets[:, BLOCKS - HALO :], offsets[:, :HALO]
        )
    for k, near in enumerate((near_0, near_1)):
        base = jnp.where(odd() == k, HALO + BLOCKS, 0)
        for j in range(HALO):
            x0[base + j] = near[:, j * LANES : (j + 1) * LANES]
    for j in range(BLOCKS):
        x0[HALO + j] = src[:, j * LANES : (j + 1) * LANES]
    for r in range(PARTS):
        out[r, 0:SLAB, :] = src[:, r * PART : (r + 1) * PART]
    for j in range(HALO, BLOCKS - HALO):
        x1[j] = inner[j - HALO]
        part, place = divmod(j, PART // LANES)
        out[part, SLAB:, place * LANES : (place + 1) * LANES] = inner[j - HALO]
    wait_all(copies)

    def step(i, _):
        for u in range(UNROLL):
            b = i * (BLOCKS - HALO) + u
            value = apply(
                lambda c: x0[c],
                b + HALO,
                diag[b],
                lambda s: weights[s : s + 1, column(0, b)],
                lambda s: nb[s, b],
            )
            x1[b] = value
            out[lax.div(b, PART // LANES), SLAB:, column(0, lax.rem(b, PART // LANES))] = value
        return 0

    lax.fori_loop(0, 2, step, 0)


def outer_kernel(x0_near, x1_own, far_0, far_1, weights, diag, nb_in, out, x0, x1, nbv, nbs, nb, sems):
    nbv[0] = far_0[:, TAIL:].astype(jnp.int32)
    nbv[1] = far_1[:, TAIL:].astype(jnp.int32)
    copies = start_all(sems, [(nbv.at[k], nbs.at[k]) for k in range(2)] + [(nb_in, nb)])
    for k, far in enumerate((far_0, far_1)):
        base = jnp.where(odd() == k, 3 * HALO + BLOCKS, 0)
        for j in range(HALO):
            half, place = divmod(j, HALO // 2)
            x0[base + j] = far[half * SLAB : (half + 1) * SLAB, place * LANES : (place + 1) * LANES]
    for j in range(EXT1):
        x0[HALO + j] = x0_near[j]
    for j in range(BLOCKS):
        x1[HALO + j] = x1_own[j]
    wait_all(copies)
    for side, ref in ((0, far_0), (1, far_1)):
        base = jnp.where(odd() == side, HALO + BLOCKS, 0)
        for j in range(HALO):
            e = base + j
            cols = slice(HALF + j * LANES, HALF + (j + 1) * LANES)
            x1[e] = apply(
                lambda c: x0[c],
                e + HALO,
                jnp.sum(ref[:, cols], axis=0, keepdims=True),
                lambda s: ref[s : s + 1, cols],
                lambda s: nbs[side, s, j],
            )

    def step(i, _):
        for u in range(UNROLL):
            b = i * UNROLL + u
            value = apply(
                lambda c: x1[c],
                b + HALO,
                diag[b],
                lambda s: weights[s : s + 1, column(0, b)],
                lambda s: nb[s, b],
            )
            place = lax.rem(b, PART // LANES)
            for half in range(SLAB // 8):
                out[lax.div(b, PART // LANES), :, column(half * PART, place)] = value[half * 8 : half * 8 + 8]
        return 0

    lax.fori_loop(0, BLOCKS // UNROLL, step, 0)


def sums(pairs, first):
    folded = []
    for a, b in pairs:
        p = a * b
        folded.append(sum(p[:, k * LANES : (k + 1) * LANES] for k in range(PART // LANES)))
    stack = jnp.concatenate(folded, axis=1)
    shape = (8, stack.shape[1])
    which = lax.broadcasted_iota(jnp.int32, shape, 1) // LANES + first
    pick = (which == lax.broadcasted_iota(jnp.int32, shape, 0)).astype(jnp.float32)
    return lax.dot_general(
        pick, stack, (((1,), (1,)), ((), ())), precision=HIGHEST, preferred_element_type=jnp.float32
    )


def gram_kernel(z01, second, to_modes, own, out, modal, image, partial, s):
    for r in range(PARTS):
        rows = slice(r * SLAB, (r + 1) * SLAB)
        s[rows, 0:PART] = z01[r, 0:SLAB, :]
        s[rows, PART : 2 * PART] = z01[r, SLAB:, :]
    m = mm(to_modes[...], s[...])
    row = lax.broadcasted_iota(jnp.int32, (MODES, MODES), 0)
    col = lax.broadcasted_iota(jnp.int32, (MODES, MODES), 1)
    e = jnp.sum(jnp.where(row == col, own[0:1, :], 0.0), axis=1, keepdims=True)
    m0, m1 = m[:, 0:PART], m[:, PART : 2 * PART]
    i0 = m1 + e * m0
    modal[...] = m0
    image[...] = i0
    partial[...] = e * (m1 + i0)
    g = sums(((m0, m0), (m0, i0), (i0, i0)), 0)
    for r in range(PARTS):
        out[r, :, 0:FLAT] = second[r]
        out[r, :, FLAT:] = g


def again_kernel(z2, modal, image, partial, to_modes, out, s):
    for r in range(PARTS):
        for half in range(SLAB // 8):
            row = r * SLAB + half * 8
            s[row : row + 8, :] = z2[r, :, half * PART : (half + 1) * PART]
    again = mm(to_modes[...], s[...]) + partial[...]
    m0, i0 = modal[...], image[...]
    g = jnp.sum(z2[:, :, FLAT:], axis=0) + sums(((m0, again), (i0, again), (again, again)), 3)
    out[...] = jnp.broadcast_to(g[None], out.shape)


def finish_kernel(got, z01, to_modes, from_modes, own, out, side, s):
    g = jnp.sum(got[...], axis=0)
    mm_, mi, ii, mj, ij, jj = (g[k : k + 1, :] for k in range(6))
    e = own[0:1, :]
    scale = mm_ + 1e-06
    upper = 1.5 * jnp.sqrt(ii / scale)
    lower = upper * 0.125
    center = (upper + lower) * 0.5
    half_width = (upper - lower) * 0.5
    sigma = center / half_width
    rho_zero = 1.0 / sigma
    rho_one = 1.0 / (2.0 * sigma - rho_zero)
    over = 1.0 / center
    c2 = 2.0 * rho_one / half_width
    u0 = rho_one * rho_zero * over + c2
    u1 = -c2 * over
    a = -over - u0
    b = -u1
    side[0:1, :] = mm_ + a * (2.0 * mi + a * ii)
    side[1:2, :] = scale
    ours = jnp.broadcast_to(b * (2.0 * (mj + a * ij) + b * jj), (8, LANES))
    for r in range(PARTS):
        s[r * SLAB : (r + 1) * SLAB, :] = z01[r, 0:SLAB, :]
        s[MODES + r * SLAB : MODES + (r + 1) * SLAB, :] = z01[r, SLAB:, :]
    from_m = from_modes[...]
    to_m = to_modes[...]
    mix = jnp.concatenate([mm(from_m * (over + u0 + u1 * e), to_m), mm(from_m * u1, to_m)], axis=1)
    value = mm(mix, s[...])
    for r in range(PARTS):
        for half in range(SLAB // 8):
            row = r * SLAB + half * 8
            out[r, :, half * PART : (half + 1) * PART] = value[row : row + 8, :]
        out[r, :, FLAT:] = ours


def unpack_kernel(got, side, place, out, mine):
    for r in range(PARTS):
        for half in range(SLAB // 8):
            rows = slice(half * 8, half * 8 + 8)
            out[rows, r * PART : (r + 1) * PART] = got[r, :, half * PART : (half + 1) * PART]
    squares = side[0:1, :] + sum(got[r, 0:1, FLAT:] for r in range(PARTS))
    norm = jnp.sqrt(jnp.maximum(squares, 0.0) / side[1:2, :])
    here = place[0:1, 0:SLAB]
    picked = norm[:, 0:SLAB]
    for r in range(1, PARTS):
        picked = jnp.where(here == r, norm[:, r * SLAB : (r + 1) * SLAB], picked)
    mine[...] = picked


def call(kernel, out_shape, in_specs, scratch=(), out_specs=None, cost=None):
    if out_specs is None:
        out_specs = (VMEM,) * len(out_shape) if isinstance(out_shape, tuple) else VMEM
    return pl.pallas_call(
        kernel,
        out_shape=out_shape,
        in_specs=in_specs,
        out_specs=out_specs,
        scratch_shapes=scratch,
        cost_estimate=cost,
        compiler_params=pltpu.CompilerParams(vmem_limit_bytes=32 * 1024 * 1024),
    )


def pinned(value):
    return pltpu.with_memory_space_constraint(value, pltpu.HBM)


def on_device(sizes, source, to_modes, from_modes, eigenvalue, shifts, weights, neighbors):
    lat = sizes["y"] * sizes["z"]
    place = jnp.full((8, LANES), lax.axis_index(RAD).astype(jnp.float32))
    shift_row = shifts.reshape(1, -1)
    eig = eigenvalue.reshape(1, -1)
    nears, fars = f32(SLAB, NEAR), f32(ROWS, TAIL + LANES)
    offsets = jax.ShapeDtypeStruct(neighbors.shape, neighbors.dtype)
    near_0, near_1, own, nb, shift_row = call(
        pack_kernel,
        (nears, nears, f32(8, LANES), offsets, f32(1, BLOCKS * LANES)),
        [HBM] * 5,
        [pltpu.VMEM((1, LANES), jnp.float32), pltpu.SemaphoreType.DMA((5,))],
    )(*(pinned(v) for v in (source, weights, shift_row, neighbors, eig)))
    swaps = [
        [(i, (i + turn) % lat) for i, turn in ((i, 1 if i % 2 == k else -1) for i in range(lat))]
        for k in range(2)
    ]
    near_0, near_1 = lax.ppermute(near_0, LAT, swaps[0]), lax.ppermute(near_1, LAT, swaps[1])
    smem_offsets = pltpu.SMEM((STENCIL, BLOCKS), jnp.int32)
    inner, diag, place = call(
        inner_kernel,
        (f32(BLOCKS - 2 * HALO, SLAB, LANES), f32(BLOCKS, 1, LANES), f32(8, LANES)),
        [VMEM] * 5,
        [smem_offsets, pltpu.SemaphoreType.DMA((1,))],
        cost=COST_0,
    )(source, weights, shift_row, nb, place)
    first, x0, x1, far_0, far_1 = call(
        edge_kernel,
        (
            f32(PARTS, 2 * SLAB, PART),
            f32(EXT1, SLAB, LANES),
            f32(BLOCKS, SLAB, LANES),
            fars,
            fars,
        ),
        [VMEM] * 8,
        [smem_offsets, pltpu.SemaphoreType.DMA((1,))],
        cost=COST_1,
    )(source, near_0, near_1, weights, shift_row, diag, inner, nb)
    far_0, far_1 = lax.ppermute(far_0, LAT, swaps[0]), lax.ppermute(far_1, LAT, swaps[1])
    z01 = lax.all_to_all(first, RAD, 0, 0, tiled=True)
    second = call(
        outer_kernel,
        f32(PARTS, 8, FLAT),
        [VMEM] * 7,
        [
            pltpu.VMEM((EXT2, SLAB, LANES), jnp.float32),
            pltpu.VMEM((EXT1, SLAB, LANES), jnp.float32),
            pltpu.VMEM((2, ROWS, LANES), jnp.int32),
            pltpu.SMEM((2, ROWS, LANES), jnp.int32),
            smem_offsets,
            pltpu.SemaphoreType.DMA((3,)),
        ],
        cost=COST_2,
    )(x0, x1, far_0, far_1, weights, diag, nb)
    sent, modal, image, partial = call(
        gram_kernel,
        (f32(PARTS, 8, FLAT + LANES),) + (f32(MODES, PART),) * 3,
        [VMEM] * 4,
        [pltpu.VMEM((MODES, 2 * PART), jnp.float32)],
    )(z01, second, to_modes, own)
    z2 = lax.all_to_all(sent, RAD, 0, 0, tiled=True)
    g = call(
        again_kernel,
        f32(lat, 8, LANES),
        [VMEM] * 5,
        [pltpu.VMEM((MODES, PART), jnp.float32)],
    )(z2, modal, image, partial, to_modes)
    g = lax.all_to_all(g, LAT, 0, 0, tiled=True)
    mixed, side = call(
        finish_kernel,
        (f32(PARTS, 8, FLAT + LANES), f32(8, LANES)),
        [VMEM] * 5,
        [pltpu.VMEM((2 * MODES, PART), jnp.float32)],
    )(g, z01, to_modes, from_modes, own)
    got = lax.all_to_all(mixed, RAD, 0, 0, tiled=True)
    smoothed, residual_norm = call(
        unpack_kernel, (f32(SLAB, BLOCKS * LANES), f32(1, SLAB)), [VMEM] * 3
    )(got, side, place)
    return smoothed, residual_norm.reshape(SLAB)


def solution(mesh):
    names = ("y", "z", "x", "core")
    fine = Mesh(np.asarray(mesh.devices).reshape(4, 8, 4, 2), names)
    return jax.shard_map(
        functools.partial(on_device, dict(fine.shape)),
        mesh=fine,
        in_specs=(P(RAD, LAT), P(), P(), P(), P(LAT), P(None, LAT), P(None, LAT)),
        out_specs=(P(RAD, LAT), P(RAD)),
        check_vma=False,
    )
```

```python
import functools

import jax
import jax.numpy as jnp
import numpy as np
from jax import lax
from jax.experimental import pallas as pl
from jax.experimental.pallas import tpu as pltpu
from jax.sharding import Mesh, PartitionSpec as P

LANES = 128
HALO = 8
UNROLL = 8
STENCIL = 31
ROWS = STENCIL + 1
BLOCKS = 32
EXT1 = BLOCKS + 2 * HALO
EXT2 = BLOCKS + 4 * HALO
SLAB = 16
PARTS = 8
PART = BLOCKS * LANES // PARTS
MODES = 128
FLAT = SLAB * PART // 8
WIDE = 2 * HALO * LANES
NEAR = HALO * LANES
HALF = NEAR // 2
TAIL = HALF + NEAR
LAT = ("y", "z")
RAD = ("x", "core")


def work(microseconds):
    return pl.CostEstimate(
        flops=int(microseconds * 1e9), transcendentals=0, bytes_accessed=0
    )


VMEM = pl.BlockSpec(memory_space=pltpu.VMEM)
SMEM = pl.BlockSpec(memory_space=pltpu.SMEM)
HBM = pl.BlockSpec(memory_space=pltpu.HBM)
COST_0 = work(3)
COST_1 = work(3)
COST_2 = work(10)
HIGHEST = lax.Precision.HIGHEST


def f32(*shape):
    return jax.ShapeDtypeStruct(shape, jnp.float32)


def split(a):
    high = a.astype(jnp.bfloat16)
    return high, (a - high.astype(jnp.float32)).astype(jnp.bfloat16)


def mm(a, b):
    (ah, al), (bh, bl) = split(a), split(b)
    dot = functools.partial(jnp.dot, preferred_element_type=jnp.float32)
    return dot(ah, bh) + (dot(ah, bl) + dot(al, bh))


def start_all(sems, pairs):
    copies = [pltpu.make_async_copy(src, dst, sems.at[k]) for k, (src, dst) in enumerate(pairs)]
    for copy in copies:
        copy.start()
    return copies


def wait_all(copies):
    for copy in copies:
        copy.wait()


def odd():
    return lax.rem(lax.axis_index("z"), 2)


def aligned(start):
    return pl.multiple_of(start, LANES)


def rightward(swap):
    return odd() != swap


def pack_kernel(src, weights, shifts, neighbors, eig, near_0, near_1, own, nb, shift_row, eig_in, sems):
    pairs = [(neighbors, nb), (eig, eig_in), (shifts, shift_row)]
    for k, near in enumerate((near_0, near_1)):
        start = aligned(jnp.where(rightward(k), BLOCKS * LANES - NEAR, 0))
        pairs.append((src.at[:, pl.ds(start, NEAR)], near))
    wait_all(start_all(sems, pairs))
    own[...] = jnp.broadcast_to(eig_in[...], own.shape)


def column(start, block):
    return pl.ds(pl.multiple_of(start + block * LANES, LANES), LANES)


def apply(read, centre, d, weight, offset):
    acc = d * read(centre)
    for s in range(STENCIL):
        moved = read(offset(s) + centre)
        if s:
            moved = pltpu.roll(moved, LANES - s, 1)
        acc = acc - weight(s) * moved
    return acc


def inner_kernel(src, weights, shifts, nb_in, place_in, x1, diag, place, far_0, far_1, nb, sems):
    copies = start_all(sems, [(nb_in, nb)])
    place[...] = place_in[...]
    offsets = nb_in[...].astype(jnp.float32)
    for k, out in enumerate((far_0, far_1)):
        up = rightward(k)
        near = aligned(jnp.where(up, BLOCKS * LANES - NEAR, 0))
        far = aligned(jnp.where(up, BLOCKS * LANES - WIDE, NEAR))
        out[0:SLAB, 0:HALF] = src[:, pl.ds(far, HALF)]
        out[SLAB : 2 * SLAB, 0:HALF] = src[:, pl.ds(aligned(far + HALF), HALF)]
        out[0:STENCIL, HALF:TAIL] = weights[:, pl.ds(near, NEAR)]
        out[STENCIL:ROWS, HALF:TAIL] = shifts[:, pl.ds(near, NEAR)]
        out[:, TAIL:] = jnp.zeros((ROWS, LANES), jnp.float32)
        out[0:STENCIL, TAIL : TAIL + HALO] = jnp.where(
            up, offsets[:, BLOCKS - HALO :], offsets[:, :HALO]
        )
    for j in range(BLOCKS):
        cols = slice(j * LANES, (j + 1) * LANES)
        diag[j] = jnp.sum(weights[:, cols], axis=0, keepdims=True) + shifts[:, cols]
    wait_all(copies)

    for b in range(HALO, BLOCKS - HALO):
        x1[b - HALO] = apply(
            lambda c: src[:, column(0, c)],
            b,
            diag[b],
            lambda s: weights[s : s + 1, column(0, b)],
            lambda s: nb[s, b],
        )


def edge_kernel(src, near_0, near_1, weights, diag, inner, nb_in, out, x0, x1, nb, sems):
    copies = start_all(sems, [(nb_in, nb)])
    for k, near in enumerate((near_0, near_1)):
        base = jnp.where(rightward(k), HALO + BLOCKS, 0)
        for j in range(HALO):
            x0[base + j] = near[:, j * LANES : (j + 1) * LANES]
    for j in range(BLOCKS):
        x0[HALO + j] = src[:, j * LANES : (j + 1) * LANES]
    for r in range(PARTS):
        out[r, 0:SLAB, :] = src[:, r * PART : (r + 1) * PART]
    for j in range(HALO, BLOCKS - HALO):
        x1[j] = inner[j - HALO]
        part, place = divmod(j, PART // LANES)
        out[part, SLAB:, place * LANES : (place + 1) * LANES] = inner[j - HALO]
    wait_all(copies)

    for b in (*range(HALO), *range(BLOCKS - HALO, BLOCKS)):
        value = apply(
            lambda c: x0[c],
            b + HALO,
            diag[b],
            lambda s: weights[s : s + 1, column(0, b)],
            lambda s: nb[s, b],
        )
        x1[b] = value
        part, place = divmod(b, PART // LANES)
        out[part, SLAB:, place * LANES : (place + 1) * LANES] = value


def outer_kernel(x0_near, x1_own, far_0, far_1, weights, diag, nb_in, out, x0, x1, nbv, nbs, nb, sems):
    nbv[0] = far_0[:, TAIL:].astype(jnp.int32)
    nbv[1] = far_1[:, TAIL:].astype(jnp.int32)
    copies = start_all(sems, [(nbv.at[k], nbs.at[k]) for k in range(2)] + [(nb_in, nb)])
    for k, far in enumerate((far_0, far_1)):
        base = jnp.where(rightward(k), 3 * HALO + BLOCKS, 0)
        for j in range(HALO):
            half, place = divmod(j, HALO // 2)
            x0[base + j] = far[half * SLAB : (half + 1) * SLAB, place * LANES : (place + 1) * LANES]
    for j in range(EXT1):
        x0[HALO + j] = x0_near[j]
    for j in range(BLOCKS):
        x1[HALO + j] = x1_own[j]
    wait_all(copies)
    for side, ref in ((0, far_0), (1, far_1)):
        base = jnp.where(rightward(side), HALO + BLOCKS, 0)
        for j in range(HALO):
            e = base + j
            cols = slice(HALF + j * LANES, HALF + (j + 1) * LANES)
            x1[e] = apply(
                lambda c: x0[c],
                e + HALO,
                jnp.sum(ref[:, cols], axis=0, keepdims=True),
                lambda s: ref[s : s + 1, cols],
                lambda s: nbs[side, s, j],
            )

    def step(i, _):
        for u in range(UNROLL):
            b = i * UNROLL + u
            value = apply(
                lambda c: x1[c],
                b + HALO,
                diag[b],
                lambda s: weights[s : s + 1, column(0, b)],
                lambda s: nb[s, b],
            )
            place = lax.rem(b, PART // LANES)
            for half in range(SLAB // 8):
                out[lax.div(b, PART // LANES), :, column(half * PART, place)] = value[half * 8 : half * 8 + 8]
        return 0

    lax.fori_loop(0, BLOCKS // UNROLL, step, 0)


def sums(pairs, first):
    folded = []
    for a, b in pairs:
        p = a * b
        folded.append(sum(p[:, k * LANES : (k + 1) * LANES] for k in range(PART // LANES)))
    stack = jnp.concatenate(folded, axis=1)
    shape = (8, stack.shape[1])
    which = lax.broadcasted_iota(jnp.int32, shape, 1) // LANES + first
    pick = (which == lax.broadcasted_iota(jnp.int32, shape, 0)).astype(jnp.float32)
    return lax.dot_general(
        pick, stack, (((1,), (1,)), ((), ())), precision=HIGHEST, preferred_element_type=jnp.float32
    )


def gram_kernel(z01, second, to_modes, own, out, modal, image, partial, s):
    for r in range(PARTS):
        rows = slice(r * SLAB, (r + 1) * SLAB)
        s[rows, 0:PART] = z01[r, 0:SLAB, :]
        s[rows, PART : 2 * PART] = z01[r, SLAB:, :]
    m = mm(to_modes[...], s[...])
    row = lax.broadcasted_iota(jnp.int32, (MODES, MODES), 0)
    col = lax.broadcasted_iota(jnp.int32, (MODES, MODES), 1)
    e = jnp.sum(jnp.where(row == col, own[0:1, :], 0.0), axis=1, keepdims=True)
    m0, m1 = m[:, 0:PART], m[:, PART : 2 * PART]
    i0 = m1 + e * m0
    modal[...] = m0
    image[...] = i0
    partial[...] = e * (m1 + i0)
    g = sums(((m0, m0), (m0, i0), (i0, i0)), 0)
    for r in range(PARTS):
        out[r, :, 0:FLAT] = second[r]
        out[r, :, FLAT:] = g


def again_kernel(z2, modal, image, partial, to_modes, out, s):
    for r in range(PARTS):
        for half in range(SLAB // 8):
            row = r * SLAB + half * 8
            s[row : row + 8, :] = z2[r, :, half * PART : (half + 1) * PART]
    again = mm(to_modes[...], s[...]) + partial[...]
    m0, i0 = modal[...], image[...]
    g = jnp.sum(z2[:, :, FLAT:], axis=0) + sums(((m0, again), (i0, again), (again, again)), 3)
    out[...] = jnp.broadcast_to(g[None], out.shape)


def finish_kernel(got, z01, to_modes, from_modes, own, out, side, s):
    g = jnp.sum(got[...], axis=0)
    mm_, mi, ii, mj, ij, jj = (g[k : k + 1, :] for k in range(6))
    e = own[0:1, :]
    scale = mm_ + 1e-06
    upper = 1.5 * jnp.sqrt(ii / scale)
    lower = upper * 0.125
    center = (upper + lower) * 0.5
    half_width = (upper - lower) * 0.5
    sigma = center / half_width
    rho_zero = 1.0 / sigma
    rho_one = 1.0 / (2.0 * sigma - rho_zero)
    over = 1.0 / center
    c2 = 2.0 * rho_one / half_width
    u0 = rho_one * rho_zero * over + c2
    u1 = -c2 * over
    a = -over - u0
    b = -u1
    side[0:1, :] = mm_ + a * (2.0 * mi + a * ii)
    side[1:2, :] = scale
    ours = jnp.broadcast_to(b * (2.0 * (mj + a * ij) + b * jj), (8, LANES))
    for r in range(PARTS):
        s[r * SLAB : (r + 1) * SLAB, :] = z01[r, 0:SLAB, :]
        s[MODES + r * SLAB : MODES + (r + 1) * SLAB, :] = z01[r, SLAB:, :]
    from_m = from_modes[...]
    to_m = to_modes[...]
    mix = jnp.concatenate([mm(from_m * (over + u0 + u1 * e), to_m), mm(from_m * u1, to_m)], axis=1)
    value = mm(mix, s[...])
    for r in range(PARTS):
        for half in range(SLAB // 8):
            row = r * SLAB + half * 8
            out[r, :, half * PART : (half + 1) * PART] = value[row : row + 8, :]
        out[r, :, FLAT:] = ours


def unpack_kernel(got, side, place, out, mine):
    for r in range(PARTS):
        for half in range(SLAB // 8):
            rows = slice(half * 8, half * 8 + 8)
            out[rows, r * PART : (r + 1) * PART] = got[r, :, half * PART : (half + 1) * PART]
    squares = side[0:1, :] + sum(got[r, 0:1, FLAT:] for r in range(PARTS))
    norm = jnp.sqrt(jnp.maximum(squares, 0.0) / side[1:2, :])
    here = place[0:1, 0:SLAB]
    picked = norm[:, 0:SLAB]
    for r in range(1, PARTS):
        picked = jnp.where(here == r, norm[:, r * SLAB : (r + 1) * SLAB], picked)
    mine[...] = picked


def call(kernel, out_shape, in_specs, scratch=(), out_specs=None, cost=None):
    if out_specs is None:
        out_specs = (VMEM,) * len(out_shape) if isinstance(out_shape, tuple) else VMEM
    return pl.pallas_call(
        kernel,
        out_shape=out_shape,
        in_specs=in_specs,
        out_specs=out_specs,
        scratch_shapes=scratch,
        cost_estimate=cost,
        compiler_params=pltpu.CompilerParams(vmem_limit_bytes=32 * 1024 * 1024),
    )


def pinned(value):
    return pltpu.with_memory_space_constraint(value, pltpu.HBM)


def on_device(sizes, source, to_modes, from_modes, eigenvalue, shifts, weights, neighbors):
    lat = sizes["y"] * sizes["z"]
    place = jnp.full((8, LANES), lax.axis_index(RAD).astype(jnp.float32))
    shift_row = shifts.reshape(1, -1)
    eig = eigenvalue.reshape(1, -1)
    nears, fars = f32(SLAB, NEAR), f32(ROWS, TAIL + LANES)
    offsets = jax.ShapeDtypeStruct(neighbors.shape, neighbors.dtype)
    near_0, near_1, own, nb, shift_row = call(
        pack_kernel,
        (nears, nears, f32(8, LANES), offsets, f32(1, BLOCKS * LANES)),
        [HBM] * 5,
        [pltpu.VMEM((1, LANES), jnp.float32), pltpu.SemaphoreType.DMA((5,))],
    )(*(pinned(v) for v in (source, weights, shift_row, neighbors, eig)))
    swaps = [
        [(i, (i + turn) % lat) for i, turn in ((i, 1 if i % 2 != k else -1) for i in range(lat))]
        for k in range(2)
    ]
    near_0, near_1 = lax.ppermute(near_0, LAT, swaps[0]), lax.ppermute(near_1, LAT, swaps[1])
    smem_offsets = pltpu.SMEM((STENCIL, BLOCKS), jnp.int32)
    inner, diag, place, far_0, far_1 = call(
        inner_kernel,
        (f32(BLOCKS - 2 * HALO, SLAB, LANES), f32(BLOCKS, 1, LANES), f32(8, LANES), fars, fars),
        [VMEM] * 5,
        [smem_offsets, pltpu.SemaphoreType.DMA((1,))],
        cost=COST_0,
    )(source, weights, shift_row, nb, place)
    far_0, far_1 = lax.ppermute(far_0, LAT, swaps[0]), lax.ppermute(far_1, LAT, swaps[1])
    first, x0, x1 = call(
        edge_kernel,
        (f32(PARTS, 2 * SLAB, PART), f32(EXT1, SLAB, LANES), f32(BLOCKS, SLAB, LANES)),
        [VMEM] * 7,
        [smem_offsets, pltpu.SemaphoreType.DMA((1,))],
        cost=COST_1,
    )(source, near_0, near_1, weights, diag, inner, nb)
    z01 = lax.all_to_all(first, RAD, 0, 0, tiled=True)
    second = call(
        outer_kernel,
        f32(PARTS, 8, FLAT),
        [VMEM] * 7,
        [
            pltpu.VMEM((EXT2, SLAB, LANES), jnp.float32),
            pltpu.VMEM((EXT1, SLAB, LANES), jnp.float32),
            pltpu.VMEM((2, ROWS, LANES), jnp.int32),
            pltpu.SMEM((2, ROWS, LANES), jnp.int32),
            smem_offsets,
            pltpu.SemaphoreType.DMA((3,)),
        ],
        cost=COST_2,
    )(x0, x1, far_0, far_1, weights, diag, nb)
    sent, modal, image, partial = call(
        gram_kernel,
        (f32(PARTS, 8, FLAT + LANES),) + (f32(MODES, PART),) * 3,
        [VMEM] * 4,
        [pltpu.VMEM((MODES, 2 * PART), jnp.float32)],
    )(z01, second, to_modes, own)
    z2 = lax.all_to_all(sent, RAD, 0, 0, tiled=True)
    g = call(
        again_kernel,
        f32(lat, 8, LANES),
        [VMEM] * 5,
        [pltpu.VMEM((MODES, PART), jnp.float32)],
    )(z2, modal, image, partial, to_modes)
    g = lax.all_to_all(g, LAT, 0, 0, tiled=True)
    mixed, side = call(
        finish_kernel,
        (f32(PARTS, 8, FLAT + LANES), f32(8, LANES)),
        [VMEM] * 5,
        [pltpu.VMEM((2 * MODES, PART), jnp.float32)],
    )(g, z01, to_modes, from_modes, own)
    got = lax.all_to_all(mixed, RAD, 0, 0, tiled=True)
    smoothed, residual_norm = call(
        unpack_kernel, (f32(SLAB, BLOCKS * LANES), f32(1, SLAB)), [VMEM] * 3
    )(got, side, place)
    return smoothed, residual_norm.reshape(SLAB)


def solution(mesh):
    names = ("y", "z", "x", "core")
    fine = Mesh(np.asarray(mesh.devices).reshape(4, 8, 4, 2), names)
    return jax.shard_map(
        functools.partial(on_device, dict(fine.shape)),
        mesh=fine,
        in_specs=(P(RAD, LAT), P(), P(), P(), P(LAT), P(None, LAT), P(None, LAT)),
        out_specs=(P(RAD, LAT), P(RAD)),
        check_vma=False,
    )
```

```python
import functools

import jax
import jax.numpy as jnp
import numpy as np
from jax import lax
from jax.experimental import pallas as pl
from jax.experimental.pallas import tpu as pltpu
from jax.sharding import Mesh, PartitionSpec as P

LANES = 128
HALO = 8
UNROLL = 8
STENCIL = 31
ROWS = STENCIL + 1
BLOCKS = 32
EXT1 = BLOCKS + 2 * HALO
EXT2 = BLOCKS + 4 * HALO
SLAB = 16
PARTS = 8
PART = BLOCKS * LANES // PARTS
MODES = 128
FLAT = SLAB * PART // 8
WIDE = 2 * HALO * LANES
NEAR = HALO * LANES
HALF = NEAR // 2
TAIL = HALF + NEAR
LAT = ("y", "z")
RAD = ("x", "core")


def work(microseconds):
    return pl.CostEstimate(
        flops=int(microseconds * 1e9), transcendentals=0, bytes_accessed=0
    )


VMEM = pl.BlockSpec(memory_space=pltpu.VMEM)
SMEM = pl.BlockSpec(memory_space=pltpu.SMEM)
HBM = pl.BlockSpec(memory_space=pltpu.HBM)
COST_0 = work(3)
COST_1 = work(3)
COST_2 = work(10)
HIGHEST = lax.Precision.HIGHEST


def f32(*shape):
    return jax.ShapeDtypeStruct(shape, jnp.float32)


def split(a):
    high = a.astype(jnp.bfloat16)
    return high, (a - high.astype(jnp.float32)).astype(jnp.bfloat16)


def mm(a, b):
    (ah, al), (bh, bl) = split(a), split(b)
    dot = functools.partial(jnp.dot, preferred_element_type=jnp.float32)
    return dot(ah, bh) + (dot(ah, bl) + dot(al, bh))


def start_all(sems, pairs):
    copies = [pltpu.make_async_copy(src, dst, sems.at[k]) for k, (src, dst) in enumerate(pairs)]
    for copy in copies:
        copy.start()
    return copies


def wait_all(copies):
    for copy in copies:
        copy.wait()


def odd():
    return lax.rem(lax.axis_index("z"), 2)


def aligned(start):
    return pl.multiple_of(start, LANES)


def rightward(swap):
    return odd() != swap


def pack_kernel(src, weights, shifts, neighbors, eig, near_0, near_1, own, nb, shift_row, eig_in, sems):
    pairs = [(neighbors, nb), (eig, eig_in), (shifts, shift_row)]
    for k, near in enumerate((near_0, near_1)):
        start = aligned(jnp.where(rightward(k), BLOCKS * LANES - NEAR, 0))
        pairs.append((src.at[:, pl.ds(start, NEAR)], near))
    wait_all(start_all(sems, pairs))
    own[...] = jnp.broadcast_to(eig_in[...], own.shape)


def column(start, block):
    return pl.ds(pl.multiple_of(start + block * LANES, LANES), LANES)


def apply(read, centre, d, weight, offset):
    acc = d * read(centre)
    for s in range(STENCIL):
        moved = read(offset(s) + centre)
        if s:
            moved = pltpu.roll(moved, LANES - s, 1)
        acc = acc - weight(s) * moved
    return acc


def inner_kernel(src, weights, shifts, nb_in, place_in, x1, diag, place, far_0, far_1, nb, sems):
    copies = start_all(sems, [(nb_in, nb)])
    place[...] = place_in[...]
    offsets = nb_in[...].astype(jnp.float32)
    for k, out in enumerate((far_0, far_1)):
        up = rightward(k)
        near = aligned(jnp.where(up, BLOCKS * LANES - NEAR, 0))
        far = aligned(jnp.where(up, BLOCKS * LANES - WIDE, NEAR))
        out[0:SLAB, 0:HALF] = src[:, pl.ds(far, HALF)]
        out[SLAB : 2 * SLAB, 0:HALF] = src[:, pl.ds(aligned(far + HALF), HALF)]
        out[0:STENCIL, HALF:TAIL] = weights[:, pl.ds(near, NEAR)]
        out[STENCIL:ROWS, HALF:TAIL] = shifts[:, pl.ds(near, NEAR)]
        out[:, TAIL:] = jnp.zeros((ROWS, LANES), jnp.float32)
        out[0:STENCIL, TAIL : TAIL + HALO] = jnp.where(
            up, offsets[:, BLOCKS - HALO :], offsets[:, :HALO]
        )
    for j in range(BLOCKS):
        cols = slice(j * LANES, (j + 1) * LANES)
        diag[j] = jnp.sum(weights[:, cols], axis=0, keepdims=True) + shifts[:, cols]
    wait_all(copies)

    for b in range(HALO, BLOCKS - HALO):
        x1[b - HALO] = apply(
            lambda c: src[:, column(0, c)],
            b,
            diag[b],
            lambda s: weights[s : s + 1, column(0, b)],
            lambda s: nb[s, b],
        )


def edge_kernel(src, near_0, near_1, weights, diag, inner, nb_in, out, x0, x1, nb, buffer, sems):
    offsets = pltpu.make_async_copy(nb_in, nb, sems.at[PARTS])
    offsets.start()
    for k, near in enumerate((near_0, near_1)):
        base = jnp.where(rightward(k), HALO + BLOCKS, 0)
        for j in range(HALO):
            x0[base + j] = near[:, j * LANES : (j + 1) * LANES]
    for j in range(BLOCKS):
        x0[HALO + j] = src[:, j * LANES : (j + 1) * LANES]
    for r in range(PARTS):
        buffer[r, 0:SLAB, :] = src[:, r * PART : (r + 1) * PART]
    for j in range(HALO, BLOCKS - HALO):
        x1[j] = inner[j - HALO]
        part, place = divmod(j, PART // LANES)
        buffer[part, SLAB:, place * LANES : (place + 1) * LANES] = inner[j - HALO]
    parts = [pltpu.make_async_copy(buffer.at[r], out.at[r], sems.at[r]) for r in range(PARTS)]
    per_part = PART // LANES
    for r in range(HALO // per_part, (BLOCKS - HALO) // per_part):
        parts[r].start()
    offsets.wait()

    for b in (*range(HALO), *range(BLOCKS - HALO, BLOCKS)):
        value = apply(
            lambda c: x0[c],
            b + HALO,
            diag[b],
            lambda s: weights[s : s + 1, column(0, b)],
            lambda s: nb[s, b],
        )
        x1[b] = value
        part, place = divmod(b, per_part)
        buffer[part, SLAB:, place * LANES : (place + 1) * LANES] = value
        if place == per_part - 1:
            parts[part].start()
    wait_all(parts)


def outer_kernel(x0_near, x1_own, far_0, far_1, weights, diag, nb_in, out, x0, x1, nbv, nbs, nb, sems):
    nbv[0] = far_0[:, TAIL:].astype(jnp.int32)
    nbv[1] = far_1[:, TAIL:].astype(jnp.int32)
    copies = start_all(sems, [(nbv.at[k], nbs.at[k]) for k in range(2)] + [(nb_in, nb)])
    for k, far in enumerate((far_0, far_1)):
        base = jnp.where(rightward(k), 3 * HALO + BLOCKS, 0)
        for j in range(HALO):
            half, place = divmod(j, HALO // 2)
            x0[base + j] = far[half * SLAB : (half + 1) * SLAB, place * LANES : (place + 1) * LANES]
    for j in range(EXT1):
        x0[HALO + j] = x0_near[j]
    for j in range(BLOCKS):
        x1[HALO + j] = x1_own[j]
    wait_all(copies)
    for side, ref in ((0, far_0), (1, far_1)):
        base = jnp.where(rightward(side), HALO + BLOCKS, 0)
        for j in range(HALO):
            e = base + j
            cols = slice(HALF + j * LANES, HALF + (j + 1) * LANES)
            x1[e] = apply(
                lambda c: x0[c],
                e + HALO,
                jnp.sum(ref[:, cols], axis=0, keepdims=True),
                lambda s: ref[s : s + 1, cols],
                lambda s: nbs[side, s, j],
            )

    def step(i, _):
        for u in range(UNROLL):
            b = i * UNROLL + u
            value = apply(
                lambda c: x1[c],
                b + HALO,
                diag[b],
                lambda s: weights[s : s + 1, column(0, b)],
                lambda s: nb[s, b],
            )
            place = lax.rem(b, PART // LANES)
            for half in range(SLAB // 8):
                out[lax.div(b, PART // LANES), :, column(half * PART, place)] = value[half * 8 : half * 8 + 8]
        return 0

    lax.fori_loop(0, BLOCKS // UNROLL, step, 0)


def sums(pairs, first):
    folded = []
    for a, b in pairs:
        p = a * b
        folded.append(sum(p[:, k * LANES : (k + 1) * LANES] for k in range(PART // LANES)))
    stack = jnp.concatenate(folded, axis=1)
    shape = (8, stack.shape[1])
    which = lax.broadcasted_iota(jnp.int32, shape, 1) // LANES + first
    pick = (which == lax.broadcasted_iota(jnp.int32, shape, 0)).astype(jnp.float32)
    return lax.dot_general(
        pick, stack, (((1,), (1,)), ((), ())), precision=HIGHEST, preferred_element_type=jnp.float32
    )


def gram_kernel(z01, second, to_modes, own, out, modal, image, partial, s):
    for r in range(PARTS):
        rows = slice(r * SLAB, (r + 1) * SLAB)
        s[rows, 0:PART] = z01[r, 0:SLAB, :]
        s[rows, PART : 2 * PART] = z01[r, SLAB:, :]
    m = mm(to_modes[...], s[...])
    row = lax.broadcasted_iota(jnp.int32, (MODES, MODES), 0)
    col = lax.broadcasted_iota(jnp.int32, (MODES, MODES), 1)
    e = jnp.sum(jnp.where(row == col, own[0:1, :], 0.0), axis=1, keepdims=True)
    m0, m1 = m[:, 0:PART], m[:, PART : 2 * PART]
    i0 = m1 + e * m0
    modal[...] = m0
    image[...] = i0
    partial[...] = e * (m1 + i0)
    g = sums(((m0, m0), (m0, i0), (i0, i0)), 0)
    for r in range(PARTS):
        out[r, :, 0:FLAT] = second[r]
        out[r, :, FLAT:] = g


def again_kernel(z2, modal, image, partial, to_modes, out, s):
    for r in range(PARTS):
        for half in range(SLAB // 8):
            row = r * SLAB + half * 8
            s[row : row + 8, :] = z2[r, :, half * PART : (half + 1) * PART]
    again = mm(to_modes[...], s[...]) + partial[...]
    m0, i0 = modal[...], image[...]
    g = jnp.sum(z2[:, :, FLAT:], axis=0) + sums(((m0, again), (i0, again), (again, again)), 3)
    row = jnp.concatenate([g[k : k + 1, :] for k in range(6)], axis=1)
    out[...] = jnp.broadcast_to(row[None], out.shape)


def finish_kernel(got, z01, to_modes, from_modes, own, out, side, s):
    g = jnp.sum(got[...], axis=0)
    mm_, mi, ii, mj, ij, jj = (g[:, k * LANES : (k + 1) * LANES] for k in range(6))
    e = own[0:1, :]
    scale = mm_ + 1e-06
    upper = 1.5 * jnp.sqrt(ii / scale)
    lower = upper * 0.125
    center = (upper + lower) * 0.5
    half_width = (upper - lower) * 0.5
    sigma = center / half_width
    rho_zero = 1.0 / sigma
    rho_one = 1.0 / (2.0 * sigma - rho_zero)
    over = 1.0 / center
    c2 = 2.0 * rho_one / half_width
    u0 = rho_one * rho_zero * over + c2
    u1 = -c2 * over
    a = -over - u0
    b = -u1
    side[0:1, :] = mm_ + a * (2.0 * mi + a * ii)
    side[1:2, :] = scale
    ours = jnp.broadcast_to(b * (2.0 * (mj + a * ij) + b * jj), (8, LANES))
    for r in range(PARTS):
        s[r * SLAB : (r + 1) * SLAB, :] = z01[r, 0:SLAB, :]
        s[MODES + r * SLAB : MODES + (r + 1) * SLAB, :] = z01[r, SLAB:, :]
    from_m = from_modes[...]
    to_m = to_modes[...]
    mix = jnp.concatenate([mm(from_m * (over + u0 + u1 * e), to_m), mm(from_m * u1, to_m)], axis=1)
    value = mm(mix, s[...])
    for r in range(PARTS):
        for half in range(SLAB // 8):
            row = r * SLAB + half * 8
            out[r, :, half * PART : (half + 1) * PART] = value[row : row + 8, :]
        out[r, :, FLAT:] = ours


def unpack_kernel(got, side, place, out, mine):
    for r in range(PARTS):
        for half in range(SLAB // 8):
            rows = slice(half * 8, half * 8 + 8)
            out[rows, r * PART : (r + 1) * PART] = got[r, :, half * PART : (half + 1) * PART]
    squares = side[0:1, :] + sum(got[r, 0:1, FLAT:] for r in range(PARTS))
    norm = jnp.sqrt(jnp.maximum(squares, 0.0) / side[1:2, :])
    here = place[0:1, 0:SLAB]
    picked = norm[:, 0:SLAB]
    for r in range(1, PARTS):
        picked = jnp.where(here == r, norm[:, r * SLAB : (r + 1) * SLAB], picked)
    mine[...] = picked


def call(kernel, out_shape, in_specs, scratch=(), out_specs=None, cost=None):
    if out_specs is None:
        out_specs = (VMEM,) * len(out_shape) if isinstance(out_shape, tuple) else VMEM
    return pl.pallas_call(
        kernel,
        out_shape=out_shape,
        in_specs=in_specs,
        out_specs=out_specs,
        scratch_shapes=scratch,
        cost_estimate=cost,
        compiler_params=pltpu.CompilerParams(vmem_limit_bytes=32 * 1024 * 1024),
    )


def pinned(value):
    return pltpu.with_memory_space_constraint(value, pltpu.HBM)


def on_device(sizes, source, to_modes, from_modes, eigenvalue, shifts, weights, neighbors):
    lat = sizes["y"] * sizes["z"]
    place = jnp.full((8, LANES), lax.axis_index(RAD).astype(jnp.float32))
    shift_row = shifts.reshape(1, -1)
    eig = eigenvalue.reshape(1, -1)
    nears, fars = f32(SLAB, NEAR), f32(ROWS, TAIL + LANES)
    offsets = jax.ShapeDtypeStruct(neighbors.shape, neighbors.dtype)
    near_0, near_1, own, nb, shift_row = call(
        pack_kernel,
        (nears, nears, f32(8, LANES), offsets, f32(1, BLOCKS * LANES)),
        [HBM] * 5,
        [pltpu.VMEM((1, LANES), jnp.float32), pltpu.SemaphoreType.DMA((5,))],
    )(*(pinned(v) for v in (source, weights, shift_row, neighbors, eig)))
    swaps = [
        [(i, (i + turn) % lat) for i, turn in ((i, 1 if i % 2 != k else -1) for i in range(lat))]
        for k in range(2)
    ]
    near_0, near_1 = lax.ppermute(near_0, LAT, swaps[0]), lax.ppermute(near_1, LAT, swaps[1])
    smem_offsets = pltpu.SMEM((STENCIL, BLOCKS), jnp.int32)
    inner, diag, place, far_0, far_1 = call(
        inner_kernel,
        (f32(BLOCKS - 2 * HALO, SLAB, LANES), f32(BLOCKS, 1, LANES), f32(8, LANES), fars, fars),
        [VMEM] * 5,
        [smem_offsets, pltpu.SemaphoreType.DMA((1,))],
        cost=COST_0,
    )(source, weights, shift_row, nb, place)
    far_0, far_1 = lax.ppermute(far_0, LAT, swaps[0]), lax.ppermute(far_1, LAT, swaps[1])
    first, x0, x1 = call(
        edge_kernel,
        (f32(PARTS, 2 * SLAB, PART), f32(EXT1, SLAB, LANES), f32(BLOCKS, SLAB, LANES)),
        [VMEM] * 7,
        [
            smem_offsets,
            pltpu.VMEM((PARTS, 2 * SLAB, PART), jnp.float32),
            pltpu.SemaphoreType.DMA((PARTS + 1,)),
        ],
        out_specs=(HBM, VMEM, VMEM),
        cost=COST_1,
    )(source, near_0, near_1, weights, diag, inner, nb)
    z01 = lax.all_to_all(first, RAD, 0, 0, tiled=True)
    second = call(
        outer_kernel,
        f32(PARTS, 8, FLAT),
        [VMEM] * 7,
        [
            pltpu.VMEM((EXT2, SLAB, LANES), jnp.float32),
            pltpu.VMEM((EXT1, SLAB, LANES), jnp.float32),
            pltpu.VMEM((2, ROWS, LANES), jnp.int32),
            pltpu.SMEM((2, ROWS, LANES), jnp.int32),
            smem_offsets,
            pltpu.SemaphoreType.DMA((3,)),
        ],
        cost=COST_2,
    )(x0, x1, far_0, far_1, weights, diag, nb)
    sent, modal, image, partial = call(
        gram_kernel,
        (f32(PARTS, 8, FLAT + LANES),) + (f32(MODES, PART),) * 3,
        [VMEM] * 4,
        [pltpu.VMEM((MODES, 2 * PART), jnp.float32)],
    )(z01, second, to_modes, own)
    z2 = lax.all_to_all(sent, RAD, 0, 0, tiled=True)
    g = call(
        again_kernel,
        f32(lat, 1, 6 * LANES),
        [VMEM] * 5,
        [pltpu.VMEM((MODES, PART), jnp.float32)],
    )(z2, modal, image, partial, to_modes)
    g = lax.all_to_all(g, LAT, 0, 0, tiled=True)
    mixed, side = call(
        finish_kernel,
        (f32(PARTS, 8, FLAT + LANES), f32(8, LANES)),
        [VMEM] * 5,
        [pltpu.VMEM((2 * MODES, PART), jnp.float32)],
    )(g, z01, to_modes, from_modes, own)
    got = lax.all_to_all(mixed, RAD, 0, 0, tiled=True)
    smoothed, residual_norm = call(
        unpack_kernel, (f32(SLAB, BLOCKS * LANES), f32(1, SLAB)), [VMEM] * 3
    )(got, side, place)
    return smoothed, residual_norm.reshape(SLAB)


def solution(mesh):
    names = ("y", "z", "x", "core")
    fine = Mesh(np.asarray(mesh.devices).reshape(4, 8, 4, 2), names)
    return jax.shard_map(
        functools.partial(on_device, dict(fine.shape)),
        mesh=fine,
        in_specs=(P(RAD, LAT), P(), P(), P(), P(LAT), P(None, LAT), P(None, LAT)),
        out_specs=(P(RAD, LAT), P(RAD)),
        check_vma=False,
    )
```

```python
import functools

import jax
import jax.numpy as jnp
import numpy as np
from jax import lax
from jax.experimental import pallas as pl
from jax.experimental.pallas import tpu as pltpu
from jax.sharding import Mesh, PartitionSpec as P

LANES = 128
HALO = 8
UNROLL = 8
STENCIL = 31
ROWS = STENCIL + 1
BLOCKS = 32
EXT1 = BLOCKS + 2 * HALO
EXT2 = BLOCKS + 4 * HALO
SLAB = 16
PARTS = 8
PART = BLOCKS * LANES // PARTS
MODES = 128
FLAT = SLAB * PART // 8
WIDE = 2 * HALO * LANES
NEAR = HALO * LANES
HALF = NEAR // 2
TAIL = HALF + NEAR
LAT = ("y", "z")
RAD = ("x", "core")


def work(microseconds):
    return pl.CostEstimate(
        flops=int(microseconds * 1e9), transcendentals=0, bytes_accessed=0
    )


VMEM = pl.BlockSpec(memory_space=pltpu.VMEM)
SMEM = pl.BlockSpec(memory_space=pltpu.SMEM)
HBM = pl.BlockSpec(memory_space=pltpu.HBM)
COST_0 = work(3)
COST_1 = work(3)
COST_2 = work(10)
HIGHEST = lax.Precision.HIGHEST


def f32(*shape):
    return jax.ShapeDtypeStruct(shape, jnp.float32)


def split(a):
    high = a.astype(jnp.bfloat16)
    return high, (a - high.astype(jnp.float32)).astype(jnp.bfloat16)


def mm(a, b):
    (ah, al), (bh, bl) = split(a), split(b)
    dot = functools.partial(jnp.dot, preferred_element_type=jnp.float32)
    return dot(ah, bh) + (dot(ah, bl) + dot(al, bh))


def start_all(sems, pairs):
    copies = [pltpu.make_async_copy(src, dst, sems.at[k]) for k, (src, dst) in enumerate(pairs)]
    for copy in copies:
        copy.start()
    return copies


def wait_all(copies):
    for copy in copies:
        copy.wait()


def odd():
    return lax.rem(lax.axis_index("z"), 2)


def aligned(start):
    return pl.multiple_of(start, LANES)


def rightward(swap):
    return odd() != swap


def pack_kernel(src, weights, shifts, neighbors, eig, near_0, near_1, own, nb, shift_row, eig_in, sems):
    pairs = [(neighbors, nb), (eig, eig_in), (shifts, shift_row)]
    for k, near in enumerate((near_0, near_1)):
        start = aligned(jnp.where(rightward(k), BLOCKS * LANES - NEAR, 0))
        pairs.append((src.at[:, pl.ds(start, NEAR)], near))
    wait_all(start_all(sems, pairs))
    own[...] = jnp.broadcast_to(eig_in[...], own.shape)


def column(start, block):
    return pl.ds(pl.multiple_of(start + block * LANES, LANES), LANES)


def apply(read, centre, d, weight, offset):
    acc = d * read(centre)
    for s in range(STENCIL):
        moved = read(offset(s) + centre)
        if s:
            moved = pltpu.roll(moved, LANES - s, 1)
        acc = acc - weight(s) * moved
    return acc


def inner_kernel(src, weights, shifts, nb_in, place_in, x1, diag, place, far_0, far_1, nb, sems):
    copies = start_all(sems, [(nb_in, nb)])
    place[...] = place_in[...]
    offsets = nb_in[...].astype(jnp.float32)
    for k, out in enumerate((far_0, far_1)):
        up = rightward(k)
        near = aligned(jnp.where(up, BLOCKS * LANES - NEAR, 0))
        far = aligned(jnp.where(up, BLOCKS * LANES - WIDE, NEAR))
        out[0:SLAB, 0:HALF] = src[:, pl.ds(far, HALF)]
        out[SLAB : 2 * SLAB, 0:HALF] = src[:, pl.ds(aligned(far + HALF), HALF)]
        out[0:STENCIL, HALF:TAIL] = weights[:, pl.ds(near, NEAR)]
        out[STENCIL:ROWS, HALF:TAIL] = shifts[:, pl.ds(near, NEAR)]
        out[:, TAIL:] = jnp.zeros((ROWS, LANES), jnp.float32)
        out[0:STENCIL, TAIL : TAIL + HALO] = jnp.where(
            up, offsets[:, BLOCKS - HALO :], offsets[:, :HALO]
        )
    for j in range(BLOCKS):
        cols = slice(j * LANES, (j + 1) * LANES)
        diag[j] = jnp.sum(weights[:, cols], axis=0, keepdims=True) + shifts[:, cols]
    wait_all(copies)

    for b in range(HALO, BLOCKS - HALO):
        x1[b - HALO] = apply(
            lambda c: src[:, column(0, c)],
            b,
            diag[b],
            lambda s: weights[s : s + 1, column(0, b)],
            lambda s: nb[s, b],
        )


def edge_kernel(src, near_0, near_1, weights, diag, inner, nb_in, out, x0, x1, nb, buffer, sems):
    offsets = pltpu.make_async_copy(nb_in, nb, sems.at[PARTS])
    offsets.start()
    for k, near in enumerate((near_0, near_1)):
        base = jnp.where(rightward(k), HALO + BLOCKS, 0)
        for j in range(HALO):
            x0[base + j] = near[:, j * LANES : (j + 1) * LANES]
    for j in range(BLOCKS):
        x0[HALO + j] = src[:, j * LANES : (j + 1) * LANES]
    for r in range(PARTS):
        buffer[r, 0:SLAB, :] = src[:, r * PART : (r + 1) * PART]
    for j in range(HALO, BLOCKS - HALO):
        x1[j] = inner[j - HALO]
        part, place = divmod(j, PART // LANES)
        buffer[part, SLAB:, place * LANES : (place + 1) * LANES] = inner[j - HALO]
    parts = [pltpu.make_async_copy(buffer.at[r], out.at[r], sems.at[r]) for r in range(PARTS)]
    per_part = PART // LANES
    for r in range(HALO // per_part, (BLOCKS - HALO) // per_part):
        parts[r].start()
    offsets.wait()

    for b in (*range(HALO), *range(BLOCKS - HALO, BLOCKS)):
        value = apply(
            lambda c: x0[c],
            b + HALO,
            diag[b],
            lambda s: weights[s : s + 1, column(0, b)],
            lambda s: nb[s, b],
        )
        x1[b] = value
        part, place = divmod(b, per_part)
        buffer[part, SLAB:, place * LANES : (place + 1) * LANES] = value
        if place == per_part - 1:
            parts[part].start()
    wait_all(parts)


def outer_kernel(x0_near, x1_own, far_0, far_1, weights, diag, nb_in, out, x0, x1, nbv, nbs, nb, sems):
    nbv[0] = far_0[:, TAIL:].astype(jnp.int32)
    nbv[1] = far_1[:, TAIL:].astype(jnp.int32)
    copies = start_all(sems, [(nbv.at[k], nbs.at[k]) for k in range(2)] + [(nb_in, nb)])
    for k, far in enumerate((far_0, far_1)):
        base = jnp.where(rightward(k), 3 * HALO + BLOCKS, 0)
        for j in range(HALO):
            half, place = divmod(j, HALO // 2)
            x0[base + j] = far[half * SLAB : (half + 1) * SLAB, place * LANES : (place + 1) * LANES]
    for j in range(EXT1):
        x0[HALO + j] = x0_near[j]
    for j in range(BLOCKS):
        x1[HALO + j] = x1_own[j]
    wait_all(copies)
    for side, ref in ((0, far_0), (1, far_1)):
        base = jnp.where(rightward(side), HALO + BLOCKS, 0)
        for j in range(HALO):
            e = base + j
            cols = slice(HALF + j * LANES, HALF + (j + 1) * LANES)
            x1[e] = apply(
                lambda c: x0[c],
                e + HALO,
                jnp.sum(ref[:, cols], axis=0, keepdims=True),
                lambda s: ref[s : s + 1, cols],
                lambda s: nbs[side, s, j],
            )

    def step(i, _):
        for u in range(UNROLL):
            b = i * UNROLL + u
            value = apply(
                lambda c: x1[c],
                b + HALO,
                diag[b],
                lambda s: weights[s : s + 1, column(0, b)],
                lambda s: nb[s, b],
            )
            place = lax.rem(b, PART // LANES)
            for half in range(SLAB // 8):
                out[lax.div(b, PART // LANES), :, column(half * PART, place)] = value[half * 8 : half * 8 + 8]
        return 0

    lax.fori_loop(0, BLOCKS // UNROLL, step, 0)


def tile(t):
    return slice(8 * (t // 3), 8 * (t // 3) + 8), slice(LANES * (t % 3), LANES * (t % 3) + LANES)


def tiles(r):
    per_half = PART // LANES
    for t in range(SLAB // 8 * per_half):
        half, j = divmod(t, per_half)
        row = r * SLAB + half * 8
        yield t, slice(row, row + 8), slice(j * LANES, (j + 1) * LANES)


RIDE = slice(16, 24), slice(2 * LANES, 3 * LANES)


def sums(pairs, first):
    folded = []
    for a, b in pairs:
        p = a * b
        folded.append(sum(p[:, k * LANES : (k + 1) * LANES] for k in range(PART // LANES)))
    stack = jnp.concatenate(folded, axis=1)
    shape = (8, stack.shape[1])
    which = lax.broadcasted_iota(jnp.int32, shape, 1) // LANES + first
    pick = (which == lax.broadcasted_iota(jnp.int32, shape, 0)).astype(jnp.float32)
    return lax.dot_general(
        pick, stack, (((1,), (1,)), ((), ())), precision=HIGHEST, preferred_element_type=jnp.float32
    )


def gram_kernel(z01, second, to_modes, own, out, modal, image, partial, s):
    for r in range(PARTS):
        rows = slice(r * SLAB, (r + 1) * SLAB)
        s[rows, 0:PART] = z01[r, 0:SLAB, :]
        s[rows, PART : 2 * PART] = z01[r, SLAB:, :]
    m = mm(to_modes[...], s[...])
    row = lax.broadcasted_iota(jnp.int32, (MODES, MODES), 0)
    col = lax.broadcasted_iota(jnp.int32, (MODES, MODES), 1)
    e = jnp.sum(jnp.where(row == col, own[0:1, :], 0.0), axis=1, keepdims=True)
    m0, m1 = m[:, 0:PART], m[:, PART : 2 * PART]
    i0 = m1 + e * m0
    modal[...] = m0
    image[...] = i0
    partial[...] = e * (m1 + i0)
    g = sums(((m0, m0), (m0, i0), (i0, i0)), 0)
    for r in range(PARTS):
        for t, _, _ in tiles(r):
            out[(r, *tile(t))] = second[r, :, t * LANES : (t + 1) * LANES]
        out[(r, *RIDE)] = g


def again_kernel(z2, modal, image, partial, to_modes, out, s):
    for r in range(PARTS):
        for t, rows, cols in tiles(r):
            s[rows, cols] = z2[(r, *tile(t))]
    again = mm(to_modes[...], s[...]) + partial[...]
    m0, i0 = modal[...], image[...]
    g = sum(z2[(r, *RIDE)] for r in range(PARTS)) + sums(((m0, again), (i0, again), (again, again)), 3)
    row = jnp.concatenate([g[k : k + 1, :] for k in range(6)], axis=1)
    out[...] = jnp.broadcast_to(row[None], out.shape)


def finish_kernel(got, z01, to_modes, from_modes, own, out, side, s):
    g = jnp.sum(got[...], axis=0)
    mm_, mi, ii, mj, ij, jj = (g[:, k * LANES : (k + 1) * LANES] for k in range(6))
    e = own[0:1, :]
    scale = mm_ + 1e-06
    upper = 1.5 * jnp.sqrt(ii / scale)
    lower = upper * 0.125
    center = (upper + lower) * 0.5
    half_width = (upper - lower) * 0.5
    sigma = center / half_width
    rho_zero = 1.0 / sigma
    rho_one = 1.0 / (2.0 * sigma - rho_zero)
    over = 1.0 / center
    c2 = 2.0 * rho_one / half_width
    u0 = rho_one * rho_zero * over + c2
    u1 = -c2 * over
    a = -over - u0
    b = -u1
    side[0:1, :] = mm_ + a * (2.0 * mi + a * ii)
    side[1:2, :] = scale
    ours = jnp.broadcast_to(b * (2.0 * (mj + a * ij) + b * jj), (8, LANES))
    for r in range(PARTS):
        s[r * SLAB : (r + 1) * SLAB, :] = z01[r, 0:SLAB, :]
        s[MODES + r * SLAB : MODES + (r + 1) * SLAB, :] = z01[r, SLAB:, :]
    from_m = from_modes[...]
    to_m = to_modes[...]
    mix = jnp.concatenate([mm(from_m * (over + u0 + u1 * e), to_m), mm(from_m * u1, to_m)], axis=1)
    value = mm(mix, s[...])
    for r in range(PARTS):
        for t, rows, cols in tiles(r):
            out[(r, *tile(t))] = value[rows, cols]
        out[(r, *RIDE)] = ours


def unpack_kernel(got, side, place, out, mine):
    for r in range(PARTS):
        for t, rows, cols in tiles(0):
            out[rows, r * PART + cols.start : r * PART + cols.stop] = got[(r, *tile(t))]
    squares = side[0:1, :] + sum(got[r, 16:17, RIDE[1]] for r in range(PARTS))
    norm = jnp.sqrt(jnp.maximum(squares, 0.0) / side[1:2, :])
    here = place[0:1, 0:SLAB]
    picked = norm[:, 0:SLAB]
    for r in range(1, PARTS):
        picked = jnp.where(here == r, norm[:, r * SLAB : (r + 1) * SLAB], picked)
    mine[...] = picked


def call(kernel, out_shape, in_specs, scratch=(), out_specs=None, cost=None):
    if out_specs is None:
        out_specs = (VMEM,) * len(out_shape) if isinstance(out_shape, tuple) else VMEM
    return pl.pallas_call(
        kernel,
        out_shape=out_shape,
        in_specs=in_specs,
        out_specs=out_specs,
        scratch_shapes=scratch,
        cost_estimate=cost,
        compiler_params=pltpu.CompilerParams(vmem_limit_bytes=32 * 1024 * 1024),
    )


def pinned(value):
    return pltpu.with_memory_space_constraint(value, pltpu.HBM)


def on_device(sizes, source, to_modes, from_modes, eigenvalue, shifts, weights, neighbors):
    lat = sizes["y"] * sizes["z"]
    place = jnp.full((8, LANES), lax.axis_index(RAD).astype(jnp.float32))
    shift_row = shifts.reshape(1, -1)
    eig = eigenvalue.reshape(1, -1)
    nears, fars = f32(SLAB, NEAR), f32(ROWS, TAIL + LANES)
    offsets = jax.ShapeDtypeStruct(neighbors.shape, neighbors.dtype)
    near_0, near_1, own, nb, shift_row = call(
        pack_kernel,
        (nears, nears, f32(8, LANES), offsets, f32(1, BLOCKS * LANES)),
        [HBM] * 5,
        [pltpu.VMEM((1, LANES), jnp.float32), pltpu.SemaphoreType.DMA((5,))],
    )(*(pinned(v) for v in (source, weights, shift_row, neighbors, eig)))
    swaps = [
        [(i, (i + turn) % lat) for i, turn in ((i, 1 if i % 2 != k else -1) for i in range(lat))]
        for k in range(2)
    ]
    near_0, near_1 = lax.ppermute(near_0, LAT, swaps[0]), lax.ppermute(near_1, LAT, swaps[1])
    smem_offsets = pltpu.SMEM((STENCIL, BLOCKS), jnp.int32)
    inner, diag, place, far_0, far_1 = call(
        inner_kernel,
        (f32(BLOCKS - 2 * HALO, SLAB, LANES), f32(BLOCKS, 1, LANES), f32(8, LANES), fars, fars),
        [VMEM] * 5,
        [smem_offsets, pltpu.SemaphoreType.DMA((1,))],
        cost=COST_0,
    )(source, weights, shift_row, nb, place)
    far_0, far_1 = lax.ppermute(far_0, LAT, swaps[0]), lax.ppermute(far_1, LAT, swaps[1])
    first, x0, x1 = call(
        edge_kernel,
        (f32(PARTS, 2 * SLAB, PART), f32(EXT1, SLAB, LANES), f32(BLOCKS, SLAB, LANES)),
        [VMEM] * 7,
        [
            smem_offsets,
            pltpu.VMEM((PARTS, 2 * SLAB, PART), jnp.float32),
            pltpu.SemaphoreType.DMA((PARTS + 1,)),
        ],
        out_specs=(HBM, VMEM, VMEM),
        cost=COST_1,
    )(source, near_0, near_1, weights, diag, inner, nb)
    z01 = lax.all_to_all(first, RAD, 0, 0, tiled=True)
    second = call(
        outer_kernel,
        f32(PARTS, 8, FLAT),
        [VMEM] * 7,
        [
            pltpu.VMEM((EXT2, SLAB, LANES), jnp.float32),
            pltpu.VMEM((EXT1, SLAB, LANES), jnp.float32),
            pltpu.VMEM((2, ROWS, LANES), jnp.int32),
            pltpu.SMEM((2, ROWS, LANES), jnp.int32),
            smem_offsets,
            pltpu.SemaphoreType.DMA((3,)),
        ],
        cost=COST_2,
    )(x0, x1, far_0, far_1, weights, diag, nb)
    sent, modal, image, partial = call(
        gram_kernel,
        (f32(PARTS, 24, 3 * LANES),) + (f32(MODES, PART),) * 3,
        [VMEM] * 4,
        [pltpu.VMEM((MODES, 2 * PART), jnp.float32)],
    )(z01, second, to_modes, own)
    z2 = lax.all_to_all(sent, RAD, 0, 0, tiled=True)
    g = call(
        again_kernel,
        f32(lat, 1, 6 * LANES),
        [VMEM] * 5,
        [pltpu.VMEM((MODES, PART), jnp.float32)],
    )(z2, modal, image, partial, to_modes)
    g = lax.all_to_all(g, LAT, 0, 0, tiled=True)
    mixed, side = call(
        finish_kernel,
        (f32(PARTS, 24, 3 * LANES), f32(8, LANES)),
        [VMEM] * 5,
        [pltpu.VMEM((2 * MODES, PART), jnp.float32)],
    )(g, z01, to_modes, from_modes, own)
    got = lax.all_to_all(mixed, RAD, 0, 0, tiled=True)
    smoothed, residual_norm = call(
        unpack_kernel, (f32(SLAB, BLOCKS * LANES), f32(1, SLAB)), [VMEM] * 3
    )(got, side, place)
    return smoothed, residual_norm.reshape(SLAB)


def solution(mesh):
    names = ("y", "z", "x", "core")
    fine = Mesh(np.asarray(mesh.devices).reshape(4, 8, 4, 2), names)
    return jax.shard_map(
        functools.partial(on_device, dict(fine.shape)),
        mesh=fine,
        in_specs=(P(RAD, LAT), P(), P(), P(), P(LAT), P(None, LAT), P(None, LAT)),
        out_specs=(P(RAD, LAT), P(RAD)),
        check_vma=False,
    )
```

```python
import functools

import jax
import jax.numpy as jnp
import numpy as np
from jax import lax
from jax.experimental import pallas as pl
from jax.experimental.pallas import tpu as pltpu
from jax.sharding import Mesh, PartitionSpec as P

LANES = 128
HALO = 8
UNROLL = 8
STENCIL = 31
ROWS = STENCIL + 1
BLOCKS = 32
EXT1 = BLOCKS + 2 * HALO
EXT2 = BLOCKS + 4 * HALO
SLAB = 16
PARTS = 8
PART = BLOCKS * LANES // PARTS
MODES = 128
FLAT = SLAB * PART // 8
WIDE = 2 * HALO * LANES
NEAR = HALO * LANES
HALF = NEAR // 2
TAIL = HALF + NEAR
LAT = ("y", "z")
RAD = ("x", "core")


def work(microseconds):
    return pl.CostEstimate(
        flops=int(microseconds * 1e9), transcendentals=0, bytes_accessed=0
    )


VMEM = pl.BlockSpec(memory_space=pltpu.VMEM)
SMEM = pl.BlockSpec(memory_space=pltpu.SMEM)
HBM = pl.BlockSpec(memory_space=pltpu.HBM)
COST_0 = work(3)
COST_1 = work(3)
COST_2 = work(10)
HIGHEST = lax.Precision.HIGHEST


def f32(*shape):
    return jax.ShapeDtypeStruct(shape, jnp.float32)


def split(a):
    high = a.astype(jnp.bfloat16)
    return high, (a - high.astype(jnp.float32)).astype(jnp.bfloat16)


def mm(a, b):
    (ah, al), (bh, bl) = split(a), split(b)
    dot = functools.partial(jnp.dot, preferred_element_type=jnp.float32)
    return dot(ah, bh) + (dot(ah, bl) + dot(al, bh))


def start_all(sems, pairs):
    copies = [pltpu.make_async_copy(src, dst, sems.at[k]) for k, (src, dst) in enumerate(pairs)]
    for copy in copies:
        copy.start()
    return copies


def wait_all(copies):
    for copy in copies:
        copy.wait()


def odd():
    return lax.rem(lax.axis_index("z"), 2)


def aligned(start):
    return pl.multiple_of(start, LANES)


def rightward(swap):
    return odd() != swap


def pack_kernel(src, weights, shifts, neighbors, eig, near_0, near_1, own, nb, shift_row, eig_in, sems):
    pairs = [(neighbors, nb), (eig, eig_in), (shifts, shift_row)]
    for k, near in enumerate((near_0, near_1)):
        start = aligned(jnp.where(rightward(k), BLOCKS * LANES - NEAR, 0))
        pairs.append((src.at[:, pl.ds(start, NEAR)], near))
    wait_all(start_all(sems, pairs))
    own[...] = jnp.broadcast_to(eig_in[...], own.shape)


def column(start, block):
    return pl.ds(pl.multiple_of(start + block * LANES, LANES), LANES)


def apply(read, centre, d, weight, offset):
    acc = d * read(centre)
    for s in range(STENCIL):
        moved = read(offset(s) + centre)
        if s:
            moved = pltpu.roll(moved, LANES - s, 1)
        acc = acc - weight(s) * moved
    return acc


def inner_kernel(src, weights, shifts, nb_in, place_in, x1, diag, place, nb, sems):
    copies = start_all(sems, [(nb_in, nb)])
    place[...] = place_in[...]
    for j in range(BLOCKS):
        cols = slice(j * LANES, (j + 1) * LANES)
        diag[j] = jnp.sum(weights[:, cols], axis=0, keepdims=True) + shifts[:, cols]
    wait_all(copies)

    for b in range(HALO, BLOCKS - HALO):
        x1[b - HALO] = apply(
            lambda c: src[:, column(0, c)],
            b,
            diag[b],
            lambda s: weights[s : s + 1, column(0, b)],
            lambda s: nb[s, b],
        )


def side(swap):
    return jnp.where(rightward(swap), BLOCKS - HALO, 0)


def extend(x0, src, nears):
    for k, near in nears:
        base = jnp.where(rightward(k), HALO + BLOCKS, 0)
        for j in range(HALO):
            x0[base + j] = near[:, j * LANES : (j + 1) * LANES]
    for j in range(BLOCKS):
        x0[HALO + j] = src[:, j * LANES : (j + 1) * LANES]


def apply_side(swap, x0, diag, weights, nb, put):
    for j in range(HALO):
        b = side(swap) + j
        put(
            j,
            apply(
                lambda c: x0[c],
                b + HALO,
                diag[b],
                lambda s: weights[s : s + 1, column(0, b)],
                lambda s: nb[s, b],
            ),
        )


def early_kernel(src, near_1, weights, shifts, diag, nb_in, done, far_0, far_1, x0, nb, sems):
    copies = start_all(sems, [(nb_in, nb)])
    offsets = nb_in[...].astype(jnp.float32)
    for k, out in enumerate((far_0, far_1)):
        up = rightward(k)
        near = aligned(jnp.where(up, BLOCKS * LANES - NEAR, 0))
        far = aligned(jnp.where(up, BLOCKS * LANES - WIDE, NEAR))
        out[0:SLAB, 0:HALF] = src[:, pl.ds(far, HALF)]
        out[SLAB : 2 * SLAB, 0:HALF] = src[:, pl.ds(aligned(far + HALF), HALF)]
        out[0:STENCIL, HALF:TAIL] = weights[:, pl.ds(near, NEAR)]
        out[STENCIL:ROWS, HALF:TAIL] = shifts[:, pl.ds(near, NEAR)]
        out[:, TAIL:] = jnp.zeros((ROWS, LANES), jnp.float32)
        out[0:STENCIL, TAIL : TAIL + HALO] = jnp.where(
            up, offsets[:, BLOCKS - HALO :], offsets[:, :HALO]
        )
    extend(x0, src, ((1, near_1),))
    wait_all(copies)

    def put(j, value):
        done[j] = value

    apply_side(1, x0, diag, weights, nb, put)


def edge_kernel(src, near_0, near_1, weights, diag, inner, early, nb_in, out, x0, x1, nb, buffer, sems):
    offsets = pltpu.make_async_copy(nb_in, nb, sems.at[PARTS])
    offsets.start()
    extend(x0, src, ((0, near_0), (1, near_1)))
    for r in range(PARTS):
        buffer[r, 0:SLAB, :] = src[:, r * PART : (r + 1) * PART]
    per_part = PART // LANES
    for j in range(HALO, BLOCKS - HALO):
        x1[j] = inner[j - HALO]
        part, place = divmod(j, per_part)
        buffer[part, SLAB:, place * LANES : (place + 1) * LANES] = inner[j - HALO]
    parts = [pltpu.make_async_copy(buffer.at[r], out.at[r], sems.at[r]) for r in range(PARTS)]
    inside = range(HALO // per_part, (BLOCKS - HALO) // per_part)
    for r in inside:
        parts[r].start()

    def put_at(swap):
        def put(j, value):
            x1[side(swap) + j] = value
            part, place = divmod(j, per_part)
            cols = slice(place * LANES, (place + 1) * LANES)
            buffer[lax.div(side(swap), per_part) + part, SLAB:, cols] = value

        return put

    for j in range(HALO):
        put_at(1)(j, early[j])
    offsets.wait()
    apply_side(0, x0, diag, weights, nb, put_at(0))
    for r in range(PARTS):
        if r not in inside:
            parts[r].start()
    wait_all(parts)


def outer_kernel(x0_near, x1_own, far_0, far_1, weights, diag, nb_in, out, x0, x1, nbv, nbs, nb, sems):
    nbv[0] = far_0[:, TAIL:].astype(jnp.int32)
    nbv[1] = far_1[:, TAIL:].astype(jnp.int32)
    copies = start_all(sems, [(nbv.at[k], nbs.at[k]) for k in range(2)] + [(nb_in, nb)])
    for k, far in enumerate((far_0, far_1)):
        base = jnp.where(rightward(k), 3 * HALO + BLOCKS, 0)
        for j in range(HALO):
            half, place = divmod(j, HALO // 2)
            x0[base + j] = far[half * SLAB : (half + 1) * SLAB, place * LANES : (place + 1) * LANES]
    for j in range(EXT1):
        x0[HALO + j] = x0_near[j]
    for j in range(BLOCKS):
        x1[HALO + j] = x1_own[j]
    wait_all(copies)
    for side, ref in ((0, far_0), (1, far_1)):
        base = jnp.where(rightward(side), HALO + BLOCKS, 0)
        for j in range(HALO):
            e = base + j
            cols = slice(HALF + j * LANES, HALF + (j + 1) * LANES)
            x1[e] = apply(
                lambda c: x0[c],
                e + HALO,
                jnp.sum(ref[:, cols], axis=0, keepdims=True),
                lambda s: ref[s : s + 1, cols],
                lambda s: nbs[side, s, j],
            )

    def step(i, _):
        for u in range(UNROLL):
            b = i * UNROLL + u
            value = apply(
                lambda c: x1[c],
                b + HALO,
                diag[b],
                lambda s: weights[s : s + 1, column(0, b)],
                lambda s: nb[s, b],
            )
            place = lax.rem(b, PART // LANES)
            for half in range(SLAB // 8):
                out[lax.div(b, PART // LANES), :, column(half * PART, place)] = value[half * 8 : half * 8 + 8]
        return 0

    lax.fori_loop(0, BLOCKS // UNROLL, step, 0)


def tile(t):
    return slice(8 * (t // 3), 8 * (t // 3) + 8), slice(LANES * (t % 3), LANES * (t % 3) + LANES)


def tiles(r):
    per_half = PART // LANES
    for t in range(SLAB // 8 * per_half):
        half, j = divmod(t, per_half)
        row = r * SLAB + half * 8
        yield t, slice(row, row + 8), slice(j * LANES, (j + 1) * LANES)


RIDE = slice(16, 24), slice(2 * LANES, 3 * LANES)


def sums(pairs, first):
    folded = []
    for a, b in pairs:
        p = a * b
        folded.append(sum(p[:, k * LANES : (k + 1) * LANES] for k in range(PART // LANES)))
    stack = jnp.concatenate(folded, axis=1)
    shape = (8, stack.shape[1])
    which = lax.broadcasted_iota(jnp.int32, shape, 1) // LANES + first
    pick = (which == lax.broadcasted_iota(jnp.int32, shape, 0)).astype(jnp.float32)
    return lax.dot_general(
        pick, stack, (((1,), (1,)), ((), ())), precision=HIGHEST, preferred_element_type=jnp.float32
    )


def gram_kernel(z01, second, to_modes, own, out, modal, image, partial, s):
    for r in range(PARTS):
        rows = slice(r * SLAB, (r + 1) * SLAB)
        s[rows, 0:PART] = z01[r, 0:SLAB, :]
        s[rows, PART : 2 * PART] = z01[r, SLAB:, :]
    m = mm(to_modes[...], s[...])
    row = lax.broadcasted_iota(jnp.int32, (MODES, MODES), 0)
    col = lax.broadcasted_iota(jnp.int32, (MODES, MODES), 1)
    e = jnp.sum(jnp.where(row == col, own[0:1, :], 0.0), axis=1, keepdims=True)
    m0, m1 = m[:, 0:PART], m[:, PART : 2 * PART]
    i0 = m1 + e * m0
    modal[...] = m0
    image[...] = i0
    partial[...] = e * (m1 + i0)
    g = sums(((m0, m0), (m0, i0), (i0, i0)), 0)
    for r in range(PARTS):
        for t, _, _ in tiles(r):
            out[(r, *tile(t))] = second[r, :, t * LANES : (t + 1) * LANES]
        out[(r, *RIDE)] = g


def again_kernel(z2, modal, image, partial, to_modes, out, s):
    for r in range(PARTS):
        for t, rows, cols in tiles(r):
            s[rows, cols] = z2[(r, *tile(t))]
    again = mm(to_modes[...], s[...]) + partial[...]
    m0, i0 = modal[...], image[...]
    g = sum(z2[(r, *RIDE)] for r in range(PARTS)) + sums(((m0, again), (i0, again), (again, again)), 3)
    row = jnp.concatenate([g[k : k + 1, :] for k in range(6)], axis=1)
    out[...] = jnp.broadcast_to(row[None], out.shape)


def finish_kernel(got, z01, to_modes, from_modes, own, out, side, s):
    g = jnp.sum(got[...], axis=0)
    mm_, mi, ii, mj, ij, jj = (g[:, k * LANES : (k + 1) * LANES] for k in range(6))
    e = own[0:1, :]
    scale = mm_ + 1e-06
    upper = 1.5 * jnp.sqrt(ii / scale)
    lower = upper * 0.125
    center = (upper + lower) * 0.5
    half_width = (upper - lower) * 0.5
    sigma = center / half_width
    rho_zero = 1.0 / sigma
    rho_one = 1.0 / (2.0 * sigma - rho_zero)
    over = 1.0 / center
    c2 = 2.0 * rho_one / half_width
    u0 = rho_one * rho_zero * over + c2
    u1 = -c2 * over
    a = -over - u0
    b = -u1
    side[0:1, :] = mm_ + a * (2.0 * mi + a * ii)
    side[1:2, :] = scale
    ours = jnp.broadcast_to(b * (2.0 * (mj + a * ij) + b * jj), (8, LANES))
    for r in range(PARTS):
        s[r * SLAB : (r + 1) * SLAB, :] = z01[r, 0:SLAB, :]
        s[MODES + r * SLAB : MODES + (r + 1) * SLAB, :] = z01[r, SLAB:, :]
    from_m = from_modes[...]
    to_m = to_modes[...]
    mix = jnp.concatenate([mm(from_m * (over + u0 + u1 * e), to_m), mm(from_m * u1, to_m)], axis=1)
    value = mm(mix, s[...])
    for r in range(PARTS):
        for t, rows, cols in tiles(r):
            out[(r, *tile(t))] = value[rows, cols]
        out[(r, *RIDE)] = ours


def unpack_kernel(got, side, place, out, mine):
    for r in range(PARTS):
        for t, rows, cols in tiles(0):
            out[rows, r * PART + cols.start : r * PART + cols.stop] = got[(r, *tile(t))]
    squares = side[0:1, :] + sum(got[r, 16:17, RIDE[1]] for r in range(PARTS))
    norm = jnp.sqrt(jnp.maximum(squares, 0.0) / side[1:2, :])
    here = place[0:1, 0:SLAB]
    picked = norm[:, 0:SLAB]
    for r in range(1, PARTS):
        picked = jnp.where(here == r, norm[:, r * SLAB : (r + 1) * SLAB], picked)
    mine[...] = picked


def call(kernel, out_shape, in_specs, scratch=(), out_specs=None, cost=None):
    if out_specs is None:
        out_specs = (VMEM,) * len(out_shape) if isinstance(out_shape, tuple) else VMEM
    return pl.pallas_call(
        kernel,
        out_shape=out_shape,
        in_specs=in_specs,
        out_specs=out_specs,
        scratch_shapes=scratch,
        cost_estimate=cost,
        compiler_params=pltpu.CompilerParams(vmem_limit_bytes=32 * 1024 * 1024),
    )


def pinned(value):
    return pltpu.with_memory_space_constraint(value, pltpu.HBM)


def on_device(sizes, source, to_modes, from_modes, eigenvalue, shifts, weights, neighbors):
    lat = sizes["y"] * sizes["z"]
    place = jnp.full((8, LANES), lax.axis_index(RAD).astype(jnp.float32))
    shift_row = shifts.reshape(1, -1)
    eig = eigenvalue.reshape(1, -1)
    nears, fars = f32(SLAB, NEAR), f32(ROWS, TAIL + LANES)
    offsets = jax.ShapeDtypeStruct(neighbors.shape, neighbors.dtype)
    near_0, near_1, own, nb, shift_row = call(
        pack_kernel,
        (nears, nears, f32(8, LANES), offsets, f32(1, BLOCKS * LANES)),
        [HBM] * 5,
        [pltpu.VMEM((1, LANES), jnp.float32), pltpu.SemaphoreType.DMA((5,))],
    )(*(pinned(v) for v in (source, weights, shift_row, neighbors, eig)))
    swaps = [
        [(i, (i + turn) % lat) for i, turn in ((i, 1 if i % 2 != k else -1) for i in range(lat))]
        for k in range(2)
    ]
    near_0, near_1 = lax.ppermute(near_0, LAT, swaps[0]), lax.ppermute(near_1, LAT, swaps[1])
    smem_offsets = pltpu.SMEM((STENCIL, BLOCKS), jnp.int32)
    inner, diag, place = call(
        inner_kernel,
        (f32(BLOCKS - 2 * HALO, SLAB, LANES), f32(BLOCKS, 1, LANES), f32(8, LANES)),
        [VMEM] * 5,
        [smem_offsets, pltpu.SemaphoreType.DMA((1,))],
        cost=COST_0,
    )(source, weights, shift_row, nb, place)
    early, far_0, far_1 = call(
        early_kernel,
        (f32(HALO, SLAB, LANES), fars, fars),
        [VMEM] * 6,
        [
            pltpu.VMEM((EXT1, SLAB, LANES), jnp.float32),
            smem_offsets,
            pltpu.SemaphoreType.DMA((1,)),
        ],
        cost=COST_0,
    )(source, near_1, weights, shift_row, diag, nb)
    far_0, far_1 = lax.ppermute(far_0, LAT, swaps[0]), lax.ppermute(far_1, LAT, swaps[1])
    first, x0, x1 = call(
        edge_kernel,
        (f32(PARTS, 2 * SLAB, PART), f32(EXT1, SLAB, LANES), f32(BLOCKS, SLAB, LANES)),
        [VMEM] * 8,
        [
            smem_offsets,
            pltpu.VMEM((PARTS, 2 * SLAB, PART), jnp.float32),
            pltpu.SemaphoreType.DMA((PARTS + 1,)),
        ],
        out_specs=(HBM, VMEM, VMEM),
        cost=COST_1,
    )(source, near_0, near_1, weights, diag, inner, early, nb)
    z01 = lax.all_to_all(first, RAD, 0, 0, tiled=True)
    second = call(
        outer_kernel,
        f32(PARTS, 8, FLAT),
        [VMEM] * 7,
        [
            pltpu.VMEM((EXT2, SLAB, LANES), jnp.float32),
            pltpu.VMEM((EXT1, SLAB, LANES), jnp.float32),
            pltpu.VMEM((2, ROWS, LANES), jnp.int32),
            pltpu.SMEM((2, ROWS, LANES), jnp.int32),
            smem_offsets,
            pltpu.SemaphoreType.DMA((3,)),
        ],
        cost=COST_2,
    )(x0, x1, far_0, far_1, weights, diag, nb)
    sent, modal, image, partial = call(
        gram_kernel,
        (f32(PARTS, 24, 3 * LANES),) + (f32(MODES, PART),) * 3,
        [VMEM] * 4,
        [pltpu.VMEM((MODES, 2 * PART), jnp.float32)],
    )(z01, second, to_modes, own)
    z2 = lax.all_to_all(sent, RAD, 0, 0, tiled=True)
    g = call(
        again_kernel,
        f32(lat, 1, 6 * LANES),
        [VMEM] * 5,
        [pltpu.VMEM((MODES, PART), jnp.float32)],
    )(z2, modal, image, partial, to_modes)
    g = lax.all_to_all(g, LAT, 0, 0, tiled=True)
    mixed, side = call(
        finish_kernel,
        (f32(PARTS, 24, 3 * LANES), f32(8, LANES)),
        [VMEM] * 5,
        [pltpu.VMEM((2 * MODES, PART), jnp.float32)],
    )(g, z01, to_modes, from_modes, own)
    got = lax.all_to_all(mixed, RAD, 0, 0, tiled=True)
    smoothed, residual_norm = call(
        unpack_kernel, (f32(SLAB, BLOCKS * LANES), f32(1, SLAB)), [VMEM] * 3
    )(got, side, place)
    return smoothed, residual_norm.reshape(SLAB)


def solution(mesh):
    names = ("y", "z", "x", "core")
    fine = Mesh(np.asarray(mesh.devices).reshape(4, 8, 4, 2), names)
    return jax.shard_map(
        functools.partial(on_device, dict(fine.shape)),
        mesh=fine,
        in_specs=(P(RAD, LAT), P(), P(), P(), P(LAT), P(None, LAT), P(None, LAT)),
        out_specs=(P(RAD, LAT), P(RAD)),
        check_vma=False,
    )
```

```python
import functools

import jax
import jax.numpy as jnp
import numpy as np
from jax import lax
from jax.experimental import pallas as pl
from jax.experimental.pallas import tpu as pltpu
from jax.sharding import Mesh, PartitionSpec as P

LANES = 128
HALO = 8
UNROLL = 8
STENCIL = 31
ROWS = STENCIL + 1
BLOCKS = 32
EXT1 = BLOCKS + 2 * HALO
EXT2 = BLOCKS + 4 * HALO
SLAB = 16
PARTS = 8
PART = BLOCKS * LANES // PARTS
MODES = 128
FLAT = SLAB * PART // 8
WIDE = 2 * HALO * LANES
NEAR = HALO * LANES
HALF = NEAR // 2
TAIL = HALF + NEAR
LAT = ("y", "z")
RAD = ("x", "core")


def work(microseconds):
    return pl.CostEstimate(
        flops=int(microseconds * 1e9), transcendentals=0, bytes_accessed=0
    )


VMEM = pl.BlockSpec(memory_space=pltpu.VMEM)
SMEM = pl.BlockSpec(memory_space=pltpu.SMEM)
HBM = pl.BlockSpec(memory_space=pltpu.HBM)
COST_0 = work(3)
COST_1 = work(3)
COST_2 = work(10)
HIGHEST = lax.Precision.HIGHEST


def f32(*shape):
    return jax.ShapeDtypeStruct(shape, jnp.float32)


def split(a):
    high = a.astype(jnp.bfloat16)
    return high, (a - high.astype(jnp.float32)).astype(jnp.bfloat16)


def mm(a, b):
    (ah, al), (bh, bl) = split(a), split(b)
    dot = functools.partial(jnp.dot, preferred_element_type=jnp.float32)
    return dot(ah, bh) + (dot(ah, bl) + dot(al, bh))


def start_all(sems, pairs):
    copies = [pltpu.make_async_copy(src, dst, sems.at[k]) for k, (src, dst) in enumerate(pairs)]
    for copy in copies:
        copy.start()
    return copies


def wait_all(copies):
    for copy in copies:
        copy.wait()


def odd():
    return lax.rem(lax.axis_index("z"), 2)


def aligned(start):
    return pl.multiple_of(start, LANES)


def rightward(swap):
    return odd() != swap


def pack_kernel(src, weights, shifts, neighbors, eig, near_0, near_1, own, nb, shift_row, eig_in, sems):
    pairs = [(neighbors, nb), (eig, eig_in), (shifts, shift_row)]
    for k, near in enumerate((near_0, near_1)):
        start = aligned(jnp.where(rightward(k), BLOCKS * LANES - NEAR, 0))
        pairs.append((src.at[:, pl.ds(start, NEAR)], near))
    wait_all(start_all(sems, pairs))
    own[...] = jnp.broadcast_to(eig_in[...], own.shape)


def column(start, block):
    return pl.ds(pl.multiple_of(start + block * LANES, LANES), LANES)


def apply(read, centre, d, weight, offset):
    acc = d * read(centre)
    for s in range(STENCIL):
        moved = read(offset(s) + centre)
        if s:
            moved = pltpu.roll(moved, LANES - s, 1)
        acc = acc - weight(s) * moved
    return acc


def inner_kernel(src, weights, shifts, nb_in, place_in, x1, diag, place, far_0, far_1, nb, sems):
    copies = start_all(sems, [(nb_in, nb)])
    place[...] = place_in[...]
    offsets = nb_in[...].astype(jnp.float32)
    for k, out in enumerate((far_0, far_1)):
        up = rightward(k)
        near = aligned(jnp.where(up, BLOCKS * LANES - NEAR, 0))
        far = aligned(jnp.where(up, BLOCKS * LANES - WIDE, NEAR))
        out[0:SLAB, 0:HALF] = src[:, pl.ds(far, HALF)]
        out[SLAB : 2 * SLAB, 0:HALF] = src[:, pl.ds(aligned(far + HALF), HALF)]
        out[0:STENCIL, HALF:TAIL] = weights[:, pl.ds(near, NEAR)]
        out[STENCIL:ROWS, HALF:TAIL] = shifts[:, pl.ds(near, NEAR)]
        out[:, TAIL:] = jnp.zeros((ROWS, LANES), jnp.float32)
        out[0:STENCIL, TAIL : TAIL + HALO] = jnp.where(
            up, offsets[:, BLOCKS - HALO :], offsets[:, :HALO]
        )
    for j in range(BLOCKS):
        cols = slice(j * LANES, (j + 1) * LANES)
        diag[j] = jnp.sum(weights[:, cols], axis=0, keepdims=True) + shifts[:, cols]
    wait_all(copies)

    for b in range(HALO, BLOCKS - HALO):
        x1[b - HALO] = apply(
            lambda c: src[:, column(0, c)],
            b,
            diag[b],
            lambda s: weights[s : s + 1, column(0, b)],
            lambda s: nb[s, b],
        )


def edge_kernel(src, near_0, near_1, weights, diag, inner, nb_in, out, x0, x1, nb, buffer, sems):
    offsets = pltpu.make_async_copy(nb_in, nb, sems.at[PARTS])
    offsets.start()
    for k, near in enumerate((near_0, near_1)):
        base = jnp.where(rightward(k), HALO + BLOCKS, 0)
        for j in range(HALO):
            x0[base + j] = near[:, j * LANES : (j + 1) * LANES]
    for j in range(BLOCKS):
        x0[HALO + j] = src[:, j * LANES : (j + 1) * LANES]
    for r in range(PARTS):
        buffer[r, 0:SLAB, :] = src[:, r * PART : (r + 1) * PART]
    for j in range(HALO, BLOCKS - HALO):
        x1[j] = inner[j - HALO]
        part, place = divmod(j, PART // LANES)
        buffer[part, SLAB:, place * LANES : (place + 1) * LANES] = inner[j - HALO]
    parts = [pltpu.make_async_copy(buffer.at[r], out.at[r], sems.at[r]) for r in range(PARTS)]
    per_part = PART // LANES
    for r in range(HALO // per_part, (BLOCKS - HALO) // per_part):
        parts[r].start()
    offsets.wait()

    for b in (*range(HALO), *range(BLOCKS - HALO, BLOCKS)):
        value = apply(
            lambda c: x0[c],
            b + HALO,
            diag[b],
            lambda s: weights[s : s + 1, column(0, b)],
            lambda s: nb[s, b],
        )
        x1[b] = value
        part, place = divmod(b, per_part)
        buffer[part, SLAB:, place * LANES : (place + 1) * LANES] = value
        if place == per_part - 1:
            parts[part].start()
    wait_all(parts)


def outer_kernel(x0_near, x1_own, far_0, far_1, weights, diag, nb_in, out, x0, x1, nbv, nbs, nb, sems):
    nbv[0] = far_0[:, TAIL:].astype(jnp.int32)
    nbv[1] = far_1[:, TAIL:].astype(jnp.int32)
    copies = start_all(sems, [(nbv.at[k], nbs.at[k]) for k in range(2)] + [(nb_in, nb)])
    for k, far in enumerate((far_0, far_1)):
        base = jnp.where(rightward(k), 3 * HALO + BLOCKS, 0)
        for j in range(HALO):
            half, place = divmod(j, HALO // 2)
            x0[base + j] = far[half * SLAB : (half + 1) * SLAB, place * LANES : (place + 1) * LANES]
    for j in range(EXT1):
        x0[HALO + j] = x0_near[j]
    for j in range(BLOCKS):
        x1[HALO + j] = x1_own[j]
    wait_all(copies)
    for side, ref in ((0, far_0), (1, far_1)):
        base = jnp.where(rightward(side), HALO + BLOCKS, 0)
        for j in range(HALO):
            e = base + j
            cols = slice(HALF + j * LANES, HALF + (j + 1) * LANES)
            x1[e] = apply(
                lambda c: x0[c],
                e + HALO,
                jnp.sum(ref[:, cols], axis=0, keepdims=True),
                lambda s: ref[s : s + 1, cols],
                lambda s: nbs[side, s, j],
            )

    def step(i, _):
        for u in range(UNROLL):
            b = i * UNROLL + u
            value = apply(
                lambda c: x1[c],
                b + HALO,
                diag[b],
                lambda s: weights[s : s + 1, column(0, b)],
                lambda s: nb[s, b],
            )
            place = lax.rem(b, PART // LANES)
            for half in range(SLAB // 8):
                out[lax.div(b, PART // LANES), :, column(half * PART, place)] = value[half * 8 : half * 8 + 8]
        return 0

    lax.fori_loop(0, BLOCKS // UNROLL, step, 0)


def tile(t):
    return slice(8 * (t // 3), 8 * (t // 3) + 8), slice(LANES * (t % 3), LANES * (t % 3) + LANES)


def tiles(r):
    per_half = PART // LANES
    for t in range(SLAB // 8 * per_half):
        half, j = divmod(t, per_half)
        row = r * SLAB + half * 8
        yield t, slice(row, row + 8), slice(j * LANES, (j + 1) * LANES)


RIDE = slice(16, 24), slice(2 * LANES, 3 * LANES)


def sums(pairs, first):
    folded = []
    for a, b in pairs:
        p = a * b
        folded.append(sum(p[:, k * LANES : (k + 1) * LANES] for k in range(PART // LANES)))
    stack = jnp.concatenate(folded, axis=1)
    shape = (8, stack.shape[1])
    which = lax.broadcasted_iota(jnp.int32, shape, 1) // LANES + first
    pick = (which == lax.broadcasted_iota(jnp.int32, shape, 0)).astype(jnp.bfloat16)
    over_lanes = functools.partial(
        lax.dot_general,
        dimension_numbers=(((1,), (1,)), ((), ())),
        preferred_element_type=jnp.float32,
    )
    high, low = split(stack)
    return over_lanes(pick, high) + over_lanes(pick, low)


def gram_kernel(z01, second, to_modes, own, out, modal, image, partial, s):
    for r in range(PARTS):
        rows = slice(r * SLAB, (r + 1) * SLAB)
        s[rows, 0:PART] = z01[r, 0:SLAB, :]
        s[rows, PART : 2 * PART] = z01[r, SLAB:, :]
    m = mm(to_modes[...], s[...])
    row = lax.broadcasted_iota(jnp.int32, (MODES, MODES), 0)
    col = lax.broadcasted_iota(jnp.int32, (MODES, MODES), 1)
    e = jnp.sum(jnp.where(row == col, own[0:1, :], 0.0), axis=1, keepdims=True)
    m0, m1 = m[:, 0:PART], m[:, PART : 2 * PART]
    i0 = m1 + e * m0
    modal[...] = m0
    image[...] = i0
    partial[...] = e * (m1 + i0)
    g = sums(((m0, m0), (m0, i0), (i0, i0)), 0)
    for r in range(PARTS):
        for t, _, _ in tiles(r):
            out[(r, *tile(t))] = second[r, :, t * LANES : (t + 1) * LANES]
        out[(r, *RIDE)] = g


def again_kernel(z2, modal, image, partial, to_modes, out, s):
    for r in range(PARTS):
        for t, rows, cols in tiles(r):
            s[rows, cols] = z2[(r, *tile(t))]
    again = mm(to_modes[...], s[...]) + partial[...]
    m0, i0 = modal[...], image[...]
    g = sum(z2[(r, *RIDE)] for r in range(PARTS)) + sums(((m0, again), (i0, again), (again, again)), 3)
    row = jnp.concatenate([g[k : k + 1, :] for k in range(6)], axis=1)
    out[...] = jnp.broadcast_to(row[None], out.shape)


def finish_kernel(got, z01, to_modes, from_modes, own, out, side, s):
    g = jnp.sum(got[...], axis=0)
    mm_, mi, ii, mj, ij, jj = (g[:, k * LANES : (k + 1) * LANES] for k in range(6))
    e = own[0:1, :]
    scale = mm_ + 1e-06
    upper = 1.5 * jnp.sqrt(ii / scale)
    lower = upper * 0.125
    center = (upper + lower) * 0.5
    half_width = (upper - lower) * 0.5
    sigma = center / half_width
    rho_zero = 1.0 / sigma
    rho_one = 1.0 / (2.0 * sigma - rho_zero)
    over = 1.0 / center
    c2 = 2.0 * rho_one / half_width
    u0 = rho_one * rho_zero * over + c2
    u1 = -c2 * over
    a = -over - u0
    b = -u1
    side[0:1, :] = mm_ + a * (2.0 * mi + a * ii)
    side[1:2, :] = scale
    ours = jnp.broadcast_to(b * (2.0 * (mj + a * ij) + b * jj), (8, LANES))
    for r in range(PARTS):
        s[r * SLAB : (r + 1) * SLAB, :] = z01[r, 0:SLAB, :]
        s[MODES + r * SLAB : MODES + (r + 1) * SLAB, :] = z01[r, SLAB:, :]
    from_m = from_modes[...]
    to_m = to_modes[...]
    mix = jnp.concatenate([mm(from_m * (over + u0 + u1 * e), to_m), mm(from_m * u1, to_m)], axis=1)
    value = mm(mix, s[...])
    for r in range(PARTS):
        for t, rows, cols in tiles(r):
            out[(r, *tile(t))] = value[rows, cols]
        out[(r, *RIDE)] = ours


def unpack_kernel(got, side, place, out, mine, columns, sems):
    copies = []
    for r in range(PARTS):
        for t, rows, cols in tiles(0):
            columns[rows, r * PART + cols.start : r * PART + cols.stop] = got[(r, *tile(t))]
        if r % 2:
            done = pl.ds((r - 1) * PART, 2 * PART)
            copies.append(
                pltpu.make_async_copy(columns.at[:, done], out.at[:, done], sems.at[r // 2])
            )
            copies[-1].start()
    squares = side[0:1, :] + sum(got[r, 16:17, RIDE[1]] for r in range(PARTS))
    norm = jnp.sqrt(jnp.maximum(squares, 0.0) / side[1:2, :])
    here = place[0:1, 0:SLAB]
    picked = norm[:, 0:SLAB]
    for r in range(1, PARTS):
        picked = jnp.where(here == r, norm[:, r * SLAB : (r + 1) * SLAB], picked)
    mine[...] = picked
    wait_all(copies)


def call(kernel, out_shape, in_specs, scratch=(), out_specs=None, cost=None):
    if out_specs is None:
        out_specs = (VMEM,) * len(out_shape) if isinstance(out_shape, tuple) else VMEM
    return pl.pallas_call(
        kernel,
        out_shape=out_shape,
        in_specs=in_specs,
        out_specs=out_specs,
        scratch_shapes=scratch,
        cost_estimate=cost,
        compiler_params=pltpu.CompilerParams(vmem_limit_bytes=32 * 1024 * 1024),
    )


def pinned(value):
    return pltpu.with_memory_space_constraint(value, pltpu.HBM)


def on_device(sizes, source, to_modes, from_modes, eigenvalue, shifts, weights, neighbors):
    lat = sizes["y"] * sizes["z"]
    place = jnp.full((8, LANES), lax.axis_index(RAD).astype(jnp.float32))
    shift_row = shifts.reshape(1, -1)
    eig = eigenvalue.reshape(1, -1)
    nears, fars = f32(SLAB, NEAR), f32(ROWS, TAIL + LANES)
    offsets = jax.ShapeDtypeStruct(neighbors.shape, neighbors.dtype)
    near_0, near_1, own, nb, shift_row = call(
        pack_kernel,
        (nears, nears, f32(8, LANES), offsets, f32(1, BLOCKS * LANES)),
        [HBM] * 5,
        [pltpu.VMEM((1, LANES), jnp.float32), pltpu.SemaphoreType.DMA((5,))],
    )(*(pinned(v) for v in (source, weights, shift_row, neighbors, eig)))
    swaps = [
        [(i, (i + turn) % lat) for i, turn in ((i, 1 if i % 2 != k else -1) for i in range(lat))]
        for k in range(2)
    ]
    near_0, near_1 = lax.ppermute(near_0, LAT, swaps[0]), lax.ppermute(near_1, LAT, swaps[1])
    smem_offsets = pltpu.SMEM((STENCIL, BLOCKS), jnp.int32)
    inner, diag, place, far_0, far_1 = call(
        inner_kernel,
        (f32(BLOCKS - 2 * HALO, SLAB, LANES), f32(BLOCKS, 1, LANES), f32(8, LANES), fars, fars),
        [VMEM] * 5,
        [smem_offsets, pltpu.SemaphoreType.DMA((1,))],
        cost=COST_0,
    )(source, weights, shift_row, nb, place)
    far_0, far_1 = lax.ppermute(far_0, LAT, swaps[0]), lax.ppermute(far_1, LAT, swaps[1])
    first, x0, x1 = call(
        edge_kernel,
        (f32(PARTS, 2 * SLAB, PART), f32(EXT1, SLAB, LANES), f32(BLOCKS, SLAB, LANES)),
        [VMEM] * 7,
        [
            smem_offsets,
            pltpu.VMEM((PARTS, 2 * SLAB, PART), jnp.float32),
            pltpu.SemaphoreType.DMA((PARTS + 1,)),
        ],
        out_specs=(HBM, VMEM, VMEM),
        cost=COST_1,
    )(source, near_0, near_1, weights, diag, inner, nb)
    z01 = lax.all_to_all(first, RAD, 0, 0, tiled=True)
    second = call(
        outer_kernel,
        f32(PARTS, 8, FLAT),
        [VMEM] * 7,
        [
            pltpu.VMEM((EXT2, SLAB, LANES), jnp.float32),
            pltpu.VMEM((EXT1, SLAB, LANES), jnp.float32),
            pltpu.VMEM((2, ROWS, LANES), jnp.int32),
            pltpu.SMEM((2, ROWS, LANES), jnp.int32),
            smem_offsets,
            pltpu.SemaphoreType.DMA((3,)),
        ],
        cost=COST_2,
    )(x0, x1, far_0, far_1, weights, diag, nb)
    sent, modal, image, partial = call(
        gram_kernel,
        (f32(PARTS, 24, 3 * LANES),) + (f32(MODES, PART),) * 3,
        [VMEM] * 4,
        [pltpu.VMEM((MODES, 2 * PART), jnp.float32)],
    )(z01, second, to_modes, own)
    z2 = lax.all_to_all(sent, RAD, 0, 0, tiled=True)
    g = call(
        again_kernel,
        f32(lat, 1, 6 * LANES),
        [VMEM] * 5,
        [pltpu.VMEM((MODES, PART), jnp.float32)],
    )(z2, modal, image, partial, to_modes)
    g = lax.all_to_all(g, LAT, 0, 0, tiled=True)
    mixed, side = call(
        finish_kernel,
        (f32(PARTS, 24, 3 * LANES), f32(8, LANES)),
        [VMEM] * 5,
        [pltpu.VMEM((2 * MODES, PART), jnp.float32)],
    )(g, z01, to_modes, from_modes, own)
    got = lax.all_to_all(mixed, RAD, 0, 0, tiled=True)
    smoothed, residual_norm = call(
        unpack_kernel,
        (f32(SLAB, BLOCKS * LANES), f32(1, SLAB)),
        [VMEM] * 3,
        [
            pltpu.VMEM((SLAB, BLOCKS * LANES), jnp.float32),
            pltpu.SemaphoreType.DMA((PARTS // 2,)),
        ],
        out_specs=(HBM, VMEM),
    )(got, side, place)
    return smoothed, residual_norm.reshape(SLAB)


def solution(mesh):
    names = ("y", "z", "x", "core")
    fine = Mesh(np.asarray(mesh.devices).reshape(4, 8, 4, 2), names)
    return jax.shard_map(
        functools.partial(on_device, dict(fine.shape)),
        mesh=fine,
        in_specs=(P(RAD, LAT), P(), P(), P(), P(LAT), P(None, LAT), P(None, LAT)),
        out_specs=(P(RAD, LAT), P(RAD)),
        check_vma=False,
    )
```

```python
import functools

import jax
import jax.numpy as jnp
import numpy as np
from jax import lax
from jax.experimental import pallas as pl
from jax.experimental.pallas import tpu as pltpu
from jax.sharding import Mesh, PartitionSpec as P

LANES = 128
HALO = 8
UNROLL = 8
STENCIL = 31
ROWS = STENCIL + 1
BLOCKS = 32
EXT1 = BLOCKS + 2 * HALO
EXT2 = BLOCKS + 4 * HALO
SLAB = 16
PARTS = 8
PART = BLOCKS * LANES // PARTS
MODES = 128
FLAT = SLAB * PART // 8
WIDE = 2 * HALO * LANES
NEAR = HALO * LANES
HALF = NEAR // 2
TAIL = HALF + NEAR
LAT = ("y", "z")
RAD = ("x", "core")


def work(microseconds):
    return pl.CostEstimate(
        flops=int(microseconds * 1e9), transcendentals=0, bytes_accessed=0
    )


VMEM = pl.BlockSpec(memory_space=pltpu.VMEM)
SMEM = pl.BlockSpec(memory_space=pltpu.SMEM)
HBM = pl.BlockSpec(memory_space=pltpu.HBM)
COST_0 = work(3)
COST_1 = work(3)
COST_2 = work(10)
HIGHEST = lax.Precision.HIGHEST


def f32(*shape):
    return jax.ShapeDtypeStruct(shape, jnp.float32)


def split(a):
    high = a.astype(jnp.bfloat16)
    return high, (a - high.astype(jnp.float32)).astype(jnp.bfloat16)


def mm(a, b):
    (ah, al), (bh, bl) = split(a), split(b)
    dot = functools.partial(jnp.dot, preferred_element_type=jnp.float32)
    return dot(ah, bh) + (dot(ah, bl) + dot(al, bh))


def start_all(sems, pairs):
    copies = [pltpu.make_async_copy(src, dst, sems.at[k]) for k, (src, dst) in enumerate(pairs)]
    for copy in copies:
        copy.start()
    return copies


def wait_all(copies):
    for copy in copies:
        copy.wait()


def odd():
    return lax.rem(lax.axis_index("z"), 2)


def aligned(start):
    return pl.multiple_of(start, LANES)


def rightward(swap):
    return odd() != swap


def pack_kernel(src, weights, shifts, neighbors, eig, near_0, near_1, own, nb, shift_row, eig_in, sems):
    pairs = [(neighbors, nb), (eig, eig_in), (shifts, shift_row)]
    for k, near in enumerate((near_0, near_1)):
        start = aligned(jnp.where(rightward(k), BLOCKS * LANES - NEAR, 0))
        pairs.append((src.at[:, pl.ds(start, NEAR)], near))
    wait_all(start_all(sems, pairs))
    own[...] = jnp.broadcast_to(eig_in[...], own.shape)


def column(start, block):
    return pl.ds(pl.multiple_of(start + block * LANES, LANES), LANES)


def apply(read, centre, d, weight, offset):
    acc = d * read(centre)
    for s in range(STENCIL):
        moved = read(offset(s) + centre)
        if s:
            moved = pltpu.roll(moved, LANES - s, 1)
        acc = acc - weight(s) * moved
    return acc


def inner_kernel(src, weights, shifts, nb_in, place_in, x1, diag, place, far_0, far_1, nb, sems):
    copies = start_all(sems, [(nb_in, nb)])
    place[...] = place_in[...]
    offsets = nb_in[...].astype(jnp.float32)
    for k, out in enumerate((far_0, far_1)):
        up = rightward(k)
        near = aligned(jnp.where(up, BLOCKS * LANES - NEAR, 0))
        far = aligned(jnp.where(up, BLOCKS * LANES - WIDE, NEAR))
        out[0:SLAB, 0:HALF] = src[:, pl.ds(far, HALF)]
        out[SLAB : 2 * SLAB, 0:HALF] = src[:, pl.ds(aligned(far + HALF), HALF)]
        out[0:STENCIL, HALF:TAIL] = weights[:, pl.ds(near, NEAR)]
        out[STENCIL:ROWS, HALF:TAIL] = shifts[:, pl.ds(near, NEAR)]
        out[:, TAIL:] = jnp.zeros((ROWS, LANES), jnp.float32)
        out[0:STENCIL, TAIL : TAIL + HALO] = jnp.where(
            up, offsets[:, BLOCKS - HALO :], offsets[:, :HALO]
        )
    for j in range(BLOCKS):
        cols = slice(j * LANES, (j + 1) * LANES)
        diag[j] = jnp.sum(weights[:, cols], axis=0, keepdims=True) + shifts[:, cols]
    wait_all(copies)

    for b in range(HALO, BLOCKS - HALO):
        x1[b - HALO] = apply(
            lambda c: src[:, column(0, c)],
            b,
            diag[b],
            lambda s: weights[s : s + 1, column(0, b)],
            lambda s: nb[s, b],
        )


def edge_kernel(src, near_0, near_1, weights, diag, inner, nb_in, out, x0, x1, nb, buffer, sems):
    offsets = pltpu.make_async_copy(nb_in, nb, sems.at[PARTS])
    offsets.start()
    for k, near in enumerate((near_0, near_1)):
        base = jnp.where(rightward(k), HALO + BLOCKS, 0)
        for j in range(HALO):
            x0[base + j] = near[:, j * LANES : (j + 1) * LANES]
    for j in range(BLOCKS):
        x0[HALO + j] = src[:, j * LANES : (j + 1) * LANES]
    for r in range(PARTS):
        buffer[r, 0:SLAB, :] = src[:, r * PART : (r + 1) * PART]
    for j in range(HALO, BLOCKS - HALO):
        x1[j] = inner[j - HALO]
        part, place = divmod(j, PART // LANES)
        buffer[part, SLAB:, place * LANES : (place + 1) * LANES] = inner[j - HALO]
    parts = [pltpu.make_async_copy(buffer.at[r], out.at[r], sems.at[r]) for r in range(PARTS)]
    per_part = PART // LANES
    for r in range(HALO // per_part, (BLOCKS - HALO) // per_part):
        parts[r].start()
    offsets.wait()

    for b in (*range(HALO), *range(BLOCKS - HALO, BLOCKS)):
        value = apply(
            lambda c: x0[c],
            b + HALO,
            diag[b],
            lambda s: weights[s : s + 1, column(0, b)],
            lambda s: nb[s, b],
        )
        x1[b] = value
        part, place = divmod(b, per_part)
        buffer[part, SLAB:, place * LANES : (place + 1) * LANES] = value
        if place == per_part - 1:
            parts[part].start()
    wait_all(parts)


def outer_kernel(x0_near, x1_own, far_0, far_1, weights, diag, nb_in, out, x0, x1, nbv, nbs, nb, sems):
    nbv[0] = far_0[:, TAIL:].astype(jnp.int32)
    nbv[1] = far_1[:, TAIL:].astype(jnp.int32)
    copies = start_all(sems, [(nbv.at[k], nbs.at[k]) for k in range(2)] + [(nb_in, nb)])
    for k, far in enumerate((far_0, far_1)):
        base = jnp.where(rightward(k), 3 * HALO + BLOCKS, 0)
        for j in range(HALO):
            half, place = divmod(j, HALO // 2)
            x0[base + j] = far[half * SLAB : (half + 1) * SLAB, place * LANES : (place + 1) * LANES]
    for j in range(EXT1):
        x0[HALO + j] = x0_near[j]
    for j in range(BLOCKS):
        x1[HALO + j] = x1_own[j]
    wait_all(copies)
    for side, ref in ((0, far_0), (1, far_1)):
        base = jnp.where(rightward(side), HALO + BLOCKS, 0)
        for j in range(HALO):
            e = base + j
            cols = slice(HALF + j * LANES, HALF + (j + 1) * LANES)
            x1[e] = apply(
                lambda c: x0[c],
                e + HALO,
                jnp.sum(ref[:, cols], axis=0, keepdims=True),
                lambda s: ref[s : s + 1, cols],
                lambda s: nbs[side, s, j],
            )

    def step(i, _):
        for u in range(UNROLL):
            b = i * UNROLL + u
            value = apply(
                lambda c: x1[c],
                b + HALO,
                diag[b],
                lambda s: weights[s : s + 1, column(0, b)],
                lambda s: nb[s, b],
            )
            place = lax.rem(b, PART // LANES)
            for half in range(SLAB // 8):
                out[lax.div(b, PART // LANES), :, column(half * PART, place)] = value[half * 8 : half * 8 + 8]
        return 0

    lax.fori_loop(0, BLOCKS // UNROLL, step, 0)


def tile(t):
    return slice(8 * (t // 3), 8 * (t // 3) + 8), slice(LANES * (t % 3), LANES * (t % 3) + LANES)


def tiles(r):
    per_half = PART // LANES
    for t in range(SLAB // 8 * per_half):
        half, j = divmod(t, per_half)
        row = r * SLAB + half * 8
        yield t, slice(row, row + 8), slice(j * LANES, (j + 1) * LANES)


RIDE = slice(16, 24), slice(2 * LANES, 3 * LANES)


def sums(pairs, first):
    folded = []
    for a, b in pairs:
        p = a * b
        folded.append(sum(p[:, k * LANES : (k + 1) * LANES] for k in range(PART // LANES)))
    stack = jnp.concatenate(folded, axis=1)
    shape = (8, stack.shape[1])
    which = lax.broadcasted_iota(jnp.int32, shape, 1) // LANES + first
    pick = (which == lax.broadcasted_iota(jnp.int32, shape, 0)).astype(jnp.bfloat16)
    over_lanes = functools.partial(
        lax.dot_general,
        dimension_numbers=(((1,), (1,)), ((), ())),
        preferred_element_type=jnp.float32,
    )
    high, low = split(stack)
    return over_lanes(pick, high) + over_lanes(pick, low)


def gram_kernel(z01, second, to_modes, own, out, modal, image, partial, s):
    for r in range(PARTS):
        rows = slice(r * SLAB, (r + 1) * SLAB)
        s[rows, 0:PART] = z01[r, 0:SLAB, :]
        s[rows, PART : 2 * PART] = z01[r, SLAB:, :]
    m = mm(to_modes[...], s[...])
    row = lax.broadcasted_iota(jnp.int32, (MODES, MODES), 0)
    col = lax.broadcasted_iota(jnp.int32, (MODES, MODES), 1)
    e = jnp.sum(jnp.where(row == col, own[0:1, :], 0.0), axis=1, keepdims=True)
    m0, m1 = m[:, 0:PART], m[:, PART : 2 * PART]
    i0 = m1 + e * m0
    modal[...] = m0
    image[...] = i0
    partial[...] = e * (m1 + i0)
    g = sums(((m0, m0), (m0, i0), (i0, i0)), 0)
    for r in range(PARTS):
        for t, _, _ in tiles(r):
            out[(r, *tile(t))] = second[r, :, t * LANES : (t + 1) * LANES]
        out[(r, *RIDE)] = g


def again_kernel(z2, modal, image, partial, to_modes, out, s):
    for r in range(PARTS):
        for t, rows, cols in tiles(r):
            s[rows, cols] = z2[(r, *tile(t))]
    again = mm(to_modes[...], s[...]) + partial[...]
    m0, i0 = modal[...], image[...]
    g = sum(z2[(r, *RIDE)] for r in range(PARTS)) + sums(((m0, again), (i0, again), (again, again)), 3)
    row = jnp.concatenate([g[k : k + 1, :] for k in range(6)], axis=1)
    out[...] = jnp.broadcast_to(row[None], out.shape)


def finish_kernel(got, z01, to_modes, from_modes, own, out, side, s):
    g = jnp.sum(got[...], axis=0)
    mm_, mi, ii, mj, ij, jj = (g[:, k * LANES : (k + 1) * LANES] for k in range(6))
    e = own[0:1, :]
    scale = mm_ + 1e-06
    upper = 1.5 * jnp.sqrt(ii / scale)
    lower = upper * 0.125
    center = (upper + lower) * 0.5
    half_width = (upper - lower) * 0.5
    sigma = center / half_width
    rho_zero = 1.0 / sigma
    rho_one = 1.0 / (2.0 * sigma - rho_zero)
    over = 1.0 / center
    c2 = 2.0 * rho_one / half_width
    u0 = rho_one * rho_zero * over + c2
    u1 = -c2 * over
    a = -over - u0
    b = -u1
    side[0:1, :] = mm_ + a * (2.0 * mi + a * ii)
    side[1:2, :] = scale
    ours = jnp.broadcast_to(b * (2.0 * (mj + a * ij) + b * jj), (8, LANES))
    for r in range(PARTS):
        s[r * SLAB : (r + 1) * SLAB, :] = z01[r, 0:SLAB, :]
        s[MODES + r * SLAB : MODES + (r + 1) * SLAB, :] = z01[r, SLAB:, :]
    from_m = from_modes[...]
    to_m = to_modes[...]
    mix = jnp.concatenate([mm(from_m * (over + u0 + u1 * e), to_m), mm(from_m * u1, to_m)], axis=1)
    value = mm(mix, s[...])
    for r in range(PARTS):
        for t, rows, cols in tiles(r):
            out[(r, *tile(t))] = value[rows, cols]
        out[(r, *RIDE)] = ours


def unpack_kernel(got, side, place, out, mine):
    for r in range(PARTS):
        for t, rows, cols in tiles(0):
            out[rows, r * PART + cols.start : r * PART + cols.stop] = got[(r, *tile(t))]
    squares = side[0:1, :] + sum(got[r, 16:17, RIDE[1]] for r in range(PARTS))
    norm = jnp.sqrt(jnp.maximum(squares, 0.0) / side[1:2, :])
    here = place[0:1, 0:SLAB]
    picked = norm[:, 0:SLAB]
    for r in range(1, PARTS):
        picked = jnp.where(here == r, norm[:, r * SLAB : (r + 1) * SLAB], picked)
    mine[...] = picked


def call(kernel, out_shape, in_specs, scratch=(), out_specs=None, cost=None):
    if out_specs is None:
        out_specs = (VMEM,) * len(out_shape) if isinstance(out_shape, tuple) else VMEM
    return pl.pallas_call(
        kernel,
        out_shape=out_shape,
        in_specs=in_specs,
        out_specs=out_specs,
        scratch_shapes=scratch,
        cost_estimate=cost,
        compiler_params=pltpu.CompilerParams(vmem_limit_bytes=32 * 1024 * 1024),
    )


def pinned(value):
    return pltpu.with_memory_space_constraint(value, pltpu.HBM)


def on_device(sizes, source, to_modes, from_modes, eigenvalue, shifts, weights, neighbors):
    lat = sizes["y"] * sizes["z"]
    place = jnp.full((8, LANES), lax.axis_index(RAD).astype(jnp.float32))
    shift_row = shifts.reshape(1, -1)
    eig = eigenvalue.reshape(1, -1)
    nears, fars = f32(SLAB, NEAR), f32(ROWS, TAIL + LANES)
    offsets = jax.ShapeDtypeStruct(neighbors.shape, neighbors.dtype)
    near_0, near_1, own, nb, shift_row = call(
        pack_kernel,
        (nears, nears, f32(8, LANES), offsets, f32(1, BLOCKS * LANES)),
        [HBM] * 5,
        [pltpu.VMEM((1, LANES), jnp.float32), pltpu.SemaphoreType.DMA((5,))],
    )(*(pinned(v) for v in (source, weights, shift_row, neighbors, eig)))
    swaps = [
        [(i, (i + turn) % lat) for i, turn in ((i, 1 if i % 2 != k else -1) for i in range(lat))]
        for k in range(2)
    ]
    near_0, near_1 = lax.ppermute(near_0, LAT, swaps[0]), lax.ppermute(near_1, LAT, swaps[1])
    smem_offsets = pltpu.SMEM((STENCIL, BLOCKS), jnp.int32)
    inner, diag, place, far_0, far_1 = call(
        inner_kernel,
        (f32(BLOCKS - 2 * HALO, SLAB, LANES), f32(BLOCKS, 1, LANES), f32(8, LANES), fars, fars),
        [VMEM] * 5,
        [smem_offsets, pltpu.SemaphoreType.DMA((1,))],
        cost=COST_0,
    )(source, weights, shift_row, nb, place)
    far_0, far_1 = lax.ppermute(far_0, LAT, swaps[0]), lax.ppermute(far_1, LAT, swaps[1])
    first, x0, x1 = call(
        edge_kernel,
        (f32(PARTS, 2 * SLAB, PART), f32(EXT1, SLAB, LANES), f32(BLOCKS, SLAB, LANES)),
        [VMEM] * 7,
        [
            smem_offsets,
            pltpu.VMEM((PARTS, 2 * SLAB, PART), jnp.float32),
            pltpu.SemaphoreType.DMA((PARTS + 1,)),
        ],
        out_specs=(HBM, VMEM, VMEM),
        cost=COST_1,
    )(source, near_0, near_1, weights, diag, inner, nb)
    z01 = lax.all_to_all(first, RAD, 0, 0, tiled=True)
    second = call(
        outer_kernel,
        f32(PARTS, 8, FLAT),
        [VMEM] * 7,
        [
            pltpu.VMEM((EXT2, SLAB, LANES), jnp.float32),
            pltpu.VMEM((EXT1, SLAB, LANES), jnp.float32),
            pltpu.VMEM((2, ROWS, LANES), jnp.int32),
            pltpu.SMEM((2, ROWS, LANES), jnp.int32),
            smem_offsets,
            pltpu.SemaphoreType.DMA((3,)),
        ],
        cost=COST_2,
    )(x0, x1, far_0, far_1, weights, diag, nb)
    sent, modal, image, partial = call(
        gram_kernel,
        (f32(PARTS, 24, 3 * LANES),) + (f32(MODES, PART),) * 3,
        [VMEM] * 4,
        [pltpu.VMEM((MODES, 2 * PART), jnp.float32)],
    )(z01, second, to_modes, own)
    z2 = lax.all_to_all(sent, RAD, 0, 0, tiled=True)
    g = call(
        again_kernel,
        f32(lat, 1, 6 * LANES),
        [VMEM] * 5,
        [pltpu.VMEM((MODES, PART), jnp.float32)],
    )(z2, modal, image, partial, to_modes)
    g = lax.all_to_all(g, LAT, 0, 0, tiled=True)
    mixed, side = call(
        finish_kernel,
        (f32(PARTS, 24, 3 * LANES), f32(8, LANES)),
        [VMEM] * 5,
        [pltpu.VMEM((2 * MODES, PART), jnp.float32)],
    )(g, z01, to_modes, from_modes, own)
    got = lax.all_to_all(mixed, RAD, 0, 0, tiled=True)
    smoothed, residual_norm = call(
        unpack_kernel, (f32(SLAB, BLOCKS * LANES), f32(1, SLAB)), [VMEM] * 3
    )(got, side, place)
    return smoothed, residual_norm.reshape(SLAB)


def solution(mesh):
    names = ("y", "z", "x", "core")
    fine = Mesh(np.asarray(mesh.devices).reshape(4, 8, 4, 2), names)
    return jax.shard_map(
        functools.partial(on_device, dict(fine.shape)),
        mesh=fine,
        in_specs=(P(RAD, LAT), P(), P(), P(), P(LAT), P(None, LAT), P(None, LAT)),
        out_specs=(P(RAD, LAT), P(RAD)),
        check_vma=False,
    )
```
